32 devices in a mesh: rows: 16 (over z, y, x), cols: 2 (over core).
Axes of the slice: x: 2, y: 2, z: 4, core: 2. Of those that a mesh axis runs over, the one named last changes fastest.
Arguments:
- tokens: bfloat16 [128, 32, 384], P('rows', 'cols'), may hold values from -6 to 6
- teacher: bfloat16 [128, 32, 384], P('rows', 'cols'), may hold values from -6 to 6
- tissue: int32 [16, 4], P('rows', 'cols'), may hold values 0 or 1
- weights: bfloat16 [589824], P(('rows', 'cols')), may hold values from -0.3125 to 0.3125
Outputs:
- token_grads: bfloat16 [128, 32, 384], P('rows', 'cols')
- weight_grads: float32 [589824], P(('rows', 'cols'))
The draws below stay inside these ranges and needn't reach their ends.
All inputs are finite; a program needn't handle non-finite values. No bound on the sum of `tissue` on one device may be relied on, other than what follows from the above.
Results may differ from the reference program's by a relative error of at most 0.0075.
Values may be sent and summed in bfloat16 or wider, within the bound.
No kernel may reach another device: no remote copies, remote signals or barrier semaphores. Data moves between devices by JAX's collectives and lax.ppermute only.
A program may use at most 64 MiB of HBM per device.

```python
import math
import jax
import jax.numpy as jnp
from jax import lax

D = 384
HEADS = 6
TILE = 8
NR = 128
NC = 32


def set_ends(values, own_key, smallest, top_value):
    longest = values.shape.index(max(values.shape))
    spots = []
    for shift in (0, 1):
        where = [jax.random.randint(jax.random.fold_in(own_key, axis), (), 0, length) for axis, length in enumerate(values.shape)]
        where[longest] = (where[longest] + shift) % values.shape[longest]
        spots.append(tuple(where))
    return values.at[spots[0]].set(smallest).at[spots[1]].set(top_value)


def block_scale(own_key, dims, cuts, low, top_value):
    gain, own = 1.0, jax.random.fold_in(own_key, 6)
    for axis_at, parts in cuts:
        heights = jnp.exp(jax.random.uniform(jax.random.fold_in(own, axis_at), (parts,), jnp.float32, low / len(cuts), top_value / len(cuts)))
        gain = gain * jnp.repeat(heights, dims[axis_at] // parts).reshape([-1 if axis == axis_at else 1 for axis in range(len(dims))])
    return gain


def bell_draw(own_key, extent, width, limit, split=(), kind=jnp.bfloat16):
    array = jax.random.normal(own_key, extent, jnp.float32) * width
    if len(split) > 0:
        array = block_scale(own_key, extent, split, -0.22, 0.18) * array
    return jnp.clip(array, min=-limit, max=limit).astype(kind)


def setup_inputs(seed: int = 0) -> dict:
    key_list = jax.random.split(jax.random.key(seed), 5)
    return {
        "tokens": bell_draw(key_list[0], (NR, NC, D), 1.0, 6.0, ((0, 16), (1, 2))),
        "teacher": bell_draw(key_list[1], (NR, NC, D), 1.0, 6.0, ((0, 16), (1, 2))),
        "tissue": set_ends((jax.random.randint(key_list[2], (NR // TILE, NC // TILE), 0, 3) < 2).astype(jnp.int32), jax.random.fold_in(key_list[2], 1), 0, 1),
        "weights": bell_draw(key_list[3], (4 * D * D,), D ** -0.5, 0.3125, ((0, 32),)),
    }


norm_epsilon = 1e-05
head_epsilon = 1e-06

def layer_norm(flat_tokens):
    widened = flat_tokens.astype(jnp.float32)
    centred = widened - lax.optimization_barrier(jnp.mean(widened, axis=-1, keepdims=True))
    inv_std = lax.rsqrt(lax.optimization_barrier(jnp.mean(centred * centred, axis=-1, keepdims=True)) + norm_epsilon)
    return (centred * inv_std, inv_std)

def head_norm(projected):
    shaped = projected.reshape(projected.shape[0], HEADS, projected.shape[1] // HEADS)
    factor = lax.rsqrt(lax.optimization_barrier(jnp.mean(shaped * shaped, axis=-1, keepdims=True)) + head_epsilon)
    return (shaped * factor, factor)

def head_norm_back(normal, factor, upstream):
    shaped = upstream.reshape(normal.shape)
    inner_mean = lax.optimization_barrier(jnp.mean(shaped * normal, axis=-1, keepdims=True))
    return (factor * (shaped - normal * inner_mean)).reshape(upstream.shape)

def to_tiles(field_grid):
    height, across = (field_grid.shape[0], field_grid.shape[1])
    remains = field_grid.shape[2:]
    shaped = field_grid.reshape((height // TILE, TILE, across // TILE, TILE) + remains)
    order_axes = (0, 2, 1, 3) + tuple(range(4, 4 + len(remains)))
    return shaped.transpose(order_axes).reshape((height // TILE * (across // TILE), TILE * TILE) + remains)

def from_tiles(blocks, height, across):
    remains = blocks.shape[2:]
    shaped = blocks.reshape((height // TILE, across // TILE, TILE, TILE) + remains)
    order_axes = (0, 2, 1, 3) + tuple(range(4, 4 + len(remains)))
    return shaped.transpose(order_axes).reshape((height, across) + remains)

def neighbours(padded, height, across):
    pieces = []
    for offset_row in range(3):
        for offset_col in range(3):
            window = padded[offset_row * TILE:offset_row * TILE + height, offset_col * TILE:offset_col * TILE + across]
            pieces.append(to_tiles(window))
    return jnp.concatenate(pieces, axis=1)

def heads_first(blocks):
    tile_count, length, model_width = blocks.shape
    return blocks.reshape(tile_count, length, HEADS, model_width // HEADS).transpose(2, 0, 1, 3)

def heads_last(stacked):
    return stacked.transpose(1, 2, 0, 3).reshape(stacked.shape[1], stacked.shape[2], -1)

def wide_einsum(form, left, right):
    return jnp.einsum(form, left.astype(jnp.float32), right.astype(jnp.float32))

def attend_forward(query_grid, padded_kv, padded_mask, query_mask):
    height, across, model_width = query_grid.shape
    score_scale = 1.0 / math.sqrt(model_width // HEADS)
    near_kv = neighbours(padded_kv, height, across)
    near_mask = neighbours(padded_mask[:, :, None], height, across)[:, :, 0]
    tile_mask = to_tiles(query_mask[:, :, None])[:, 0, 0]

    def one_head(head_operands):
        query_part, key_part, value_part = head_operands
        scores = wide_einsum('tqd,tkd->tqk', query_part, key_part) * score_scale
        raised = jnp.exp(scores) * near_mask[:, None, :]
        row_total = lax.optimization_barrier(jnp.sum(raised, axis=-1)) + (1.0 - tile_mask)[:, None]
        inverse = (1.0 / row_total).astype(jnp.bfloat16)
        weights_low = (raised * inverse.astype(jnp.float32)[:, :, None]).astype(jnp.bfloat16)
        return (wide_einsum('tqk,tkd->tqd', weights_low, value_part), inverse)
    operands = (heads_first(to_tiles(query_grid)), heads_first(near_kv[:, :, :model_width]), heads_first(near_kv[:, :, model_width:]))
    mixed_heads, inverse_heads = lax.map(one_head, operands)
    mixed_out = (heads_last(mixed_heads) * tile_mask[:, None, None]).astype(jnp.bfloat16)
    return (from_tiles(mixed_out, height, across), from_tiles(inverse_heads.transpose(1, 2, 0), height, across))

def attend_query_grads(query_grid, padded_kv, padded_mask, inverse_grid, delta_grid, grad_grid):
    height, across, model_width = query_grid.shape
    score_scale = 1.0 / math.sqrt(model_width // HEADS)
    near_kv = neighbours(padded_kv, height, across)
    near_mask = neighbours(padded_mask[:, :, None], height, across)[:, :, 0]

    def one_head(head_operands):
        query_part, key_part, value_part, inverse, delta_part, grad_part = head_operands
        scores = wide_einsum('tqd,tkd->tqk', query_part, key_part) * score_scale
        weights_full = jnp.exp(scores) * near_mask[:, None, :] * inverse.astype(jnp.float32)[:, :, None]
        grad_weights = wide_einsum('tqd,tkd->tqk', grad_part, value_part)
        grad_scores = (weights_full * (grad_weights - delta_part.astype(jnp.float32)[:, :, None]) * score_scale).astype(jnp.bfloat16)
        return wide_einsum('tqk,tkd->tqd', grad_scores, key_part)
    operands = (heads_first(to_tiles(query_grid)), heads_first(near_kv[:, :, :model_width]), heads_first(near_kv[:, :, model_width:]), to_tiles(inverse_grid).transpose(2, 0, 1), to_tiles(delta_grid).transpose(2, 0, 1), heads_first(to_tiles(grad_grid)))
    grad_query = lax.map(one_head, operands)
    return from_tiles(heads_last(grad_query), height, across)

def attend_key_grads(kv_grid, key_mask, padded_pack, padded_stats):
    height, across = (kv_grid.shape[0], kv_grid.shape[1])
    model_width = kv_grid.shape[2] // 2
    score_scale = 1.0 / math.sqrt(model_width // HEADS)
    kv_tiles = to_tiles(kv_grid)
    mask_tiles = to_tiles(key_mask[:, :, None])[:, :, 0]
    near_pack = neighbours(padded_pack, height, across)
    near_stats = neighbours(padded_stats, height, across)

    def one_head(head_operands):
        key_part, value_part, query_near, grad_near, inverse_near, delta_near = head_operands
        scores = wide_einsum('tkd,tqd->tkq', key_part, query_near) * score_scale
        weights_full = jnp.exp(scores) * mask_tiles[:, :, None] * inverse_near.astype(jnp.float32)[:, None, :]
        weights_low = weights_full.astype(jnp.bfloat16)
        grad_weights = wide_einsum('tkd,tqd->tkq', value_part, grad_near)
        grad_scores = (weights_full * (grad_weights - delta_near.astype(jnp.float32)[:, None, :]) * score_scale).astype(jnp.bfloat16)
        return (wide_einsum('tkq,tqd->tkd', grad_scores, query_near), wide_einsum('tkq,tqd->tkd', weights_low, grad_near))
    operands = (heads_first(kv_tiles[:, :, :model_width]), heads_first(kv_tiles[:, :, model_width:]), heads_first(near_pack[:, :, :model_width]), heads_first(near_pack[:, :, model_width:]), near_stats[:, :, :HEADS].transpose(2, 0, 1), near_stats[:, :, HEADS:].transpose(2, 0, 1))
    grad_keys, grad_values = lax.map(one_head, operands)
    merged = jnp.concatenate([heads_last(grad_keys), heads_last(grad_values)], axis=-1)
    return from_tiles(merged, height, across)

def pad_grid(field_grid):
    widths = ((TILE, TILE), (TILE, TILE)) + tuple(((0, 0) for extra_axis in field_grid.shape[2:]))
    return jnp.pad(field_grid, widths)

def reference(tokens, teacher, tissue, weights):
    rows_total, cols_total, model_width = tokens.shape
    head_width = model_width // HEADS
    matrices = weights.reshape(4, model_width, model_width)
    flat_tokens = tokens.reshape(rows_total * cols_total, model_width)
    centred_norm, inv_std = layer_norm(flat_tokens)
    lowered = centred_norm.astype(jnp.bfloat16)
    query_raw = jnp.dot(lowered, matrices[0], preferred_element_type=jnp.float32)
    key_raw = jnp.dot(lowered, matrices[1], preferred_element_type=jnp.float32)
    value_low = jnp.dot(lowered, matrices[2], preferred_element_type=jnp.float32).astype(jnp.bfloat16)
    query_normal, query_factor = head_norm(query_raw)
    key_normal, key_factor = head_norm(key_raw)
    query_low = query_normal.reshape(-1, model_width).astype(jnp.bfloat16)
    key_low = key_normal.reshape(-1, model_width).astype(jnp.bfloat16)
    token_mask = jnp.repeat(jnp.repeat(tissue.astype(jnp.float32), TILE, axis=0), TILE, axis=1)
    kv_grid = jnp.concatenate([key_low, value_low], axis=-1).reshape(rows_total, cols_total, 2 * model_width)
    query_grid = query_low.reshape(rows_total, cols_total, model_width)
    padded_kv = pad_grid(kv_grid)
    padded_mask = pad_grid(token_mask)
    band_index = jnp.arange(rows_total // TILE, dtype=jnp.int32)

    def forward_band(band_number):
        band_start = band_number * TILE
        return attend_forward(lax.dynamic_slice_in_dim(query_grid, band_start, TILE, 0), lax.dynamic_slice_in_dim(padded_kv, band_start, 3 * TILE, 0), lax.dynamic_slice_in_dim(padded_mask, band_start, 3 * TILE, 0), lax.dynamic_slice_in_dim(token_mask, band_start, TILE, 0))
    mixed_bands, inverse_bands = lax.map(forward_band, band_index)
    mixed_flat = mixed_bands.reshape(-1, model_width)
    inverse_grid = inverse_bands.reshape(rows_total, cols_total, HEADS)
    projected = jnp.dot(mixed_flat, matrices[3], preferred_element_type=jnp.float32)
    mask_flat = token_mask.reshape(-1, 1)
    residual_out = flat_tokens.astype(jnp.float32) + projected
    grad_out = mask_flat * (residual_out - teacher.reshape(-1, model_width).astype(jnp.float32))
    grad_low = grad_out.astype(jnp.bfloat16)
    grad_wo = jnp.dot(mixed_flat.T, grad_low, preferred_element_type=jnp.float32)
    grad_mixed = jnp.dot(grad_low, matrices[3].T, preferred_element_type=jnp.float32).astype(jnp.bfloat16)
    delta_heads = lax.optimization_barrier(jnp.sum((grad_mixed.astype(jnp.float32) * mixed_flat.astype(jnp.float32)).reshape(-1, HEADS, head_width), axis=-1)).astype(jnp.bfloat16)
    grad_grid = grad_mixed.reshape(rows_total, cols_total, model_width)
    delta_grid = delta_heads.reshape(rows_total, cols_total, HEADS)
    padded_inverse = pad_grid(inverse_grid)
    padded_delta = pad_grid(delta_grid)
    padded_grad = pad_grid(grad_grid)
    padded_query = pad_grid(query_grid)

    def query_band(band_number):
        band_start = band_number * TILE
        return attend_query_grads(lax.dynamic_slice_in_dim(query_grid, band_start, TILE, 0), lax.dynamic_slice_in_dim(padded_kv, band_start, 3 * TILE, 0), lax.dynamic_slice_in_dim(padded_mask, band_start, 3 * TILE, 0), lax.dynamic_slice_in_dim(inverse_grid, band_start, TILE, 0), lax.dynamic_slice_in_dim(delta_grid, band_start, TILE, 0), lax.dynamic_slice_in_dim(grad_grid, band_start, TILE, 0))

    def key_band(band_number):
        band_start = band_number * TILE
        pack_rows = jnp.concatenate([lax.dynamic_slice_in_dim(padded_query, band_start, 3 * TILE, 0), lax.dynamic_slice_in_dim(padded_grad, band_start, 3 * TILE, 0)], axis=-1)
        stats_rows = jnp.concatenate([lax.dynamic_slice_in_dim(padded_inverse, band_start, 3 * TILE, 0), lax.dynamic_slice_in_dim(padded_delta, band_start, 3 * TILE, 0)], axis=-1)
        return attend_key_grads(lax.dynamic_slice_in_dim(kv_grid, band_start, TILE, 0), lax.dynamic_slice_in_dim(token_mask, band_start, TILE, 0), pack_rows, stats_rows)
    grad_query_bands = lax.map(query_band, band_index)
    grad_kv_bands = lax.map(key_band, band_index)
    grad_query_flat = head_norm_back(query_normal, query_factor, grad_query_bands.reshape(-1, model_width)).astype(jnp.bfloat16)
    grad_kv_flat = grad_kv_bands.reshape(-1, 2 * model_width)
    grad_key_flat = head_norm_back(key_normal, key_factor, grad_kv_flat[:, :model_width]).astype(jnp.bfloat16)
    grad_value_flat = grad_kv_flat[:, model_width:].astype(jnp.bfloat16)
    grad_wq = jnp.dot(lowered.T, grad_query_flat, preferred_element_type=jnp.float32)
    grad_wk = jnp.dot(lowered.T, grad_key_flat, preferred_element_type=jnp.float32)
    grad_wv = jnp.dot(lowered.T, grad_value_flat, preferred_element_type=jnp.float32)
    grad_lowered = jnp.dot(grad_query_flat, matrices[0].T, preferred_element_type=jnp.float32) + jnp.dot(grad_key_flat, matrices[1].T, preferred_element_type=jnp.float32) + jnp.dot(grad_value_flat, matrices[2].T, preferred_element_type=jnp.float32)
    grad_tokens = grad_out + inv_std * (grad_lowered - lax.optimization_barrier(jnp.mean(grad_lowered, axis=-1, keepdims=True)) - centred_norm * lax.optimization_barrier(jnp.mean(grad_lowered * centred_norm, axis=-1, keepdims=True)))
    sums_all = jnp.stack([grad_wq, grad_wk, grad_wv, grad_wo]).reshape(-1)
    weight_grads = sums_all / math.sqrt(rows_total * cols_total)
    return (grad_tokens.reshape(rows_total, cols_total, model_width).astype(jnp.bfloat16), weight_grads)
```

```python
import functools
import math

import jax
import jax.numpy as jnp
from jax import lax
from jax.experimental import pallas as pl
from jax.experimental.pallas import tpu as pltpu
from jax.sharding import PartitionSpec as P

HEADS = 6
TILE = 8
PER = TILE * TILE
BLK = PER + 16
AXES = ("rows", "cols")

norm_epsilon = 1e-05
head_epsilon = 1e-06

F32 = jnp.float32
BF16 = jnp.bfloat16


def dot(a, b):
    return jnp.dot(a, b, preferred_element_type=F32)


def dot_nt(a, b):
    return lax.dot_general(a, b, (((1,), (1,)), ((), ())), preferred_element_type=F32)


def dot_tn(a, b):
    return lax.dot_general(a, b, (((0,), (0,)), ((), ())), preferred_element_type=F32)


def tiles_of(block):
    parts = [
        block[:, t * TILE : (t + 1) * TILE, :].reshape(PER, block.shape[2])
        for t in range(block.shape[1] // TILE)
    ]
    return jnp.concatenate(parts, axis=0)


def normalise(flat):
    mean = jnp.mean(flat, axis=-1, keepdims=True)
    centred = flat - mean
    inv_std = lax.rsqrt(jnp.mean(centred * centred, axis=-1, keepdims=True) + norm_epsilon)
    return centred * inv_std, inv_std


def pair_ones(width):
    row = lax.broadcasted_iota(jnp.int32, (2 * width, 2 * width), 0) // width
    col = lax.broadcasted_iota(jnp.int32, (2 * width, 2 * width), 1) // width
    return (row == col).astype(F32).astype(BF16)


def head_sums(x, ones):
    step = ones.shape[0]
    high = x.astype(BF16)
    low = (x - high.astype(F32)).astype(BF16)
    parts = [
        dot(high[:, p : p + step], ones) + dot(low[:, p : p + step], ones)
        for p in range(0, x.shape[1], step)
    ]
    return jnp.concatenate(parts, axis=1)


def head_normalise(raw, ones, width):
    factor = lax.rsqrt(head_sums(raw * raw, ones) * (1.0 / width) + head_epsilon)
    return raw * factor, factor


def head_back(normal, factor, upstream, ones, width):
    inner = head_sums(upstream * normal, ones) * (1.0 / width)
    return factor * (upstream - normal * inner)


def split_heads(pair, width):
    lane = lax.broadcasted_iota(jnp.int32, (1, 2 * width), 1)
    first = (lane < width).astype(F32).astype(BF16)
    second = (lane >= width).astype(F32).astype(BF16)
    return jnp.concatenate([pair * first, pair * second], axis=0)


def join_heads(stacked, width):
    half = stacked.shape[0] // 2
    lane = lax.broadcasted_iota(jnp.int32, (1, 2 * width), 1)
    return jnp.where(lane < width, stacked[:half], stacked[half:])


def near_rows(groups, odd, n_tiles):
    lanes = n_tiles * PER
    group = (lax.broadcasted_iota(jnp.int32, (1, lanes), 1) // PER) % groups
    oddf = odd.astype(F32)
    left = jnp.where(group == 2, oddf, jnp.where(group == 3, 1.0 - oddf, 1.0))
    right = jnp.where(group == 2, 1.0 - oddf, jnp.where(group == 3, oddf, 1.0))
    return left, right


def prep_kernel(scalars, tissue, tokens, low_out, send_a_out, send_b_out):
    odd = scalars[0]
    normed, _ = normalise(tiles_of(tokens[...].astype(F32)))
    low = normed.astype(BF16)
    width = low.shape[1]
    for t in range(2):
        low_out[t, 0:PER, :] = low[t * PER : (t + 1) * PER]
        low_out[t, PER:BLK, :] = jnp.full((BLK - PER, width), tissue[0, t].astype(F32)).astype(BF16)
    send_a_out[...] = low_out[1 - odd]
    if send_b_out is not None:
        send_b_out[...] = low_out[odd]


def forward_kernel(
    groups,
    place,
    scalars,
    wblk,
    mid,
    up,
    down,
    tokens,
    teacher,
    w_out,
    x_out,
    k_out,
    v_out,
    kn_out,
    kf_out,
    mixed_out,
    gout_out,
    pack_out,
):
    odd, base = scalars[0], scalars[1]
    n_blocks, per_block, model = wblk.shape
    width = model // HEADS
    own = 2 * PER
    for d in range(n_blocks):
        w_out[d * per_block : (d + 1) * per_block, :] = wblk[jnp.bitwise_xor(base, place[d])]
    strips = (mid, up, down)
    n_tiles = 3 * groups
    flag_rows = []
    for s, strip in enumerate(strips):
        for g in range(groups):
            at = (s * groups + g) * PER
            x_out[at : at + PER, :] = strip[g, 0:PER, :]
            flag_rows.append(strip[g, PER:BLK, :].astype(F32)[0:1, 0:PER])
    ones = pair_ones(width)
    x = x_out[...]
    k_raw = dot(x, w_out[model : 2 * model, :])
    k_normal, k_factor = head_normalise(k_raw, ones, width)
    kn_out[...] = k_normal[0:own]
    kf_out[...] = k_factor[0:own]
    keys = k_normal.astype(BF16)
    k_out[...] = keys
    values = dot(x, w_out[2 * model : 3 * model, :]).astype(BF16)
    v_out[...] = values
    q_normal, _ = head_normalise(dot(x[0:own], w_out[0:model, :]), ones, width)
    queries = q_normal.astype(BF16)

    flags = jnp.concatenate(flag_rows, axis=1)
    left, right = near_rows(groups, odd, n_tiles)
    near = jnp.stack([flags * left, flags * right] * 2)
    own_mask = [flag_rows[t][0:1, 0:1] for t in range(2)]
    query_mask = jnp.concatenate(
        [jnp.broadcast_to(own_mask[t], (PER, 1)) for t in range(2)], axis=0
    )
    rest = 1.0 - jnp.concatenate([query_mask, query_mask], axis=0).reshape(4, PER, 1)
    scale = 1.0 / math.sqrt(width)
    mixed_parts, inverses = [], []
    for p in range(HEADS // 2):
        lanes = slice(2 * width * p, 2 * width * (p + 1))
        scores = dot_nt(split_heads(queries[:, lanes], width), keys[:, lanes]) * scale
        raised = jnp.exp(scores).reshape(4, PER, n_tiles * PER) * near
        total = jnp.sum(raised, axis=-1, keepdims=True) + rest
        inverse = (1.0 / total).astype(BF16).astype(F32)
        low = (raised * inverse).reshape(4 * PER, n_tiles * PER).astype(BF16)
        mixed_parts.append(join_heads(dot(low, values[:, lanes]), width))
        inverse = inverse.reshape(4 * PER, 1)
        inverses += [inverse[0:own], inverse[own:]]
    mixed = (jnp.concatenate(mixed_parts, axis=1) * query_mask).astype(BF16)
    mixed_out[...] = mixed
    w_o = w_out[3 * model : 4 * model, :]
    residual = tiles_of(tokens[...].astype(F32)) + dot(mixed, w_o)
    grad_out = query_mask * (residual - tiles_of(teacher[...].astype(F32)))
    gout_out[...] = grad_out
    grad_mixed = dot_nt(grad_out.astype(BF16), w_o).astype(BF16)
    delta = head_sums(grad_mixed.astype(F32) * mixed.astype(F32), ones)
    lane = lax.broadcasted_iota(jnp.int32, (1, own), 1)
    table = jnp.zeros((own, own), F32)
    for h in range(HEADS):
        table = jnp.where(lane == h, inverses[h], table)
        table = jnp.where(lane == HEADS + h, delta[:, h * width : h * width + 1], table)
    stats = table.T[0:16, :]
    for t in range(2):
        here = slice(t * PER, (t + 1) * PER)
        pack_out[t, 0:PER, :] = grad_mixed[here]
        padded = jnp.concatenate([stats[:, here], jnp.zeros((16, model - PER), F32)], axis=1)
        pack_out[t, PER:BLK, :] = padded.astype(BF16)
    pack_out[2] = pack_out[1 - odd]


def store_terms(fast, odd, grads, outs):
    if not fast:
        for m, grad in enumerate(grads):
            outs[0][m] = grad
        return
    keep, send = outs
    rows = keep.shape[2]
    for m, grad in enumerate(grads):
        for b in range(keep.shape[1]):
            even_part = grad[2 * b * rows : (2 * b + 1) * rows]
            odd_part = grad[(2 * b + 1) * rows : (2 * b + 2) * rows]
            is_odd = odd == 1
            keep[m, b] = jnp.where(is_odd, odd_part, even_part)
            send[m, b] = jnp.where(is_odd, even_part, odd_part).astype(BF16)


def query_kernel(groups, fast, scalars, wq, x, k, v, mixed, gout, pack, mid, up, down, q_out, gl_out, *outs):
    odd, core = scalars[0], scalars[2]
    model = wq.shape[0]
    width = model // HEADS
    own = 2 * PER
    n_tiles = 3 * groups
    ones = pair_ones(width)
    q_normal, q_factor = head_normalise(dot(x[...], wq[...]), ones, width)
    q_all = q_normal.astype(BF16)
    q_out[...] = q_all
    q_normal, q_factor, queries = q_normal[0:own], q_factor[0:own], q_all[0:own]
    flag_rows = [
        strip[g, PER:BLK, :].astype(F32)[0:1, 0:PER] for strip in (mid, up, down) for g in range(groups)
    ]
    flags = jnp.concatenate(flag_rows, axis=1)
    left, right = near_rows(groups, odd, n_tiles)
    near = jnp.stack([flags * left, flags * right] * 2)
    stats = jnp.concatenate(
        [pack[t, PER:BLK, :].astype(F32)[:, 0:PER] for t in range(2)], axis=1
    )
    stats = jnp.concatenate([stats, jnp.zeros((own - 16, own), F32)], axis=0).T
    grad_mixed = jnp.concatenate([pack[t, 0:PER, :] for t in range(2)], axis=0)
    scale = 1.0 / math.sqrt(width)
    parts = []
    for p in range(HEADS // 2):
        lanes = slice(2 * width * p, 2 * width * (p + 1))
        keys, values = k[:, lanes], v[:, lanes]
        scores = dot_nt(split_heads(queries[:, lanes], width), keys) * scale
        inverse = jnp.concatenate([stats[:, 2 * p : 2 * p + 1], stats[:, 2 * p + 1 : 2 * p + 2]], axis=0)
        at = HEADS + 2 * p
        delta = jnp.concatenate([stats[:, at : at + 1], stats[:, at + 1 : at + 2]], axis=0)
        full = jnp.exp(scores).reshape(4, PER, n_tiles * PER) * near
        full = full.reshape(4 * PER, n_tiles * PER) * inverse
        grad_attn = dot_nt(split_heads(grad_mixed[:, lanes], width), values)
        grad_scores = (full * (grad_attn - delta) * scale).astype(BF16)
        parts.append(join_heads(dot(grad_scores, keys), width))
    grad_qn = jnp.concatenate(parts, axis=1)
    grad_query = head_back(q_normal, q_factor, grad_qn, ones, width).astype(BF16)
    gl_out[...] = dot_nt(grad_query, wq[...])
    grad_wq = dot_tn(x[0:own, :], grad_query)
    grad_wo = dot_tn(mixed[...], gout[...].astype(BF16))
    store_terms(fast, core, [grad_wq, grad_wo], outs)


def key_kernel(groups, fast, scalars, x, k, v, q, kn, kf, mid, pmid, pup, pdown, gk_out, gv_out, *rest):
    outs, g_scr = rest[:-1], rest[-1]
    odd, core = scalars[0], scalars[2]
    model = q.shape[1]
    width = model // HEADS
    own = 2 * PER
    n_tiles = 3 * groups
    ones = pair_ones(width)
    stat_parts = []
    for s, strip in enumerate((pmid, pup, pdown)):
        for g in range(groups):
            at = (s * groups + g) * PER
            g_scr[at : at + PER, :] = strip[g, 0:PER, :]
            stat_parts.append(strip[g, PER:BLK, :].astype(F32)[:, 0:PER])
    stats = jnp.concatenate(stat_parts, axis=1)
    left, right = near_rows(groups, odd, n_tiles)
    flags = [mid[t, PER:BLK, :].astype(F32)[0:1, 0:1] for t in range(2)]
    near = [left * flags[0], right * flags[1]]
    scale = 1.0 / math.sqrt(width)
    key_parts, value_parts = [], []
    for p in range(HEADS // 2):
        lanes = slice(2 * width * p, 2 * width * (p + 1))
        queries, grads = q[:, lanes], g_scr[:, lanes]
        scores = dot_nt(split_heads(k[0:own, lanes], width), queries) * scale
        inv = [stats[2 * p + j : 2 * p + j + 1] for j in range(2)]
        rows = jnp.stack([inv[j] * near[t] for j in range(2) for t in range(2)])
        at = HEADS + 2 * p
        delta = jnp.stack([stats[at + j : at + j + 1] for j in range(2) for _ in range(2)])
        full = jnp.exp(scores).reshape(4, PER, n_tiles * PER) * rows
        grad_attn = dot_nt(split_heads(v[0:own, lanes], width), grads)
        grad_attn = grad_attn.reshape(4, PER, n_tiles * PER) - delta
        grad_scores = (full * grad_attn * scale).reshape(4 * PER, n_tiles * PER).astype(BF16)
        low = full.reshape(4 * PER, n_tiles * PER).astype(BF16)
        key_parts.append(join_heads(dot(grad_scores, queries), width))
        value_parts.append(join_heads(dot(low, grads), width))
    grad_kn = jnp.concatenate(key_parts, axis=1)
    grad_key = head_back(kn[...], kf[...], grad_kn, ones, width).astype(BF16)
    grad_value = jnp.concatenate(value_parts, axis=1).astype(BF16)
    gk_out[...] = grad_key
    gv_out[...] = grad_value
    x_own = x[0:own, :]
    store_terms(fast, core, [dot_tn(x_own, grad_key), dot_tn(x_own, grad_value)], outs)


def final_kernel(tokens, wkv, gk, gv, gl, gout, out):
    model = gk.shape[1]
    grad_lowered = gl[...] + dot_nt(gk[...], wkv[0:model, :]) + dot_nt(gv[...], wkv[model:, :])
    normed, inv_std = normalise(tiles_of(tokens[...].astype(F32)))
    grads = gout[...] + inv_std * (
        grad_lowered
        - jnp.mean(grad_lowered, axis=-1, keepdims=True)
        - normed * jnp.mean(grad_lowered * normed, axis=-1, keepdims=True)
    )
    pieces = [grads[t * PER : (t + 1) * PER].reshape(TILE, TILE, model) for t in range(2)]
    out[...] = jnp.concatenate(pieces, axis=1).astype(BF16)


SMEM = pl.BlockSpec(memory_space=pltpu.SMEM)
VMEM = pl.BlockSpec(memory_space=pltpu.VMEM)


def call(kernel, name, in_specs, shapes, args, scratch=()):
    return pl.pallas_call(
        kernel,
        out_shape=[jax.ShapeDtypeStruct(s, t) for s, t in shapes],
        in_specs=in_specs,
        out_specs=[VMEM] * len(shapes),
        scratch_shapes=list(scratch),
        name=name,
    )(*args)


def swap(value, count, mask, keep=None):
    pairs = [(i, i ^ mask) for i in range(count) if keep is None or keep(i)]
    return lax.ppermute(value, AXES, pairs)


def col_pairs(cols, first):
    pairs = []
    for i in range(first, cols - 1, 2):
        pairs += [(i, i + 1), (i + 1, i)]
    return pairs


def row_strips(strip):
    count = lax.axis_size("rows")
    from_up = lax.ppermute(strip, "rows", [(i, i + 1) for i in range(count - 1)])
    from_down = lax.ppermute(strip, "rows", [(i + 1, i) for i in range(count - 1)])
    return from_up, from_down


def add_col_halo(own, send_a, send_b):
    cols = lax.axis_size("cols")
    parts = [own, lax.ppermute(send_a, "cols", col_pairs(cols, 0))[None]]
    if send_b is not None:
        parts.append(lax.ppermute(send_b, "cols", col_pairs(cols, 1))[None])
    return jnp.concatenate(parts, axis=0)


def gather_order(count):
    bits = [1 << b for b in range(count.bit_length() - 1)]
    return bits[3:] + bits[1:3] + bits[:1]


def body(tokens, teacher, tissue, weights):
    model = tokens.shape[2]
    rows, cols = lax.axis_size("rows"), lax.axis_size("cols")
    count = rows * cols
    groups = 3 if cols == 2 else 4
    per_block = 4 * model // count
    fast = count & (count - 1) == 0 and count >= 16 and per_block % 16 == 0
    index = lax.axis_index("rows") * cols + lax.axis_index("cols")
    odd = lax.axis_index("cols") % 2
    own = 2 * PER
    n_keys = 3 * groups * PER

    if fast:
        order = gather_order(count)
        wblk = weights.reshape(1, per_block, model)
        for mask in order:
            wblk = jnp.concatenate([wblk, swap(wblk, count, mask)], axis=0)

        def spot(d):
            return sum(((d // mask) % 2) << k for k, mask in enumerate(order))

        place = [spot(d) for d in range(count)]
        base = spot(index)
    else:
        wblk = lax.all_gather(weights, AXES, axis=0, tiled=True).reshape(4, model, model)
        place, base = list(range(4)), jnp.int32(0)
    scalars = jnp.stack([odd, base, index % 2, index]).astype(jnp.int32)

    two_sided = groups == 4
    tile_shape = ((BLK, model), BF16)
    prep = prep_kernel if two_sided else lambda *refs: prep_kernel(*refs, None)
    low, *sends = call(
        prep,
        "prep",
        [SMEM, SMEM, VMEM],
        [((2, BLK, model), BF16)] + [tile_shape] * (2 if two_sided else 1),
        (scalars, tissue, tokens),
    )
    mid = add_col_halo(low, sends[0], sends[1] if two_sided else None)
    up, down = row_strips(mid)

    w, x, k, v, kn, kf, mixed, gout, pack = call(
        functools.partial(forward_kernel, groups, place),
        "forward",
        [SMEM] + [VMEM] * 6,
        [
            ((4 * model, model), BF16),
            ((n_keys, model), BF16),
            ((n_keys, model), BF16),
            ((n_keys, model), BF16),
            ((own, model), F32),
            ((own, model), F32),
            ((own, model), BF16),
            ((own, model), F32),
            ((3, BLK, model), BF16),
        ],
        (scalars, wblk, mid, up, down, tokens, teacher),
    )
    own_pack = pack[0:2]
    other = jnp.where(odd == 1, pack[1], pack[0]) if two_sided else None
    pmid = add_col_halo(own_pack, pack[2], other)
    pup, pdown = row_strips(pmid)

    if fast:
        term_shapes = [
            ((2, count // 8, per_block, model), F32),
            ((2, count // 8, per_block, model), BF16),
        ]
    else:
        term_shapes = [((2, model, model), F32)]
    q, gl, *terms_qo = call(
        functools.partial(query_kernel, groups, fast),
        "grad_query",
        [SMEM] + [VMEM] * 10,
        [((n_keys, model), BF16), ((own, model), F32)] + term_shapes,
        (scalars, w[0:model], x, k, v, mixed, gout, own_pack, mid, up, down),
    )
    gk, gv, *terms_kv = call(
        functools.partial(key_kernel, groups, fast),
        "grad_key",
        [SMEM] + [VMEM] * 10,
        [((own, model), BF16), ((own, model), BF16)] + term_shapes,
        (scalars, x, k, v, q, kn, kf, mid, pmid, pup, pdown),
        scratch=[pltpu.VMEM((n_keys, model), BF16)],
    )
    (grads,) = call(
        final_kernel,
        "token_grads",
        [VMEM] * 6,
        [(tokens.shape, BF16)],
        (tokens, w[model : 3 * model], gk, gv, gl, gout),
    )

    n_tokens = tokens.shape[0] * rows * tokens.shape[1] * cols
    norm = math.sqrt(n_tokens)
    if not fast:
        whole = jnp.stack([terms_qo[0][0], terms_kv[0][0], terms_kv[0][1], terms_qo[0][1]])
        sums = lax.psum_scatter(whole.reshape(-1), AXES, scatter_dimension=0, tiled=True)
        return grads, sums / norm

    per_matrix = count // 4
    spots = per_matrix // 2
    here = (index // 2) % spots

    def within_matrix(keep, send):
        sums = keep + swap(send, count, 1).astype(F32)
        total = lax.dynamic_index_in_dim(sums, here, 1, keepdims=False)
        arrived = []
        for step in range(1, spots):
            out = lax.dynamic_index_in_dim(sums, here ^ step, 1, keepdims=False)
            arrived.append(swap(out.astype(BF16), count, 2 * step))
        for part in arrived:
            total = total + part.astype(F32)
        return total

    sums_qo = within_matrix(*terms_qo)
    sums_kv = within_matrix(*terms_kv)
    pieces = jnp.stack([sums_qo[0], sums_kv[0], sums_kv[1], sums_qo[1]])
    mine = index // per_matrix
    result = lax.dynamic_index_in_dim(pieces, mine, 0, keepdims=False)
    arrived = []
    for step in range(1, 4):
        out = lax.dynamic_index_in_dim(pieces, mine ^ step, 0, keepdims=False)
        arrived.append(swap(out.astype(BF16), count, per_matrix * step))
    for part in arrived:
        result = result + part.astype(F32)
    return grads, (result / norm).reshape(-1)


def solution(mesh):
    return jax.shard_map(
        body,
        mesh=mesh,
        in_specs=(
            P("rows", "cols", None),
            P("rows", "cols", None),
            P("rows", "cols"),
            P(("rows", "cols")),
        ),
        out_specs=(P("rows", "cols", None), P(("rows", "cols"))),
        check_vma=False,
    )
```

```python
import functools
import math

import jax
import jax.numpy as jnp
from jax import lax
from jax.experimental import pallas as pl
from jax.experimental.pallas import tpu as pltpu
from jax.sharding import PartitionSpec as P


HEADS = 6
TILE = 8
PER = TILE * TILE
BLK = PER + 16
AXES = ("rows", "cols")

norm_epsilon = 1e-05
head_epsilon = 1e-06

F32 = jnp.float32
BF16 = jnp.bfloat16


def dot(a, b):
    return jnp.dot(a, b, preferred_element_type=F32)


def dot_nt(a, b):
    return lax.dot_general(a, b, (((1,), (1,)), ((), ())), preferred_element_type=F32)


def dot_tn(a, b):
    return lax.dot_general(a, b, (((0,), (0,)), ((), ())), preferred_element_type=F32)


def tiles_of(block):
    parts = [
        block[:, t * TILE : (t + 1) * TILE, :].reshape(PER, block.shape[2])
        for t in range(block.shape[1] // TILE)
    ]
    return jnp.concatenate(parts, axis=0)


def normalise(flat):
    mean = jnp.mean(flat, axis=-1, keepdims=True)
    centred = flat - mean
    inv_std = lax.rsqrt(jnp.mean(centred * centred, axis=-1, keepdims=True) + norm_epsilon)
    return centred * inv_std, inv_std


def pair_ones(width):
    row = lax.broadcasted_iota(jnp.int32, (2 * width, 2 * width), 0) // width
    col = lax.broadcasted_iota(jnp.int32, (2 * width, 2 * width), 1) // width
    return (row == col).astype(F32).astype(BF16)


def head_sums(x, ones):
    step = ones.shape[0]
    high = x.astype(BF16)
    low = (x - high.astype(F32)).astype(BF16)
    parts = [
        dot(high[:, p : p + step], ones) + dot(low[:, p : p + step], ones)
        for p in range(0, x.shape[1], step)
    ]
    return jnp.concatenate(parts, axis=1)


def head_normalise(raw, ones, width):
    factor = lax.rsqrt(head_sums(raw * raw, ones) * (1.0 / width) + head_epsilon)
    return raw * factor, factor


def head_back(normal, factor, upstream, ones, width):
    inner = head_sums(upstream * normal, ones) * (1.0 / width)
    return factor * (upstream - normal * inner)


def split_heads(pair, width):
    lane = lax.broadcasted_iota(jnp.int32, (1, 2 * width), 1)
    first = (lane < width).astype(F32).astype(BF16)
    second = (lane >= width).astype(F32).astype(BF16)
    return jnp.concatenate([pair * first, pair * second], axis=0)


def join_heads(stacked, width):
    half = stacked.shape[0] // 2
    lane = lax.broadcasted_iota(jnp.int32, (1, 2 * width), 1)
    return jnp.where(lane < width, stacked[:half], stacked[half:])


def strip_tiles(groups, refs):
    tiles = []
    for s in range(3):
        own, *sides = refs[s * (groups - 1) : (s + 1) * (groups - 1)]
        tiles += [own.at[0], own.at[1]] + list(sides)
    return tiles


def near_rows(groups, odd, n_tiles):
    lanes = n_tiles * PER
    group = (lax.broadcasted_iota(jnp.int32, (1, lanes), 1) // PER) % groups
    oddf = odd.astype(F32)
    left = jnp.where(group == 2, oddf, jnp.where(group == 3, 1.0 - oddf, 1.0))
    right = jnp.where(group == 2, 1.0 - oddf, jnp.where(group == 3, oddf, 1.0))
    return left, right


def prep_kernel(scalars, tissue, tokens, low_out, send_a_out, send_b_out):
    odd = scalars[0]
    normed, _ = normalise(tiles_of(tokens[...].astype(F32)))
    low = normed.astype(BF16)
    width = low.shape[1]
    for t in range(2):
        low_out[t, 0:PER, :] = low[t * PER : (t + 1) * PER]
        low_out[t, PER:BLK, :] = jnp.full((BLK - PER, width), tissue[0, t].astype(F32)).astype(BF16)
    send_a_out[...] = low_out[1 - odd]
    if send_b_out is not None:
        send_b_out[...] = low_out[odd]


def forward_kernel(groups, place, *refs):
    scalars, wblk, tokens, teacher = refs[:4]
    n_sides = 3 * (groups - 1)
    tiles = strip_tiles(groups, refs[4 : 4 + n_sides])
    (
        wq_out,
        wk_out,
        wv_out,
        x_out,
        k_out,
        v_out,
        kn_out,
        kf_out,
        mixed_out,
        gout_out,
        near_out,
        stats_out,
        pack_out,
        *sends_out,
        wo_scr,
    ) = refs[4 + n_sides :]
    odd, base = scalars[0], scalars[1]
    n_blocks, per_block, model = wblk.shape
    width = model // HEADS
    own = 2 * PER
    per_matrix = n_blocks // 4
    for d in range(n_blocks):
        whole = (wq_out, wk_out, wv_out, wo_scr)[d // per_matrix]
        at = d % per_matrix * per_block
        whole[at : at + per_block, :] = wblk[jnp.bitwise_xor(base, place[d])]
    n_tiles = 3 * groups
    flag_rows = []
    for n, tile in enumerate(tiles):
        x_out[n * PER : (n + 1) * PER, :] = tile[0:PER, :]
        flag_rows.append(tile[PER:BLK, :].astype(F32)[0:1, 0:PER])
    ones = pair_ones(width)
    x = x_out[...]
    k_raw = dot(x, wk_out[...])
    k_normal, k_factor = head_normalise(k_raw, ones, width)
    kn_out[...] = k_normal[0:own]
    kf_out[...] = k_factor[0:own]
    keys = k_normal.astype(BF16)
    k_out[...] = keys
    values = dot(x, wv_out[...]).astype(BF16)
    v_out[...] = values
    q_normal, _ = head_normalise(dot(x[0:own], wq_out[...]), ones, width)
    queries = q_normal.astype(BF16)

    flags = jnp.concatenate(flag_rows, axis=1)
    left, right = near_rows(groups, odd, n_tiles)
    near_out[...] = jnp.concatenate([flags * left, flags * right], axis=0)
    near = jnp.stack([flags * left, flags * right] * 2)
    own_mask = [flag_rows[t][0:1, 0:1] for t in range(2)]
    query_mask = jnp.concatenate(
        [jnp.broadcast_to(own_mask[t], (PER, 1)) for t in range(2)], axis=0
    )
    rest = 1.0 - jnp.concatenate([query_mask, query_mask], axis=0).reshape(4, PER, 1)
    scale = 1.0 / math.sqrt(width)
    mixed_parts, inverses = [], []
    for p in range(HEADS // 2):
        lanes = slice(2 * width * p, 2 * width * (p + 1))
        scores = dot_nt(split_heads(queries[:, lanes], width), keys[:, lanes]) * scale
        raised = jnp.exp(scores).reshape(4, PER, n_tiles * PER) * near
        total = jnp.sum(raised, axis=-1, keepdims=True) + rest
        inverse = (1.0 / total).astype(BF16).astype(F32)
        low = (raised * inverse).reshape(4 * PER, n_tiles * PER).astype(BF16)
        mixed_parts.append(join_heads(dot(low, values[:, lanes]), width))
        inverse = inverse.reshape(4 * PER, 1)
        inverses += [inverse[0:own], inverse[own:]]
    mixed = (jnp.concatenate(mixed_parts, axis=1) * query_mask).astype(BF16)
    mixed_out[...] = mixed
    w_o = wo_scr[...]
    residual = tiles_of(tokens[...].astype(F32)) + dot(mixed, w_o)
    grad_out = query_mask * (residual - tiles_of(teacher[...].astype(F32)))
    gout_out[...] = grad_out
    grad_mixed = dot_nt(grad_out.astype(BF16), w_o).astype(BF16)
    delta = head_sums(grad_mixed.astype(F32) * mixed.astype(F32), ones)
    lane = lax.broadcasted_iota(jnp.int32, (1, own), 1)
    table = jnp.zeros((own, own), F32)
    for h in range(HEADS):
        table = jnp.where(lane == h, inverses[h], table)
        table = jnp.where(lane == HEADS + h, delta[:, h * width : h * width + 1], table)
    stats_out[...] = table
    stats = table.T[0:16, :]
    for t in range(2):
        here = slice(t * PER, (t + 1) * PER)
        pack_out[t, 0:PER, :] = grad_mixed[here]
        padded = jnp.concatenate([stats[:, here], jnp.zeros((16, model - PER), F32)], axis=1)
        pack_out[t, PER:BLK, :] = padded.astype(BF16)
    sends_out[0][...] = pack_out[1 - odd]
    if len(sends_out) > 1:
        sends_out[1][...] = pack_out[odd]


def store_terms(fast, odd, grads, outs):
    if not fast:
        for m, grad in enumerate(grads):
            outs[0][m] = grad
        return
    keep, send = outs
    rows = keep.shape[2]
    for m, grad in enumerate(grads):
        for b in range(keep.shape[1]):
            even_part = grad[2 * b * rows : (2 * b + 1) * rows]
            odd_part = grad[(2 * b + 1) * rows : (2 * b + 2) * rows]
            is_odd = odd == 1
            keep[m, b] = jnp.where(is_odd, odd_part, even_part)
            send[m, b] = jnp.where(is_odd, even_part, odd_part).astype(BF16)


def query_kernel(fast, scalars, wq, x, k, v, mixed, gout, near_in, stats_in, pack, q_out, gl_out, *outs):
    core = scalars[2]
    model = wq.shape[0]
    width = model // HEADS
    own = 2 * PER
    n_tiles = near_in.shape[1] // PER
    ones = pair_ones(width)
    q_normal, q_factor = head_normalise(dot(x[...], wq[...]), ones, width)
    q_all = q_normal.astype(BF16)
    q_out[...] = q_all
    q_normal, q_factor, queries = q_normal[0:own], q_factor[0:own], q_all[0:own]
    near = jnp.stack([near_in[0:1], near_in[1:2]] * 2)
    stats = stats_in[...].astype(BF16).astype(F32)
    grad_mixed = jnp.concatenate([pack[t, 0:PER, :] for t in range(2)], axis=0)
    scale = 1.0 / math.sqrt(width)
    parts = []
    for p in range(HEADS // 2):
        lanes = slice(2 * width * p, 2 * width * (p + 1))
        keys, values = k[:, lanes], v[:, lanes]
        scores = dot_nt(split_heads(queries[:, lanes], width), keys) * scale
        inverse = jnp.concatenate([stats[:, 2 * p : 2 * p + 1], stats[:, 2 * p + 1 : 2 * p + 2]], axis=0)
        at = HEADS + 2 * p
        delta = jnp.concatenate([stats[:, at : at + 1], stats[:, at + 1 : at + 2]], axis=0)
        full = jnp.exp(scores).reshape(4, PER, n_tiles * PER) * near
        full = full.reshape(4 * PER, n_tiles * PER) * inverse
        grad_attn = dot_nt(split_heads(grad_mixed[:, lanes], width), values)
        grad_scores = (full * (grad_attn - delta) * scale).astype(BF16)
        parts.append(join_heads(dot(grad_scores, keys), width))
    grad_qn = jnp.concatenate(parts, axis=1)
    grad_query = head_back(q_normal, q_factor, grad_qn, ones, width).astype(BF16)
    gl_out[...] = dot_nt(grad_query, wq[...])
    grad_wq = dot_tn(x[0:own, :], grad_query)
    grad_wo = dot_tn(mixed[...], gout[...].astype(BF16))
    store_terms(fast, core, [grad_wq, grad_wo], outs)


def key_kernel(groups, fast, scalars, x, k, v, q, kn, kf, near_in, *refs):
    n_sides = 3 * (groups - 1)
    tiles = strip_tiles(groups, refs[:n_sides])
    gk_out, gv_out, *outs, g_scr = refs[n_sides:]
    odd, core = scalars[0], scalars[2]
    model = q.shape[1]
    width = model // HEADS
    own = 2 * PER
    n_tiles = 3 * groups
    ones = pair_ones(width)
    stat_parts = []
    for n, tile in enumerate(tiles):
        g_scr[n * PER : (n + 1) * PER, :] = tile[0:PER, :]
        stat_parts.append(tile[PER:BLK, :].astype(F32)[:, 0:PER])
    stats = jnp.concatenate(stat_parts, axis=1)
    left, right = near_rows(groups, odd, n_tiles)
    near = [left * near_in[0:1, 0:1], right * near_in[0:1, PER : PER + 1]]
    scale = 1.0 / math.sqrt(width)
    key_parts, value_parts = [], []
    for p in range(HEADS // 2):
        lanes = slice(2 * width * p, 2 * width * (p + 1))
        queries, grads = q[:, lanes], g_scr[:, lanes]
        scores = dot_nt(split_heads(k[0:own, lanes], width), queries) * scale
        inv = [stats[2 * p + j : 2 * p + j + 1] for j in range(2)]
        rows = jnp.stack([inv[j] * near[t] for j in range(2) for t in range(2)])
        at = HEADS + 2 * p
        delta = jnp.stack([stats[at + j : at + j + 1] for j in range(2) for _ in range(2)])
        full = jnp.exp(scores).reshape(4, PER, n_tiles * PER) * rows
        grad_attn = dot_nt(split_heads(v[0:own, lanes], width), grads)
        grad_attn = grad_attn.reshape(4, PER, n_tiles * PER) - delta
        grad_scores = (full * grad_attn * scale).reshape(4 * PER, n_tiles * PER).astype(BF16)
        low = full.reshape(4 * PER, n_tiles * PER).astype(BF16)
        key_parts.append(join_heads(dot(grad_scores, queries), width))
        value_parts.append(join_heads(dot(low, grads), width))
    grad_kn = jnp.concatenate(key_parts, axis=1)
    grad_key = head_back(kn[...], kf[...], grad_kn, ones, width).astype(BF16)
    grad_value = jnp.concatenate(value_parts, axis=1).astype(BF16)
    gk_out[...] = grad_key
    gv_out[...] = grad_value
    x_own = x[0:own, :]
    store_terms(fast, core, [dot_tn(x_own, grad_key), dot_tn(x_own, grad_value)], outs)


def final_kernel(tokens, wk, wv, gk, gv, gl, gout, out):
    model = gk.shape[1]
    grad_lowered = gl[...] + dot_nt(gk[...], wk[...]) + dot_nt(gv[...], wv[...])
    normed, inv_std = normalise(tiles_of(tokens[...].astype(F32)))
    grads = gout[...] + inv_std * (
        grad_lowered
        - jnp.mean(grad_lowered, axis=-1, keepdims=True)
        - normed * jnp.mean(grad_lowered * normed, axis=-1, keepdims=True)
    )
    pieces = [grads[t * PER : (t + 1) * PER].reshape(TILE, TILE, model) for t in range(2)]
    out[...] = jnp.concatenate(pieces, axis=1).astype(BF16)


SMEM = pl.BlockSpec(memory_space=pltpu.SMEM)
VMEM = pl.BlockSpec(memory_space=pltpu.VMEM)


def call(kernel, in_specs, shapes, args, scratch=()):
    return pl.pallas_call(
        kernel,
        out_shape=[jax.ShapeDtypeStruct(s, t) for s, t in shapes],
        in_specs=in_specs,
        out_specs=[VMEM] * len(shapes),
        scratch_shapes=list(scratch),
    )(*args)


def swap(value, count, mask):
    return lax.ppermute(value, AXES, [(i, i ^ mask) for i in range(count)])


def side_pairs(length, side):
    if side is None:
        return [(i, i) for i in range(length)]
    pairs = []
    for i in range(side, length - 1, 2):
        pairs += [(i, i + 1), (i + 1, i)]
    return pairs


def around(own, sides):
    rows, cols = lax.axis_size("rows"), lax.axis_size("cols")
    parts = []
    for strip in (None, 0, 1):
        for side, value in [(None, own)] + list(enumerate(sides)):
            if strip is None and side is None:
                parts.append(value)
                continue
            pairs = [
                (r * cols + c, to_r * cols + to_c)
                for r, to_r in side_pairs(rows, strip)
                for c, to_c in side_pairs(cols, side)
            ]
            parts.append(lax.ppermute(value, AXES, pairs))
    return parts


def layer(tokens, teacher, tissue, weights):
    model = tokens.shape[2]
    rows, cols = lax.axis_size("rows"), lax.axis_size("cols")
    count = rows * cols
    groups = 3 if cols == 2 else 4
    n_sides = 3 * (groups - 1)
    per_block = 4 * model // count
    fast = count & (count - 1) == 0 and count >= 16 and per_block % 16 == 0
    per_matrix = count // 4
    spots = per_matrix // 2
    index = lax.axis_index("rows") * cols + lax.axis_index("cols")
    odd = lax.axis_index("cols") % 2
    own = 2 * PER
    n_keys = 3 * groups * PER

    def spot(d):
        return (d % 2) * (count // 2) + (d // 2 % spots) * 4 + d // per_matrix

    if fast:
        place, base = [spot(d) for d in range(count)], spot(index)
    else:
        place, base = list(range(4)), jnp.int32(0)
    scalars = jnp.stack([odd, base, index % 2, index]).astype(jnp.int32)

    tile_shape = ((BLK, model), BF16)
    sends_shape = [tile_shape] * (groups - 2)
    prep = prep_kernel if groups == 4 else lambda *refs: prep_kernel(*refs, None)
    low, *sends = call(
        prep, [SMEM, SMEM, VMEM], [((2, BLK, model), BF16)] + sends_shape, (scalars, tissue, tokens)
    )
    if fast:
        wblk = weights.reshape(1, per_block, model)
        parts = [swap(wblk, count, per_matrix * step) for step in range(1, 4)]
        wblk = jnp.concatenate([wblk] + parts, axis=0)
        wblk, low, sends = lax.optimization_barrier((wblk, low, sends))
        parts = [swap(wblk, count, 2 * step) for step in range(1, spots)]
        sides = around(low, sends)
        wblk = jnp.concatenate([wblk] + parts, axis=0)
        wblk, sides = lax.optimization_barrier((wblk, sides))
        wblk = jnp.concatenate([wblk, swap(wblk, count, 1)], axis=0)
    else:
        sides = around(low, sends)
        wblk = lax.all_gather(weights, AXES, axis=0, tiled=True).reshape(4, model, model)

    wq, wk, wv, x, k, v, kn, kf, mixed, gout, near, stats, pack, *sends = call(
        functools.partial(forward_kernel, groups, place),
        [SMEM] + [VMEM] * (3 + n_sides),
        [((model, model), BF16)] * 3
        + [((n_keys, model), BF16)] * 3
        + [
            ((own, model), F32),
            ((own, model), F32),
            ((own, model), BF16),
            ((own, model), F32),
            ((2, n_keys), F32),
            ((own, own), F32),
            ((2, BLK, model), BF16),
        ]
        + sends_shape,
        (scalars, wblk, tokens, teacher, *sides),
        scratch=[pltpu.VMEM((model, model), BF16)],
    )
    packs = around(pack, sends)

    if fast:
        term_shapes = [
            ((2, spots, per_block, model), F32),
            ((2, spots, per_block, model), BF16),
        ]
    else:
        term_shapes = [((2, model, model), F32)]
    q, gl, *terms_qo = call(
        functools.partial(query_kernel, fast),
        [SMEM] + [VMEM] * 9,
        [((n_keys, model), BF16), ((own, model), F32)] + term_shapes,
        (scalars, wq, x, k, v, mixed, gout, near, stats, pack),
    )
    gk, gv, *terms_kv = call(
        functools.partial(key_kernel, groups, fast),
        [SMEM] + [VMEM] * (7 + n_sides),
        [((own, model), BF16), ((own, model), BF16)] + term_shapes,
        (scalars, x, k, v, q, kn, kf, near, *packs),
        scratch=[pltpu.VMEM((n_keys, model), BF16)],
    )
    (grads,) = call(
        final_kernel, [VMEM] * 7, [(tokens.shape, BF16)], (tokens, wk, wv, gk, gv, gl, gout)
    )

    n_tokens = tokens.shape[0] * rows * tokens.shape[1] * cols
    norm = math.sqrt(n_tokens)
    if not fast:
        whole = jnp.stack([terms_qo[0][0], terms_kv[0][0], terms_kv[0][1], terms_qo[0][1]])
        sums = lax.psum_scatter(whole.reshape(-1), AXES, scatter_dimension=0, tiled=True)
        return grads, sums / norm

    here, mine = index // 2 % spots, index // per_matrix

    def pick(values, at, axis):
        return lax.dynamic_index_in_dim(values, at, axis, keepdims=False)

    def with_core(keep, send):
        return keep + swap(send, count, 1).astype(F32)

    sums_qo = with_core(*terms_qo)
    sums_kv = with_core(*terms_kv)

    def all_four(at):
        qo, kv = pick(sums_qo, at, 1), pick(sums_kv, at, 1)
        return jnp.concatenate([qo[0:1], kv, qo[1:2]], axis=0)

    arrived = [
        swap(all_four(here ^ step).astype(BF16), count, 2 * step) for step in range(1, spots)
    ]
    pieces = all_four(here)
    for part in arrived:
        pieces = pieces + part.astype(F32)
    arrived = [
        swap(pick(pieces, mine ^ step, 0).astype(BF16), count, per_matrix * step)
        for step in range(1, 4)
    ]
    result = pick(pieces, mine, 0)
    for part in arrived:
        result = result + part.astype(F32)
    return grads, (result / norm).reshape(-1)


def solution(mesh):
    return jax.shard_map(
        layer,
        mesh=mesh,
        in_specs=(
            P("rows", "cols", None),
            P("rows", "cols", None),
            P("rows", "cols"),
            P(("rows", "cols")),
        ),
        out_specs=(P("rows", "cols", None), P(("rows", "cols"))),
        check_vma=False,
    )
```

```python
import functools
import math

import jax
import jax.numpy as jnp
from jax import lax
from jax.experimental import pallas as pl
from jax.experimental.pallas import tpu as pltpu
from jax.sharding import PartitionSpec as P


HEADS = 6
TILE = 8
PER = TILE * TILE
BLK = PER + 16
AXES = ("rows", "cols")

norm_epsilon = 1e-05
head_epsilon = 1e-06

F32 = jnp.float32
BF16 = jnp.bfloat16
VMEM_LIMIT = 12 << 20


def dot(a, b):
    return jnp.dot(a, b, preferred_element_type=F32)


def dot_nt(a, b):
    return lax.dot_general(a, b, (((1,), (1,)), ((), ())), preferred_element_type=F32)


def dot_tn(a, b):
    return lax.dot_general(a, b, (((0,), (0,)), ((), ())), preferred_element_type=F32)


def tiles_of(block):
    parts = [
        block[:, t * TILE : (t + 1) * TILE, :].reshape(PER, block.shape[2])
        for t in range(block.shape[1] // TILE)
    ]
    return jnp.concatenate(parts, axis=0)


def normalise(flat):
    mean = jnp.mean(flat, axis=-1, keepdims=True)
    centred = flat - mean
    inv_std = lax.rsqrt(jnp.mean(centred * centred, axis=-1, keepdims=True) + norm_epsilon)
    return centred * inv_std, inv_std


def pair_ones(width):
    row = lax.broadcasted_iota(jnp.int32, (2 * width, 2 * width), 0) // width
    col = lax.broadcasted_iota(jnp.int32, (2 * width, 2 * width), 1) // width
    return (row == col).astype(F32).astype(BF16)


def head_sums(x, ones):
    step = ones.shape[0]
    high = x.astype(BF16)
    low = (x - high.astype(F32)).astype(BF16)
    parts = [
        dot(high[:, p : p + step], ones) + dot(low[:, p : p + step], ones)
        for p in range(0, x.shape[1], step)
    ]
    return jnp.concatenate(parts, axis=1)


def head_normalise(raw, ones, width):
    factor = lax.rsqrt(head_sums(raw * raw, ones) * (1.0 / width) + head_epsilon)
    return raw * factor, factor


def head_back(normal, factor, upstream, ones, width):
    inner = head_sums(upstream * normal, ones) * (1.0 / width)
    return factor * (upstream - normal * inner)


def split_heads(pair, width):
    lane = lax.broadcasted_iota(jnp.int32, (1, 2 * width), 1)
    first = (lane < width).astype(F32).astype(BF16)
    second = (lane >= width).astype(F32).astype(BF16)
    return jnp.concatenate([pair * first, pair * second], axis=0)


def join_heads(stacked, width):
    half = stacked.shape[0] // 2
    lane = lax.broadcasted_iota(jnp.int32, (1, 2 * width), 1)
    return jnp.where(lane < width, stacked[:half], stacked[half:])


def strip_tiles(strips):
    return [strip.at[g] for strip in strips for g in range(strip.shape[0])]


def near_rows(groups, odd, n_tiles):
    lanes = n_tiles * PER
    group = (lax.broadcasted_iota(jnp.int32, (1, lanes), 1) // PER) % groups
    oddf = odd.astype(F32)
    left = jnp.where(group == 2, oddf, jnp.where(group == 3, 1.0 - oddf, 1.0))
    right = jnp.where(group == 2, 1.0 - oddf, jnp.where(group == 3, oddf, 1.0))
    return left, right


def prep_kernel(scalars, tissue, tokens, low_out, send_a_out, send_b_out):
    odd = scalars[0]
    normed, _ = normalise(tiles_of(tokens[...].astype(F32)))
    low = normed.astype(BF16)
    width = low.shape[1]
    for t in range(2):
        low_out[t, 0:PER, :] = low[t * PER : (t + 1) * PER]
        low_out[t, PER:BLK, :] = jnp.full((BLK - PER, width), tissue[0, t].astype(F32)).astype(BF16)
    send_a_out[...] = low_out[1 - odd]
    if send_b_out is not None:
        send_b_out[...] = low_out[odd]


def forward_kernel(groups, place, *refs):
    scalars, wblk, tokens, teacher = refs[:4]
    tiles = strip_tiles(refs[4:7])
    (
        wq_out,
        wk_out,
        wv_out,
        x_out,
        k_out,
        v_out,
        mixed_out,
        gout_out,
        near_out,
        stats_out,
        pack_out,
        *sends_out,
        wo_scr,
    ) = refs[7:]
    odd, base = scalars[0], scalars[1]
    n_blocks, per_block, model = wblk.shape
    width = model // HEADS
    own = 2 * PER
    per_matrix = n_blocks // 4
    for d in range(n_blocks):
        whole = (wq_out, wk_out, wv_out, wo_scr)[d // per_matrix]
        at = d % per_matrix * per_block
        whole[at : at + per_block, :] = wblk[jnp.bitwise_xor(base, place[d])]
    n_tiles = 3 * groups
    flag_rows = []
    for n, tile in enumerate(tiles):
        x_out[n * PER : (n + 1) * PER, :] = tile[0:PER, :]
        flag_rows.append(tile[PER:BLK, :].astype(F32)[0:1, 0:PER])
    ones = pair_ones(width)
    x = x_out[...]
    k_normal, _ = head_normalise(dot(x, wk_out[...]), ones, width)
    keys = k_normal.astype(BF16)
    k_out[...] = keys
    values = dot(x, wv_out[...]).astype(BF16)
    v_out[...] = values
    q_normal, _ = head_normalise(dot(x[0:own], wq_out[...]), ones, width)
    queries = q_normal.astype(BF16)

    flags = jnp.concatenate(flag_rows, axis=1)
    left, right = near_rows(groups, odd, n_tiles)
    near_out[...] = jnp.concatenate([flags * left, flags * right], axis=0)
    near = jnp.stack([flags * left, flags * right] * 2)
    own_mask = [flag_rows[t][0:1, 0:1] for t in range(2)]
    query_mask = jnp.concatenate(
        [jnp.broadcast_to(own_mask[t], (PER, 1)) for t in range(2)], axis=0
    )
    rest = 1.0 - jnp.concatenate([query_mask, query_mask], axis=0).reshape(4, PER, 1)
    scale = 1.0 / math.sqrt(width)
    mixed_parts, inverses = [], []
    for p in range(HEADS // 2):
        lanes = slice(2 * width * p, 2 * width * (p + 1))
        scores = dot_nt(split_heads(queries[:, lanes], width), keys[:, lanes]) * scale
        raised = jnp.exp(scores).reshape(4, PER, n_tiles * PER) * near
        total = jnp.sum(raised, axis=-1, keepdims=True) + rest
        inverse = (1.0 / total).astype(BF16).astype(F32)
        low = (raised * inverse).reshape(4 * PER, n_tiles * PER).astype(BF16)
        mixed_parts.append(join_heads(dot(low, values[:, lanes]), width))
        inverse = inverse.reshape(4 * PER, 1)
        inverses += [inverse[0:own], inverse[own:]]
    mixed = (jnp.concatenate(mixed_parts, axis=1) * query_mask).astype(BF16)
    mixed_out[...] = mixed
    w_o = wo_scr[...]
    residual = tiles_of(tokens[...].astype(F32)) + dot(mixed, w_o)
    grad_out = query_mask * (residual - tiles_of(teacher[...].astype(F32)))
    gout_out[...] = grad_out
    grad_mixed = dot_nt(grad_out.astype(BF16), w_o).astype(BF16)
    delta = head_sums(grad_mixed.astype(F32) * mixed.astype(F32), ones)
    lane = lax.broadcasted_iota(jnp.int32, (1, own), 1)
    table = jnp.zeros((own, own), F32)
    for h in range(HEADS):
        table = jnp.where(lane == h, inverses[h], table)
        table = jnp.where(lane == HEADS + h, delta[:, h * width : h * width + 1], table)
    table = jnp.where(lane == 2 * HEADS, query_mask, table)
    stats_out[...] = table
    stats = table.T[0:16, :]
    for t in range(2):
        here = slice(t * PER, (t + 1) * PER)
        pack_out[t, 0:PER, :] = grad_mixed[here]
        padded = jnp.concatenate([stats[:, here], jnp.zeros((16, model - PER), F32)], axis=1)
        pack_out[t, PER:BLK, :] = padded.astype(BF16)
    sends_out[0][...] = pack_out[1 - odd]
    if len(sends_out) > 1:
        sends_out[1][...] = pack_out[odd]


def store_terms(fast, odd, grads, outs):
    if not fast:
        for m, grad in enumerate(grads):
            outs[0][m] = grad
        return
    keep, send = outs
    rows = keep.shape[2]
    for m, grad in enumerate(grads):
        for b in range(keep.shape[1]):
            even_part = grad[2 * b * rows : (2 * b + 1) * rows]
            odd_part = grad[(2 * b + 1) * rows : (2 * b + 2) * rows]
            is_odd = odd == 1
            keep[m, b] = jnp.where(is_odd, odd_part, even_part)
            send[m, b] = jnp.where(is_odd, even_part, odd_part).astype(BF16)


def query_kernel(fast, scalars, wq, x, k, v, mixed, gout, near_in, stats_in, pack, q_out, gl_out, *outs):
    core = scalars[2]
    model = wq.shape[0]
    width = model // HEADS
    own = 2 * PER
    n_tiles = near_in.shape[1] // PER
    ones = pair_ones(width)
    q_normal, q_factor = head_normalise(dot(x[...], wq[...]), ones, width)
    q_all = q_normal.astype(BF16)
    q_out[...] = q_all
    q_normal, q_factor, queries = q_normal[0:own], q_factor[0:own], q_all[0:own]
    near = jnp.stack([near_in[0:1], near_in[1:2]] * 2)
    stats = stats_in[...].astype(BF16).astype(F32)
    grad_mixed = jnp.concatenate([pack[t, 0:PER, :] for t in range(2)], axis=0)
    scale = 1.0 / math.sqrt(width)
    parts = []
    for p in range(HEADS // 2):
        lanes = slice(2 * width * p, 2 * width * (p + 1))
        keys, values = k[:, lanes], v[:, lanes]
        scores = dot_nt(split_heads(queries[:, lanes], width), keys) * scale
        inverse = jnp.concatenate([stats[:, 2 * p : 2 * p + 1], stats[:, 2 * p + 1 : 2 * p + 2]], axis=0)
        at = HEADS + 2 * p
        delta = jnp.concatenate([stats[:, at : at + 1], stats[:, at + 1 : at + 2]], axis=0)
        full = jnp.exp(scores).reshape(4, PER, n_tiles * PER) * near
        full = full.reshape(4 * PER, n_tiles * PER) * inverse
        grad_attn = dot_nt(split_heads(grad_mixed[:, lanes], width), values)
        grad_scores = (full * (grad_attn - delta) * scale).astype(BF16)
        parts.append(join_heads(dot(grad_scores, keys), width))
    grad_qn = jnp.concatenate(parts, axis=1)
    grad_query = head_back(q_normal, q_factor, grad_qn, ones, width).astype(BF16)
    gl_out[...] = dot_nt(grad_query, wq[...])
    grad_wq = dot_tn(x[0:own, :], grad_query)
    grad_wo = dot_tn(mixed[...], gout[...].astype(BF16))
    store_terms(fast, core, [grad_wq, grad_wo], outs)


def key_kernel(groups, fast, scalars, x, k, v, q, wk, gl, mid, near, far, gk_out, gv_out, gl_out, *rest):
    *outs, g_scr = rest
    tiles = strip_tiles((mid, near, far))
    gl_out[...] = gl[...]
    odd, core = scalars[0], scalars[2]
    model = q.shape[1]
    width = model // HEADS
    own = 2 * PER
    n_tiles = 3 * groups
    ones = pair_ones(width)
    stat_parts = []
    for n, tile in enumerate(tiles):
        g_scr[n * PER : (n + 1) * PER, :] = tile[0:PER, :]
        stat_parts.append(tile[PER:BLK, :].astype(F32)[:, 0:PER])
    stats = jnp.concatenate(stat_parts, axis=1)
    left, right = near_rows(groups, odd, n_tiles)
    flag = stats[2 * HEADS : 2 * HEADS + 1]
    near = [left * flag[:, 0:1], right * flag[:, PER : PER + 1]]
    scale = 1.0 / math.sqrt(width)
    key_parts, value_parts = [], []
    for p in range(HEADS // 2):
        lanes = slice(2 * width * p, 2 * width * (p + 1))
        queries, grads = q[:, lanes], g_scr[:, lanes]
        scores = dot_nt(split_heads(k[0:own, lanes], width), queries) * scale
        inv = [stats[2 * p + j : 2 * p + j + 1] for j in range(2)]
        rows = jnp.stack([inv[j] * near[t] for j in range(2) for t in range(2)])
        at = HEADS + 2 * p
        delta = jnp.stack([stats[at + j : at + j + 1] for j in range(2) for _ in range(2)])
        full = jnp.exp(scores).reshape(4, PER, n_tiles * PER) * rows
        grad_attn = dot_nt(split_heads(v[0:own, lanes], width), grads)
        grad_attn = grad_attn.reshape(4, PER, n_tiles * PER) - delta
        grad_scores = (full * grad_attn * scale).reshape(4 * PER, n_tiles * PER).astype(BF16)
        low = full.reshape(4 * PER, n_tiles * PER).astype(BF16)
        key_parts.append(join_heads(dot(grad_scores, queries), width))
        value_parts.append(join_heads(dot(low, grads), width))
    grad_kn = jnp.concatenate(key_parts, axis=1)
    x_own = x[0:own, :]
    k_normal, k_factor = head_normalise(dot(x_own, wk[...]), ones, width)
    grad_key = head_back(k_normal, k_factor, grad_kn, ones, width).astype(BF16)
    grad_value = jnp.concatenate(value_parts, axis=1).astype(BF16)
    gk_out[...] = grad_key
    gv_out[...] = grad_value
    store_terms(fast, core, [dot_tn(x_own, grad_key), dot_tn(x_own, grad_value)], outs)


def final_kernel(tokens, wk, wv, gk, gv, gl, gout, out):
    model = gk.shape[1]
    grad_lowered = gl[...] + dot_nt(gk[...], wk[...]) + dot_nt(gv[...], wv[...])
    normed, inv_std = normalise(tiles_of(tokens[...].astype(F32)))
    grads = gout[...] + inv_std * (
        grad_lowered
        - jnp.mean(grad_lowered, axis=-1, keepdims=True)
        - normed * jnp.mean(grad_lowered * normed, axis=-1, keepdims=True)
    )
    pieces = [grads[t * PER : (t + 1) * PER].reshape(TILE, TILE, model) for t in range(2)]
    out[...] = jnp.concatenate(pieces, axis=1).astype(BF16)


SMEM = pl.BlockSpec(memory_space=pltpu.SMEM)
VMEM = pl.BlockSpec(memory_space=pltpu.VMEM)


def call(kernel, in_specs, shapes, args, scratch=(), kept=0, held=()):
    args = [
        pltpu.with_memory_space_constraint(a, pltpu.VMEM) if n in held else a
        for n, a in enumerate(args)
    ]
    return pl.pallas_call(
        kernel,
        out_shape=[
            pltpu.VMEM(s, t) if n < kept else jax.ShapeDtypeStruct(s, t)
            for n, (s, t) in enumerate(shapes)
        ],
        in_specs=in_specs,
        out_specs=[VMEM] * len(shapes),
        scratch_shapes=list(scratch),
        compiler_params=pltpu.CompilerParams(vmem_limit_bytes=VMEM_LIMIT),
    )(*args)


def swap(value, count, mask):
    return lax.ppermute(value, AXES, [(i, i ^ mask) for i in range(count)])


def side_pairs(length, side):
    pairs = []
    for i in range(side, length - 1, 2):
        pairs += [(i, i + 1), (i + 1, i)]
    return pairs


def across(own, sides):
    cols = lax.axis_size("cols")
    parts = [lax.ppermute(v, "cols", side_pairs(cols, n))[None] for n, v in enumerate(sides)]
    return jnp.concatenate([own] + parts, axis=0)


def beside(strip):
    rows = lax.axis_size("rows")
    return [lax.ppermute(strip, "rows", side_pairs(rows, n)) for n in range(2)]


def layer(tokens, teacher, tissue, weights):
    model = tokens.shape[2]
    rows, cols = lax.axis_size("rows"), lax.axis_size("cols")
    count = rows * cols
    groups = 3 if cols == 2 else 4
    per_block = 4 * model // count
    fast = count & (count - 1) == 0 and count >= 16 and per_block % 16 == 0
    per_matrix = count // 4
    spots = per_matrix // 2
    index = lax.axis_index("rows") * cols + lax.axis_index("cols")
    odd = lax.axis_index("cols") % 2
    own = 2 * PER
    n_keys = 3 * groups * PER

    def spot(d):
        return (d % 2) * (count // 2) + (d // 2 % spots) * 4 + d // per_matrix

    if fast:
        place, base = [spot(d) for d in range(count)], spot(index)
    else:
        place, base = list(range(4)), jnp.int32(0)
    scalars = jnp.stack([odd, base, index % 2, index]).astype(jnp.int32)

    tile_shape = ((BLK, model), BF16)
    sends_shape = [tile_shape] * (groups - 2)
    prep = prep_kernel if groups == 4 else lambda *refs: prep_kernel(*refs, None)
    low, *sends = call(
        prep, [SMEM, SMEM, VMEM], [((2, BLK, model), BF16)] + sends_shape, (scalars, tissue, tokens)
    )
    if fast:
        wblk = weights.reshape(1, per_block, model)
        parts = [swap(wblk, count, per_matrix * step) for step in range(1, 4)]
        wblk = jnp.concatenate([wblk] + parts, axis=0)
        mid = across(low, sends)
        wblk, mid = lax.optimization_barrier((wblk, mid))
        parts = [swap(wblk, count, 2 * step) for step in range(1, spots)]
        sides = beside(mid)
        wblk = jnp.concatenate([wblk] + parts, axis=0)
        wblk, sides = lax.optimization_barrier((wblk, sides))
        wblk = jnp.concatenate([wblk, swap(wblk, count, 1)], axis=0)
    else:
        mid = across(low, sends)
        sides = beside(mid)
        wblk = lax.all_gather(weights, AXES, axis=0, tiled=True).reshape(4, model, model)

    wq, wk, wv, x, k, v, mixed, gout, near, stats, pack, *sends = call(
        functools.partial(forward_kernel, groups, place),
        [SMEM] + [VMEM] * 6,
        [((model, model), BF16)] * 3
        + [((n_keys, model), BF16)] * 3
        + [
            ((own, model), BF16),
            ((own, model), F32),
            ((2, n_keys), F32),
            ((own, own), F32),
            ((2, BLK, model), BF16),
        ]
        + sends_shape,
        (scalars, wblk, tokens, teacher, mid, *sides),
        scratch=[pltpu.VMEM((model, model), BF16)],
        kept=10,
    )
    packs = across(pack, sends)
    packs = [packs] + beside(packs)

    if fast:
        term_shapes = [
            ((2, spots, per_block, model), F32),
            ((2, spots, per_block, model), BF16),
        ]
    else:
        term_shapes = [((2, model, model), F32)]
    q, gl, *terms_qo = call(
        functools.partial(query_kernel, fast),
        [SMEM] + [VMEM] * 9,
        [((n_keys, model), BF16), ((own, model), F32)] + term_shapes,
        (scalars, wq, x, k, v, mixed, gout, near, stats, pack),
        kept=4 if fast else 2,
        held=range(1, 9),
    )
    gk, gv, gl, *terms_kv = call(
        functools.partial(key_kernel, groups, fast),
        [SMEM] + [VMEM] * 9,
        [((own, model), BF16), ((own, model), BF16), ((own, model), F32)] + term_shapes,
        (scalars, x, k, v, q, wk, gl, *packs),
        scratch=[pltpu.VMEM((n_keys, model), BF16)],
        kept=5 if fast else 3,
        held=range(1, 7),
    )
    (grads,) = call(
        final_kernel,
        [VMEM] * 7,
        [(tokens.shape, BF16)],
        (tokens, wk, wv, gk, gv, gl, gout),
        held=range(1, 7),
    )

    n_tokens = tokens.shape[0] * rows * tokens.shape[1] * cols
    norm = math.sqrt(n_tokens)
    if not fast:
        whole = jnp.stack([terms_qo[0][0], terms_kv[0][0], terms_kv[0][1], terms_qo[0][1]])
        sums = lax.psum_scatter(whole.reshape(-1), AXES, scatter_dimension=0, tiled=True)
        return grads, sums / norm

    here, mine = index // 2 % spots, index // per_matrix

    def pick(values, at, axis):
        return lax.dynamic_index_in_dim(values, at, axis, keepdims=False)

    def with_core(keep, send):
        return keep + swap(send, count, 1).astype(F32)

    sums_qo = with_core(*terms_qo)
    sums_kv = with_core(*terms_kv)

    def all_four(at):
        qo, kv = pick(sums_qo, at, 1), pick(sums_kv, at, 1)
        return jnp.concatenate([qo[0:1], kv, qo[1:2]], axis=0)

    arrived = [
        swap(all_four(here ^ step).astype(BF16), count, 2 * step) for step in range(1, spots)
    ]
    pieces = all_four(here)
    for part in arrived:
        pieces = pieces + part.astype(F32)
    arrived = [
        swap(pick(pieces, mine ^ step, 0).astype(BF16), count, per_matrix * step)
        for step in range(1, 4)
    ]
    result = pick(pieces, mine, 0)
    for part in arrived:
        result = result + part.astype(F32)
    return grads, (result / norm).reshape(-1)


def solution(mesh):
    return jax.shard_map(
        layer,
        mesh=mesh,
        in_specs=(
            P("rows", "cols", None),
            P("rows", "cols", None),
            P("rows", "cols"),
            P(("rows", "cols")),
        ),
        out_specs=(P("rows", "cols", None), P(("rows", "cols"))),
        check_vma=False,
    )
```

```python
import functools
import math

import jax
import jax.numpy as jnp
from jax import lax
from jax.experimental import pallas as pl
from jax.experimental.pallas import tpu as pltpu
from jax.sharding import PartitionSpec as P


HEADS = 6
TILE = 8
PER = TILE * TILE
BLK = PER + 8
AXES = ("rows", "cols")

norm_epsilon = 1e-05
head_epsilon = 1e-06

F32 = jnp.float32
BF16 = jnp.bfloat16
VMEM_LIMIT = 12 << 20


def dot(a, b):
    return jnp.dot(a, b, preferred_element_type=F32)


def dot_nt(a, b):
    return lax.dot_general(a, b, (((1,), (1,)), ((), ())), preferred_element_type=F32)


def dot_tn(a, b):
    return lax.dot_general(a, b, (((0,), (0,)), ((), ())), preferred_element_type=F32)


def tiles_of(block):
    parts = [
        block[:, t * TILE : (t + 1) * TILE, :].reshape(PER, block.shape[2])
        for t in range(block.shape[1] // TILE)
    ]
    return jnp.concatenate(parts, axis=0)


def normalise(flat):
    mean = jnp.mean(flat, axis=-1, keepdims=True)
    centred = flat - mean
    inv_std = lax.rsqrt(jnp.mean(centred * centred, axis=-1, keepdims=True) + norm_epsilon)
    return centred * inv_std, inv_std


def pair_ones(width):
    row = lax.broadcasted_iota(jnp.int32, (2 * width, 2 * width), 0) // width
    col = lax.broadcasted_iota(jnp.int32, (2 * width, 2 * width), 1) // width
    return (row == col).astype(F32).astype(BF16)


def head_sums(x, ones):
    step = ones.shape[0]
    high = x.astype(BF16)
    low = (x - high.astype(F32)).astype(BF16)
    parts = [
        dot(high[:, p : p + step], ones) + dot(low[:, p : p + step], ones)
        for p in range(0, x.shape[1], step)
    ]
    return jnp.concatenate(parts, axis=1)


def head_normalise(raw, ones, width):
    squares = (raw * raw).astype(BF16)
    step = ones.shape[0]
    sums = [dot(squares[:, p : p + step], ones) for p in range(0, raw.shape[1], step)]
    factor = lax.rsqrt(jnp.concatenate(sums, axis=1) * (1.0 / width) + head_epsilon)
    return raw * factor, factor


def head_back(normal, factor, upstream, ones, width):
    inner = head_sums(upstream * normal, ones) * (1.0 / width)
    return factor * (upstream - normal * inner)


def split_heads(pair, width):
    lane = lax.broadcasted_iota(jnp.int32, (1, 2 * width), 1)
    first = (lane < width).astype(F32).astype(BF16)
    second = (lane >= width).astype(F32).astype(BF16)
    return jnp.concatenate([pair * first, pair * second], axis=0)


def join_heads(stacked, width):
    half = stacked.shape[0] // 2
    lane = lax.broadcasted_iota(jnp.int32, (1, 2 * width), 1)
    return jnp.where(lane < width, stacked[:half], stacked[half:])


def strip_tiles(strips, odd):
    tiles = []
    for n in range(3):
        tiles += strips[0] if n == 0 else [strips[n].at[0], strips[n].at[1]]
        for side in range(1, len(strips) // 3):
            tiles.append(strips[3 * side + n].at[odd if side == 1 else 1 - odd])
    return tiles


def packed_tiles(v, n_tiles):
    return [v.at[pl.ds(n_tiles * PER + t * BLK, BLK)] for t in range(2)]


def pack_stats(stats, width):
    blank = jnp.zeros((8, width - 2 * PER), F32)
    return jnp.concatenate([stats[0:8], stats[8:16], blank], axis=1).astype(BF16)


def unpack_stats(tile):
    rows = tile[PER:BLK, 0 : 2 * PER].astype(F32)
    return jnp.concatenate([rows[:, 0:PER], rows[:, PER:]], axis=0)


def near_rows(groups, odd, n_tiles):
    lanes = n_tiles * PER
    group = (lax.broadcasted_iota(jnp.int32, (1, lanes), 1) // PER) % groups
    oddf = odd.astype(F32)
    left = jnp.where(group == 2, oddf, jnp.where(group == 3, 1.0 - oddf, 1.0))
    right = jnp.where(group == 2, 1.0 - oddf, jnp.where(group == 3, oddf, 1.0))
    return left, right


def prep_kernel(tissue, tokens, low_out):
    normed, _ = normalise(tiles_of(tokens[...].astype(F32)))
    low = normed.astype(BF16)
    width = low.shape[1]
    for t in range(2):
        low_out[t, 0:PER, :] = low[t * PER : (t + 1) * PER]
        low_out[t, PER:BLK, :] = jnp.full((BLK - PER, width), tissue[0, t].astype(F32)).astype(BF16)


def forward_kernel(groups, place, *refs):
    scalars, first_half, second_half, tokens, teacher, *refs = refs
    n_strips = 3 * (groups - 1)
    (
        wq_out,
        wk_out,
        wv_out,
        x_out,
        k_out,
        v_out,
        mixed_out,
        gout_out,
        near_out,
        stats_out,
        pack_out,
        wo_scr,
    ) = refs[n_strips:]
    odd, base = scalars[0], scalars[1]
    own_strip, *others = refs[:n_strips]
    tiles = strip_tiles([[own_strip.at[0], own_strip.at[1]], *others], odd)
    half, per_block, model = first_half.shape
    n_blocks = 2 * half
    width = model // HEADS
    own = 2 * PER
    per_matrix = n_blocks // 4
    swapped = (base >= half).astype(jnp.int32)
    for way in (0, 1):

        @pl.when(swapped == way)
        def _():
            for d in range(n_blocks):
                whole = (wq_out, wk_out, wv_out, wo_scr)[d // per_matrix]
                at = d % per_matrix * per_block
                source = first_half if (place[d] >= half) == way else second_half
                whole[at : at + per_block, :] = source[jnp.bitwise_xor(base, place[d]) % half]

    n_tiles = 3 * groups
    flag_rows = []
    ones = pair_ones(width)
    key_parts, value_parts = [], []
    for first, last in ((0, groups), (groups, n_tiles)):
        for n in range(first, last):
            x_out[n * PER : (n + 1) * PER, :] = tiles[n][0:PER, :]
            flag_rows.append(tiles[n][PER:BLK, :].astype(F32)[0:1, 0:PER])
        x = x_out[first * PER : last * PER, :]
        if first == 0:
            q_normal, _ = head_normalise(dot(x[0:own], wq_out[...]), ones, width)
            queries = q_normal.astype(BF16)
        k_normal, _ = head_normalise(dot(x, wk_out[...]), ones, width)
        key_parts.append(k_normal.astype(BF16))
        value_parts.append(dot(x, wv_out[...]).astype(BF16))
    keys = jnp.concatenate(key_parts, axis=0)
    values = jnp.concatenate(value_parts, axis=0)
    k_out[...] = keys
    v_out[0 : n_tiles * PER, :] = values

    flags = jnp.concatenate(flag_rows, axis=1)
    left, right = near_rows(groups, odd, n_tiles)
    near_out[...] = jnp.concatenate([flags * left, flags * right], axis=0)
    near = jnp.stack([flags * left, flags * right] * 2)
    own_mask = [flag_rows[t][0:1, 0:1] for t in range(2)]
    query_mask = jnp.concatenate(
        [jnp.broadcast_to(own_mask[t], (PER, 1)) for t in range(2)], axis=0
    )
    rest = 1.0 - jnp.concatenate([query_mask, query_mask], axis=0).reshape(4, PER, 1)
    scale = 1.0 / math.sqrt(width)
    mixed_parts, inverses = [], []
    for p in range(HEADS // 2):
        lanes = slice(2 * width * p, 2 * width * (p + 1))
        scores = dot_nt(split_heads(queries[:, lanes], width), keys[:, lanes]) * scale
        raised = jnp.exp(scores).reshape(4, PER, n_tiles * PER) * near
        total = jnp.sum(raised, axis=-1, keepdims=True) + rest
        inverse = (1.0 / total).astype(BF16).astype(F32)
        low = (raised * inverse).reshape(4 * PER, n_tiles * PER).astype(BF16)
        mixed_parts.append(join_heads(dot(low, values[:, lanes]), width))
        inverse = inverse.reshape(4 * PER, 1)
        inverses += [inverse[0:own], inverse[own:]]
    mixed = (jnp.concatenate(mixed_parts, axis=1) * query_mask).astype(BF16)
    mixed_out[...] = mixed
    w_o = wo_scr[...]
    residual = tiles_of(tokens[...].astype(F32)) + dot(mixed, w_o)
    grad_out = query_mask * (residual - tiles_of(teacher[...].astype(F32)))
    gout_out[...] = grad_out
    grad_mixed = dot_nt(grad_out.astype(BF16), w_o).astype(BF16)
    delta = head_sums(grad_mixed.astype(F32) * mixed.astype(F32), ones)
    lane = lax.broadcasted_iota(jnp.int32, (1, own), 1)
    table = jnp.zeros((own, own), F32)
    for h in range(HEADS):
        table = jnp.where(lane == h, inverses[h], table)
        table = jnp.where(lane == HEADS + h, delta[:, h * width : h * width + 1], table)
    table = jnp.where(lane == 2 * HEADS, query_mask, table)
    stats_out[...] = table
    stats = table.T[0:16, :]
    for t in range(2):
        here = slice(t * PER, (t + 1) * PER)
        pack_out[t, 0:PER, :] = grad_mixed[here]
        pack_out[t, PER:BLK, :] = pack_stats(stats[:, here], model)
        packed_tiles(v_out, n_tiles)[t][...] = pack_out[t]


def store_terms(fast, odd, grads, outs):
    if not fast:
        for m, grad in enumerate(grads):
            outs[0][m] = grad
        return
    keep, send = outs
    rows = keep.shape[2]
    for m, grad in enumerate(grads):
        for b in range(keep.shape[1]):
            even_part = grad[2 * b * rows : (2 * b + 1) * rows]
            odd_part = grad[(2 * b + 1) * rows : (2 * b + 2) * rows]
            is_odd = odd == 1
            keep[m, b] = jnp.where(is_odd, odd_part, even_part)
            send[m, b] = jnp.where(is_odd, even_part, odd_part).astype(BF16)


def halo_query_kernel(wq, x, q_out):
    model = x.shape[1]
    width = model // HEADS
    q_normal, _ = head_normalise(dot(x[...], wq[...]), pair_ones(width), width)
    q_out[...] = q_normal.astype(BF16)


def query_kernel(fast, scalars, wq, x, k, v, mixed, gout, near_in, stats_in, *outs):
    core = scalars[2]
    model = wq.shape[0]
    width = model // HEADS
    own = 2 * PER
    n_tiles = near_in.shape[1] // PER
    ones = pair_ones(width)
    q_normal, q_factor = head_normalise(dot(x[0:own, :], wq[...]), ones, width)
    queries = q_normal.astype(BF16)
    near = jnp.stack([near_in[0:1], near_in[1:2]] * 2)
    stats = stats_in[...].astype(BF16).astype(F32)
    gq_out, *outs = outs
    grad_mixed = jnp.concatenate([pack[0:PER, :] for pack in packed_tiles(v, n_tiles)], axis=0)
    scale = 1.0 / math.sqrt(width)
    parts = []
    for p in range(HEADS // 2):
        lanes = slice(2 * width * p, 2 * width * (p + 1))
        keys, values = k[:, lanes], v[0 : n_tiles * PER, lanes]
        scores = dot_nt(split_heads(queries[:, lanes], width), keys) * scale
        inverse = jnp.concatenate([stats[:, 2 * p : 2 * p + 1], stats[:, 2 * p + 1 : 2 * p + 2]], axis=0)
        at = HEADS + 2 * p
        delta = jnp.concatenate([stats[:, at : at + 1], stats[:, at + 1 : at + 2]], axis=0)
        full = jnp.exp(scores).reshape(4, PER, n_tiles * PER) * near
        full = full.reshape(4 * PER, n_tiles * PER) * inverse
        grad_attn = dot_nt(split_heads(grad_mixed[:, lanes], width), values)
        grad_scores = (full * (grad_attn - delta) * scale).astype(BF16)
        parts.append(join_heads(dot(grad_scores, keys), width))
    grad_qn = jnp.concatenate(parts, axis=1)
    grad_query = head_back(q_normal, q_factor, grad_qn, ones, width).astype(BF16)
    gq_out[...] = grad_query
    grad_wq = dot_tn(x[0:own, :], grad_query)
    grad_wo = dot_tn(mixed[...], gout[...].astype(BF16))
    store_terms(fast, core, [grad_wq, grad_wo], outs)


def key_kernel(groups, fast, scalars, x, k, v, wk, q, *refs):
    n_strips = 3 * (groups - 1)
    sources, refs = refs[: n_strips - 1], refs[n_strips - 1 :]
    if fast:
        kept, arrived, sums_out, *refs = refs
        sums_out[...] = kept[...] + arrived[...].astype(F32)
    *refs, g_scr = refs
    gk_out, gv_out, *outs = refs
    odd, core = scalars[0], scalars[2]
    model = x.shape[1]
    width = model // HEADS
    own = 2 * PER
    n_tiles = 3 * groups
    ones = pair_ones(width)
    tiles = strip_tiles([packed_tiles(v, n_tiles), *sources], odd)
    x_own = x[0:own, :]
    k_normal, k_factor = head_normalise(dot(x_own, wk[...]), ones, width)
    stat_parts = []
    for n, tile in enumerate(tiles):
        g_scr[n * PER : (n + 1) * PER, :] = tile[0:PER, :]
        stat_parts.append(unpack_stats(tile))
    stats = jnp.concatenate(stat_parts, axis=1)
    left, right = near_rows(groups, odd, n_tiles)
    flag = stats[2 * HEADS : 2 * HEADS + 1]
    near = [left * flag[:, 0:1], right * flag[:, PER : PER + 1]]
    scale = 1.0 / math.sqrt(width)
    key_parts, value_parts = [], []
    for p in range(HEADS // 2):
        lanes = slice(2 * width * p, 2 * width * (p + 1))
        queries, grads = q[:, lanes], g_scr[:, lanes]
        scores = dot_nt(split_heads(k[0:own, lanes], width), queries) * scale
        inv = [stats[2 * p + j : 2 * p + j + 1] for j in range(2)]
        rows = jnp.stack([inv[j] * near[t] for j in range(2) for t in range(2)])
        at = HEADS + 2 * p
        delta = jnp.stack([stats[at + j : at + j + 1] for j in range(2) for _ in range(2)])
        full = jnp.exp(scores).reshape(4, PER, n_tiles * PER) * rows
        grad_attn = dot_nt(split_heads(v[0:own, lanes], width), grads)
        grad_attn = grad_attn.reshape(4, PER, n_tiles * PER) - delta
        grad_scores = (full * grad_attn * scale).reshape(4 * PER, n_tiles * PER).astype(BF16)
        low = full.reshape(4 * PER, n_tiles * PER).astype(BF16)
        key_parts.append(join_heads(dot(grad_scores, queries), width))
        value_parts.append(join_heads(dot(low, grads), width))
    grad_kn = jnp.concatenate(key_parts, axis=1)
    grad_key = head_back(k_normal, k_factor, grad_kn, ones, width).astype(BF16)
    grad_value = jnp.concatenate(value_parts, axis=1).astype(BF16)
    gk_out[...] = grad_key
    gv_out[...] = grad_value
    store_terms(fast, core, [dot_tn(x_own, grad_key), dot_tn(x_own, grad_value)], outs)


def final_kernel(tokens, wq, wk, wv, gq, gk, gv, gout, out):
    model = gk.shape[1]
    grad_lowered = (
        dot_nt(gq[...], wq[...]) + dot_nt(gk[...], wk[...]) + dot_nt(gv[...], wv[...])
    )
    normed, inv_std = normalise(tiles_of(tokens[...].astype(F32)))
    grads = gout[...] + inv_std * (
        grad_lowered
        - jnp.mean(grad_lowered, axis=-1, keepdims=True)
        - normed * jnp.mean(grad_lowered * normed, axis=-1, keepdims=True)
    )
    pieces = [grads[t * PER : (t + 1) * PER].reshape(TILE, TILE, model) for t in range(2)]
    out[...] = jnp.concatenate(pieces, axis=1).astype(BF16)


ANY = pl.BlockSpec(memory_space=pl.ANY)
SMEM = pl.BlockSpec(memory_space=pltpu.SMEM)
VMEM = pl.BlockSpec(memory_space=pltpu.VMEM)


def in_hbm(value):
    return pltpu.with_memory_space_constraint(value, pltpu.HBM)


def call(kernel, in_specs, shapes, args, scratch=(), kept=0, held=()):
    args = [
        pltpu.with_memory_space_constraint(a, pltpu.VMEM) if n in held else a
        for n, a in enumerate(args)
    ]
    return pl.pallas_call(
        kernel,
        out_shape=[
            pltpu.VMEM(s, t) if n < kept else jax.ShapeDtypeStruct(s, t)
            for n, (s, t) in enumerate(shapes)
        ],
        in_specs=in_specs,
        out_specs=[VMEM] * len(shapes),
        scratch_shapes=list(scratch),
        compiler_params=pltpu.CompilerParams(vmem_limit_bytes=VMEM_LIMIT),
    )(*args)


def swap(value, count, mask):
    return lax.ppermute(value, AXES, [(i, i ^ mask) for i in range(count)])


def side_pairs(length, side):
    pairs = []
    for i in range(side, length - 1, 2):
        pairs += [(i, i + 1), (i + 1, i)]
    return pairs


def beside(strip):
    rows = lax.axis_size("rows")
    near = lax.ppermute(strip, "rows", side_pairs(rows, 0))
    return [strip, near, lax.ppermute(strip, "rows", side_pairs(rows, 1))]


def across(strips):
    cols = lax.axis_size("cols")
    return [
        lax.ppermute(strip, "cols", side_pairs(cols, n))
        for n in range(1 if cols == 2 else 2)
        for strip in strips
    ]


def layer(tokens, teacher, tissue, weights):
    model = tokens.shape[2]
    rows, cols = lax.axis_size("rows"), lax.axis_size("cols")
    count = rows * cols
    groups = 3 if cols == 2 else 4
    per_block = 4 * model // count
    fast = count & (count - 1) == 0 and count >= 16 and per_block % 16 == 0
    per_matrix = count // 4
    spots = per_matrix // 2
    index = lax.axis_index("rows") * cols + lax.axis_index("cols")
    odd = lax.axis_index("cols") % 2
    own = 2 * PER
    n_keys = 3 * groups * PER
    n_strips = 3 * (groups - 1)

    def spot(d):
        return (d % 2) * (count // 2) + (d // 2 % spots) * 4 + d // per_matrix

    if fast:
        place, base = [spot(d) for d in range(count)], spot(index)
    else:
        place, base = list(range(4)), jnp.int32(0)
    scalars = jnp.stack([odd, base, index % 2, index]).astype(jnp.int32)

    (low,) = call(
        prep_kernel,
        [SMEM, VMEM],
        [((2, BLK, model), BF16)],
        (
            in_hbm(tissue),
            in_hbm(tokens),
        ),
    )
    if fast:
        wblk = weights.reshape(1, per_block, model)
        parts = [swap(wblk, count, per_matrix * step) for step in range(1, 4)]
        wblk = jnp.concatenate([wblk] + parts, axis=0)
        parts = [swap(wblk, count, 2 * step) for step in range(1, spots)]
        strips = beside(low)
        wblk = jnp.concatenate([wblk] + parts, axis=0)
        halves = [wblk, swap(wblk, count, 1)]
        strips = strips + across(strips)
    else:
        strips = beside(low)
        strips = strips + across(strips)
        wblk = lax.all_gather(weights, AXES, axis=0, tiled=True).reshape(4, model, model)
        halves = [wblk[0:2], wblk[2:4]]

    wq, wk, wv, x, k, v, mixed, gout, near, stats, pack = call(
        functools.partial(forward_kernel, groups, place),
        [SMEM] + [VMEM] * (4 + n_strips),
        [((model, model), BF16)] * 3
        + [((n_keys, model), BF16)] * 2
        + [((n_keys + 2 * BLK, model), BF16)]
        + [
            ((own, model), BF16),
            ((own, model), F32),
            ((2, n_keys), F32),
            ((own, own), F32),
            ((2, BLK, model), BF16),
        ],
        (scalars, *halves, tokens, in_hbm(teacher), *map(in_hbm, strips[:3]), *strips[3:]),
        scratch=[pltpu.VMEM((model, model), BF16)],
        kept=10,
    )
    packs = beside(pack)
    packs = packs + across(packs)

    if fast:
        term_shapes = [
            ((2, spots, per_block, model), F32),
            ((2, spots, per_block, model), BF16),
        ]
    else:
        term_shapes = [((2, model, model), F32)]
    gq, *terms_qo = call(
        functools.partial(query_kernel, fast),
        [SMEM] + [VMEM] * 8,
        [((own, model), BF16)] + term_shapes,
        (scalars, wq, x, k, v, mixed, gout, near, stats),
        kept=2,
        held=range(1, 9),
    )
    (q,) = call(
        halo_query_kernel, [VMEM] * 2, [((n_keys, model), BF16)], (wq, x), kept=1, held=range(2)
    )
    more = []
    if fast:
        more = [terms_qo[0], swap(terms_qo[1], count, 1)]
    results = call(
        functools.partial(key_kernel, groups, fast),
        [SMEM] + [VMEM] * (4 + n_strips + len(more)),
        term_shapes[: len(more) // 2] + [((own, model), BF16)] * 2 + term_shapes,
        (scalars, x, k, v, wk, q, *packs[1:], *more),
        scratch=[pltpu.VMEM((n_keys, model), BF16)],
        kept=5 if fast else 2,
        held=[*range(1, 6)] + ([5 + n_strips] if fast else []),
    )
    sums_qo, results = (results[0], results[1:]) if fast else (None, results)
    gk, gv, *terms_kv = results
    (grads,) = call(
        final_kernel,
        [VMEM] * 8,
        [(tokens.shape, BF16)],
        (tokens, wq, wk, wv, gq, gk, gv, gout),
        held=range(1, 8),
    )

    n_tokens = tokens.shape[0] * rows * tokens.shape[1] * cols
    norm = math.sqrt(n_tokens)
    if not fast:
        whole = jnp.stack([terms_qo[0][0], terms_kv[0][0], terms_kv[0][1], terms_qo[0][1]])
        sums = lax.psum_scatter(whole.reshape(-1), AXES, scatter_dimension=0, tiled=True)
        return grads, sums / norm

    here, mine = index // 2 % spots, index // per_matrix

    def pick(values, at, axis):
        return lax.dynamic_index_in_dim(values, at, axis, keepdims=False)

    sums_kv = terms_kv[0] + swap(terms_kv[1], count, 1).astype(F32)

    def all_four(at):
        qo, kv = pick(sums_qo, at, 1), pick(sums_kv, at, 1)
        return jnp.concatenate([qo[0:1], kv, qo[1:2]], axis=0)

    arrived = [
        swap(all_four(here ^ step).astype(BF16), count, 2 * step) for step in range(1, spots)
    ]
    pieces = all_four(here)
    for part in arrived:
        pieces = pieces + part.astype(F32)
    arrived = [
        swap(pick(pieces, mine ^ step, 0).astype(BF16), count, per_matrix * step)
        for step in range(1, 4)
    ]
    result = pick(pieces, mine, 0)
    for part in arrived:
        result = result + part.astype(F32)
    return grads, (result / norm).reshape(-1)


def solution(mesh):
    return jax.shard_map(
        layer,
        mesh=mesh,
        in_specs=(
            P("rows", "cols", None),
            P("rows", "cols", None),
            P("rows", "cols"),
            P(("rows", "cols")),
        ),
        out_specs=(P("rows", "cols", None), P(("rows", "cols"))),
        check_vma=False,
    )
```

```python
import functools
import math

import jax
import jax.numpy as jnp
from jax import lax
from jax.experimental import pallas as pl
from jax.experimental.pallas import tpu as pltpu
from jax.sharding import PartitionSpec as P


HEADS = 6
TILE = 8
PER = TILE * TILE
BLK = PER + 8
AXES = ("rows", "cols")

norm_epsilon = 1e-05
head_epsilon = 1e-06

F32 = jnp.float32
BF16 = jnp.bfloat16
VMEM_LIMIT = 12 << 20


def dot(a, b):
    return jnp.dot(a, b, preferred_element_type=F32)


def dot_nt(a, b):
    return lax.dot_general(a, b, (((1,), (1,)), ((), ())), preferred_element_type=F32)


def dot_tn(a, b):
    return lax.dot_general(a, b, (((0,), (0,)), ((), ())), preferred_element_type=F32)


def tiles_of(block):
    parts = [
        block[:, t * TILE : (t + 1) * TILE, :].reshape(PER, block.shape[2])
        for t in range(block.shape[1] // TILE)
    ]
    return jnp.concatenate(parts, axis=0)


def normalise(flat):
    mean = jnp.mean(flat, axis=-1, keepdims=True)
    centred = flat - mean
    inv_std = lax.rsqrt(jnp.mean(centred * centred, axis=-1, keepdims=True) + norm_epsilon)
    return centred * inv_std, inv_std


def pair_ones(width):
    row = lax.broadcasted_iota(jnp.int32, (2 * width, 2 * width), 0) // width
    col = lax.broadcasted_iota(jnp.int32, (2 * width, 2 * width), 1) // width
    return (row == col).astype(F32).astype(BF16)


def head_sums(x, ones):
    step = ones.shape[0]
    high = x.astype(BF16)
    low = (x - high.astype(F32)).astype(BF16)
    parts = [
        dot(high[:, p : p + step], ones) + dot(low[:, p : p + step], ones)
        for p in range(0, x.shape[1], step)
    ]
    return jnp.concatenate(parts, axis=1)


def head_normalise(raw, ones, width):
    squares = (raw * raw).astype(BF16)
    step = ones.shape[0]
    sums = [dot(squares[:, p : p + step], ones) for p in range(0, raw.shape[1], step)]
    factor = lax.rsqrt(jnp.concatenate(sums, axis=1) * (1.0 / width) + head_epsilon)
    return raw * factor, factor


def head_back(normal, factor, upstream, ones, width):
    inner = head_sums(upstream * normal, ones) * (1.0 / width)
    return factor * (upstream - normal * inner)


def split_heads(pair, width):
    lane = lax.broadcasted_iota(jnp.int32, (1, 2 * width), 1)
    first = (lane < width).astype(F32).astype(BF16)
    second = (lane >= width).astype(F32).astype(BF16)
    return jnp.concatenate([pair * first, pair * second], axis=0)


def join_heads(stacked, width):
    half = stacked.shape[0] // 2
    lane = lax.broadcasted_iota(jnp.int32, (1, 2 * width), 1)
    return jnp.where(lane < width, stacked[:half], stacked[half:])


def strip_tiles(strips, odd):
    tiles = []
    for n in range(3):
        tiles += strips[0] if n == 0 else [strips[n].at[0], strips[n].at[1]]
        for side in range(1, len(strips) // 3):
            tiles.append(strips[3 * side + n].at[odd if side == 1 else 1 - odd])
    return tiles


def own_parts(mine):
    own = 2 * PER
    packs = [mine.at[pl.ds(3 * own + t * BLK, BLK)] for t in range(2)]
    return [mine.at[pl.ds(n * own, own)] for n in range(3)] + [packs]


def pack_stats(stats, width):
    blank = jnp.zeros((8, width - 2 * PER), F32)
    return jnp.concatenate([stats[0:8], stats[8:16], blank], axis=1).astype(BF16)


def unpack_stats(tile):
    rows = tile[PER:BLK, 0 : 2 * PER].astype(F32)
    return jnp.concatenate([rows[:, 0:PER], rows[:, PER:]], axis=0)


def near_rows(groups, odd, n_tiles):
    lanes = n_tiles * PER
    group = (lax.broadcasted_iota(jnp.int32, (1, lanes), 1) // PER) % groups
    oddf = odd.astype(F32)
    left = jnp.where(group == 2, oddf, jnp.where(group == 3, 1.0 - oddf, 1.0))
    right = jnp.where(group == 2, 1.0 - oddf, jnp.where(group == 3, oddf, 1.0))
    return left, right


def prep_kernel(tissue, tokens, low_out):
    normed, _ = normalise(tiles_of(tokens[...].astype(F32)))
    low = normed.astype(BF16)
    width = low.shape[1]
    for t in range(2):
        low_out[t, 0:PER, :] = low[t * PER : (t + 1) * PER]
        low_out[t, PER:BLK, :] = jnp.full((BLK - PER, width), tissue[0, t].astype(F32)).astype(BF16)


def pile_kernel(*refs):
    *parts, out = refs
    for n, part in enumerate(parts):
        out[n] = part[0]


def assemble(index, spots, parts, out):
    z_count, per_block, _ = parts[0].shape
    for p, part in enumerate(parts):
        inner = jnp.bitwise_xor(index % (2 * spots), p)
        at = pl.multiple_of(inner * per_block, 16)
        for z in range(z_count):
            matrix = jnp.bitwise_xor(index // (2 * spots), z)
            out[matrix, pl.ds(at, per_block), :] = part[z]


def forward_kernel(groups, spots, *refs):
    scalars, tokens, teacher, *refs = refs
    n_strips = 3 * (groups - 1)
    n_parts = max(1, 2 * spots)
    parts, refs = refs[:n_parts], refs[n_parts:]
    (
        wq_out,
        wk_out,
        wv_out,
        x_out,
        k_out,
        v_out,
        mixed_out,
        gout_out,
        near_out,
        stats_out,
        mine_out,
        pack_out,
        w_scr,
        teacher_scr,
        sem,
    ) = refs[n_strips:]
    copy = pltpu.make_async_copy(teacher, teacher_scr, sem)
    copy.start()
    odd, index = scalars[0], scalars[3]
    own_strip, *others = refs[:n_strips]
    tiles = strip_tiles([[own_strip.at[0], own_strip.at[1]], *others], odd)
    model = tokens.shape[2]
    width = model // HEADS
    own = 2 * PER
    if spots > 0:
        assemble(index, spots, parts, w_scr)
    else:
        w_scr[...] = parts[0][...]
    for n, whole in enumerate((wq_out, wk_out, wv_out)):
        whole[...] = w_scr[n]
    n_tiles = 3 * groups
    flag_rows = []
    ones = pair_ones(width)
    for n, tile in enumerate(tiles):
        x_out[n * PER : (n + 1) * PER, :] = tile[0:PER, :]
        flag_rows.append(tile[PER:BLK, :].astype(F32)[0:1, 0:PER])
    x = x_out[...]
    k_normal, _ = head_normalise(dot(x, wk_out[...]), ones, width)
    keys = k_normal.astype(BF16)
    values = dot(x, wv_out[...]).astype(BF16)
    q_normal, _ = head_normalise(dot(x[0:own], wq_out[...]), ones, width)
    queries = q_normal.astype(BF16)
    k_out[...] = keys
    v_out[...] = values
    *own_outs, packs = own_parts(mine_out)
    for own_out, source in zip(own_outs, (x_out, k_out, v_out), strict=True):
        own_out[...] = source[0:own, :]

    flags = jnp.concatenate(flag_rows, axis=1)
    left, right = near_rows(groups, odd, n_tiles)
    near_out[...] = jnp.concatenate([flags * left, flags * right], axis=0)
    near = jnp.stack([flags * left, flags * right] * 2)
    own_mask = [flag_rows[t][0:1, 0:1] for t in range(2)]
    query_mask = jnp.concatenate(
        [jnp.broadcast_to(own_mask[t], (PER, 1)) for t in range(2)], axis=0
    )
    rest = 1.0 - jnp.concatenate([query_mask, query_mask], axis=0).reshape(4, PER, 1)
    scale = 1.0 / math.sqrt(width)
    mixed_parts, inverses = [], []
    for p in range(HEADS // 2):
        lanes = slice(2 * width * p, 2 * width * (p + 1))
        scores = dot_nt(split_heads(queries[:, lanes] * scale, width), keys[:, lanes])
        raised = jnp.exp(scores).reshape(4, PER, n_tiles * PER) * near
        total = jnp.sum(raised, axis=-1, keepdims=True) + rest
        inverse = (1.0 / total).astype(BF16).astype(F32)
        low = (raised * inverse).reshape(4 * PER, n_tiles * PER).astype(BF16)
        mixed_parts.append(join_heads(dot(low, values[:, lanes]), width))
        inverse = inverse.reshape(4 * PER, 1)
        inverses += [inverse[0:own], inverse[own:]]
    mixed = (jnp.concatenate(mixed_parts, axis=1) * query_mask).astype(BF16)
    mixed_out[...] = mixed
    w_o = w_scr[3]
    copy.wait()
    residual = tiles_of(tokens[...].astype(F32)) + dot(mixed, w_o)
    grad_out = query_mask * (residual - tiles_of(teacher_scr[...].astype(F32)))
    gout_out[...] = grad_out
    grad_mixed = dot_nt(grad_out.astype(BF16), w_o).astype(BF16)
    delta = head_sums(grad_mixed.astype(F32) * mixed.astype(F32), ones)
    lane = lax.broadcasted_iota(jnp.int32, (1, own), 1)
    table = jnp.zeros((own, own), F32)
    for h in range(HEADS):
        table = jnp.where(lane == h, inverses[h], table)
        table = jnp.where(lane == HEADS + h, delta[:, h * width : h * width + 1], table)
    table = jnp.where(lane == 2 * HEADS, query_mask, table)
    stats_out[...] = table
    stats = table.T[0:16, :]
    for t in range(2):
        here = slice(t * PER, (t + 1) * PER)
        pack_out[t, 0:PER, :] = grad_mixed[here]
        pack_out[t, PER:BLK, :] = pack_stats(stats[:, here], model)
        packs[t][...] = pack_out[t]


def store_terms(fast, odd, grads, outs):
    if not fast:
        for m, grad in enumerate(grads):
            outs[0][m] = grad
        return
    keep, send = outs
    rows = keep.shape[2]
    for m, grad in enumerate(grads):
        for b in range(keep.shape[1]):
            even_part = grad[2 * b * rows : (2 * b + 1) * rows]
            odd_part = grad[(2 * b + 1) * rows : (2 * b + 2) * rows]
            is_odd = odd == 1
            keep[m, b] = jnp.where(is_odd, odd_part, even_part).astype(BF16)
            send[m, b] = jnp.where(is_odd, even_part, odd_part).astype(BF16)


def halo_query_kernel(wq, x, q_out):
    model = x.shape[1]
    width = model // HEADS
    q_normal, _ = head_normalise(dot(x[...], wq[...]), pair_ones(width), width)
    q_out[...] = q_normal.astype(BF16)


def query_kernel(fast, scalars, wq, k, v, mixed, gout, near_in, stats_in, mine, *outs):
    core = scalars[2]
    model = wq.shape[0]
    width = model // HEADS
    n_tiles = near_in.shape[1] // PER
    ones = pair_ones(width)
    x_own, _, _, packs = own_parts(mine)
    q_normal, q_factor = head_normalise(dot(x_own[...], wq[...]), ones, width)
    queries = q_normal.astype(BF16)
    near = jnp.stack([near_in[0:1], near_in[1:2]] * 2)
    stats = stats_in[...].astype(BF16).astype(F32)
    gq_out, *outs = outs
    grad_mixed = jnp.concatenate([pack[0:PER, :] for pack in packs], axis=0)
    scale = 1.0 / math.sqrt(width)
    parts = []
    for p in range(HEADS // 2):
        lanes = slice(2 * width * p, 2 * width * (p + 1))
        keys, values = k[:, lanes], v[:, lanes]
        scores = dot_nt(split_heads(queries[:, lanes] * scale, width), keys)
        inverse = jnp.concatenate([stats[:, 2 * p : 2 * p + 1], stats[:, 2 * p + 1 : 2 * p + 2]], axis=0)
        at = HEADS + 2 * p
        delta = jnp.concatenate([stats[:, at : at + 1], stats[:, at + 1 : at + 2]], axis=0)
        full = jnp.exp(scores).reshape(4, PER, n_tiles * PER) * near
        full = full.reshape(4 * PER, n_tiles * PER) * inverse
        grad_attn = dot_nt(split_heads(grad_mixed[:, lanes], width), values)
        grad_scores = (full * (grad_attn - delta)).astype(BF16)
        parts.append(join_heads(dot(grad_scores, keys), width) * scale)
    grad_qn = jnp.concatenate(parts, axis=1)
    grad_query = head_back(q_normal, q_factor, grad_qn, ones, width).astype(BF16)
    gq_out[...] = grad_query
    grad_wq = dot_tn(x_own[...], grad_query)
    grad_wo = dot_tn(mixed[...], gout[...].astype(BF16))
    store_terms(fast, core, [grad_wq, grad_wo], outs)


def key_kernel(groups, fast, scalars, mine, wk, q, *refs):
    n_strips = 3 * (groups - 1)
    sources, refs = refs[: n_strips - 1], refs[n_strips - 1 :]
    if fast:
        kept, arrived, sums_out, *refs = refs
        sums_out[...] = (kept[...].astype(F32) + arrived[...].astype(F32)).astype(BF16)
    *refs, g_scr = refs
    gk_out, gv_out, *outs = refs
    odd, core = scalars[0], scalars[2]
    model = q.shape[1]
    width = model // HEADS
    n_tiles = 3 * groups
    ones = pair_ones(width)
    x, k, v, packs = own_parts(mine)
    tiles = strip_tiles([packs, *sources], odd)
    x_own = x[...]
    k_normal, k_factor = head_normalise(dot(x_own, wk[...]), ones, width)
    stat_parts = []
    for n, tile in enumerate(tiles):
        g_scr[n * PER : (n + 1) * PER, :] = tile[0:PER, :]
        stat_parts.append(unpack_stats(tile))
    stats = jnp.concatenate(stat_parts, axis=1)
    left, right = near_rows(groups, odd, n_tiles)
    flag = stats[2 * HEADS : 2 * HEADS + 1]
    near = [left * flag[:, 0:1], right * flag[:, PER : PER + 1]]
    scale = 1.0 / math.sqrt(width)
    key_parts, value_parts = [], []
    for p in range(HEADS // 2):
        lanes = slice(2 * width * p, 2 * width * (p + 1))
        queries, grads = q[:, lanes], g_scr[:, lanes]
        scores = dot_nt(split_heads(k[:, lanes] * scale, width), queries)
        inv = [stats[2 * p + j : 2 * p + j + 1] for j in range(2)]
        rows = jnp.stack([inv[j] * near[t] for j in range(2) for t in range(2)])
        at = HEADS + 2 * p
        delta = jnp.stack([stats[at + j : at + j + 1] for j in range(2) for _ in range(2)])
        full = jnp.exp(scores).reshape(4, PER, n_tiles * PER) * rows
        grad_attn = dot_nt(split_heads(v[:, lanes], width), grads)
        grad_attn = grad_attn.reshape(4, PER, n_tiles * PER) - delta
        grad_scores = (full * grad_attn).reshape(4 * PER, n_tiles * PER).astype(BF16)
        low = full.reshape(4 * PER, n_tiles * PER).astype(BF16)
        key_parts.append(join_heads(dot(grad_scores, queries), width) * scale)
        value_parts.append(join_heads(dot(low, grads), width))
    grad_kn = jnp.concatenate(key_parts, axis=1)
    grad_key = head_back(k_normal, k_factor, grad_kn, ones, width).astype(BF16)
    grad_value = jnp.concatenate(value_parts, axis=1).astype(BF16)
    gk_out[...] = grad_key
    gv_out[...] = grad_value
    store_terms(fast, core, [dot_tn(x_own, grad_key), dot_tn(x_own, grad_value)], outs)


def final_kernel(tokens, wq, wk, wv, gq, gk, gv, gout, out):
    model = gk.shape[1]
    grad_lowered = (
        dot_nt(gq[...], wq[...]) + dot_nt(gk[...], wk[...]) + dot_nt(gv[...], wv[...])
    )
    normed, inv_std = normalise(tiles_of(tokens[...].astype(F32)))
    grads = gout[...] + inv_std * (
        grad_lowered
        - jnp.mean(grad_lowered, axis=-1, keepdims=True)
        - normed * jnp.mean(grad_lowered * normed, axis=-1, keepdims=True)
    )
    pieces = [grads[t * PER : (t + 1) * PER].reshape(TILE, TILE, model) for t in range(2)]
    out[...] = jnp.concatenate(pieces, axis=1).astype(BF16)


ANY = pl.BlockSpec(memory_space=pl.ANY)
SMEM = pl.BlockSpec(memory_space=pltpu.SMEM)
VMEM = pl.BlockSpec(memory_space=pltpu.VMEM)


def in_hbm(value):
    return pltpu.with_memory_space_constraint(value, pltpu.HBM)


def in_vmem(value):
    return pltpu.with_memory_space_constraint(value, pltpu.VMEM)


def call(kernel, in_specs, shapes, args, scratch=(), kept=0, held=()):
    args = [
        pltpu.with_memory_space_constraint(a, pltpu.VMEM) if n in held else a
        for n, a in enumerate(args)
    ]
    return pl.pallas_call(
        kernel,
        out_shape=[
            pltpu.VMEM(s, t) if n < kept else jax.ShapeDtypeStruct(s, t)
            for n, (s, t) in enumerate(shapes)
        ],
        in_specs=in_specs,
        out_specs=[VMEM] * len(shapes),
        scratch_shapes=list(scratch),
        compiler_params=pltpu.CompilerParams(vmem_limit_bytes=VMEM_LIMIT),
    )(*args)


def swap(value, count, mask):
    return lax.ppermute(value, AXES, [(i, i ^ mask) for i in range(count)])


def side_pairs(length, side):
    pairs = []
    for i in range(side, length - 1, 2):
        pairs += [(i, i + 1), (i + 1, i)]
    return pairs


def beside(strip):
    rows = lax.axis_size("rows")
    near = lax.ppermute(strip, "rows", side_pairs(rows, 0))
    return [strip, near, lax.ppermute(strip, "rows", side_pairs(rows, 1))]


def across(strips):
    cols = lax.axis_size("cols")
    return [
        lax.ppermute(strip, "cols", side_pairs(cols, n))
        for n in range(1 if cols == 2 else 2)
        for strip in strips
    ]


def layer(tokens, teacher, tissue, weights):
    model = tokens.shape[2]
    rows, cols = lax.axis_size("rows"), lax.axis_size("cols")
    count = rows * cols
    groups = 3 if cols == 2 else 4
    per_block = 4 * model // count
    fast = count & (count - 1) == 0 and count >= 16 and per_block % 16 == 0
    per_matrix = count // 4
    spots = per_matrix // 2
    index = lax.axis_index("rows") * cols + lax.axis_index("cols")
    odd = lax.axis_index("cols") % 2
    own = 2 * PER
    n_keys = 3 * groups * PER
    n_strips = 3 * (groups - 1)

    scalars = jnp.stack([odd, index % 2, index % 2, index]).astype(jnp.int32)

    (low,) = call(
        prep_kernel,
        [SMEM, VMEM],
        [((2, BLK, model), BF16)],
        (
            in_hbm(tissue),
            in_hbm(tokens),
        ),
    )
    if fast:
        block = weights.reshape(1, per_block, model)
        parts = [block] + [swap(block, count, per_matrix * step) for step in range(1, 4)]
        (pile,) = call(
            pile_kernel,
            [VMEM] * 4,
            [((4, per_block, model), BF16)],
            parts,
            kept=1,
            held=range(1, 4),
        )
        piles = [pile] + [swap(pile, count, 2 * step) for step in range(1, spots)]
        strips = beside(low)
        wide = [swap(pile, count, 1) for pile in piles]
        parts = [in_vmem(part) for pair in zip(piles, wide, strict=True) for part in pair]
        strips = strips + across(strips)
    else:
        strips = beside(low)
        strips = strips + across(strips)
        whole = lax.all_gather(weights, AXES, axis=0, tiled=True)
        parts = [whole.reshape(4, model, model)]

    wq, wk, wv, x, k, v, mixed, gout, near, stats, mine, pack = call(
        functools.partial(forward_kernel, groups, spots if fast else 0),
        [SMEM, VMEM, ANY] + [VMEM] * (len(parts) + n_strips),
        [((model, model), BF16)] * 3
        + [((n_keys, model), BF16)] * 3
        + [
            ((own, model), BF16),
            ((own, model), F32),
            ((2, n_keys), F32),
            ((own, own), F32),
            ((3 * own + 2 * BLK, model), BF16),
            ((2, BLK, model), BF16),
        ],
        (scalars, tokens, in_hbm(teacher), *parts, *map(in_vmem, strips)),
        scratch=[
            pltpu.VMEM((4, model, model), BF16),
            pltpu.VMEM(teacher.shape, BF16),
            pltpu.SemaphoreType.DMA,
        ],
        kept=11,
    )
    packs = beside(pack)
    packs = packs + across(packs)

    if fast:
        term_shapes = [((2, spots, per_block, model), BF16)] * 2
    else:
        term_shapes = [((2, model, model), F32)]
    gq, *terms_qo = call(
        functools.partial(query_kernel, fast),
        [SMEM] + [VMEM] * 8,
        [((own, model), BF16)] + term_shapes,
        (scalars, wq, k, v, mixed, gout, near, stats, mine),
        kept=2,
        held=range(1, 9),
    )
    (q,) = call(
        halo_query_kernel, [VMEM] * 2, [((n_keys, model), BF16)], (wq, x), kept=1, held=range(2)
    )
    more = []
    if fast:
        more = [terms_qo[0], swap(terms_qo[1], count, 1)]
    results = call(
        functools.partial(key_kernel, groups, fast),
        [SMEM] + [VMEM] * (2 + n_strips + len(more)),
        term_shapes[: len(more) // 2] + [((own, model), BF16)] * 2 + term_shapes,
        (scalars, mine, wk, q, *map(in_vmem, packs[1:]), *more),
        scratch=[pltpu.VMEM((n_keys, model), BF16)],
        kept=5 if fast else 2,
        held=[1, 2, 3] + ([3 + n_strips] if fast else []),
    )
    sums_qo, results = (results[0], results[1:]) if fast else (None, results)
    gk, gv, *terms_kv = results
    (grads,) = call(
        final_kernel,
        [VMEM] * 8,
        [(tokens.shape, BF16)],
        (tokens, wq, wk, wv, gq, gk, gv, gout),
        held=range(1, 8),
    )

    n_tokens = tokens.shape[0] * rows * tokens.shape[1] * cols
    norm = math.sqrt(n_tokens)
    if not fast:
        whole = jnp.stack([terms_qo[0][0], terms_kv[0][0], terms_kv[0][1], terms_qo[0][1]])
        sums = lax.psum_scatter(whole.reshape(-1), AXES, scatter_dimension=0, tiled=True)
        return grads, sums / norm

    here, mine = index // 2 % spots, index // per_matrix

    def pick(values, at, axis):
        return lax.dynamic_index_in_dim(values, at, axis, keepdims=False)

    arrived = swap(terms_kv[1], count, 1).astype(F32)
    sums_kv = (terms_kv[0].astype(F32) + arrived).astype(BF16)

    def all_four(at):
        qo, kv = pick(sums_qo, at, 1), pick(sums_kv, at, 1)
        return jnp.concatenate([qo[0:1], kv, qo[1:2]], axis=0)

    arrived = [
        swap(all_four(here ^ step), count, 2 * step) for step in range(1, spots)
    ]
    pieces = all_four(here).astype(F32)
    for part in arrived:
        pieces = pieces + part.astype(F32)
    arrived = [
        swap(pick(pieces, mine ^ step, 0).astype(BF16), count, per_matrix * step)
        for step in range(1, 4)
    ]
    result = pick(pieces, mine, 0)
    for part in arrived:
        result = result + part.astype(F32)
    return grads, (result / norm).reshape(-1)


def solution(mesh):
    return jax.shard_map(
        layer,
        mesh=mesh,
        in_specs=(
            P("rows", "cols", None),
            P("rows", "cols", None),
            P("rows", "cols"),
            P(("rows", "cols")),
        ),
        out_specs=(P("rows", "cols", None), P(("rows", "cols"))),
        check_vma=False,
    )
```

```python
import functools
import math

import jax
import jax.numpy as jnp
from jax import lax
from jax.experimental import pallas as pl
from jax.experimental.pallas import tpu as pltpu
from jax.sharding import PartitionSpec as P


HEADS = 6
TILE = 8
PER = TILE * TILE
BLK = PER + 8
AXES = ("rows", "cols")

norm_epsilon = 1e-05
head_epsilon = 1e-06

F32 = jnp.float32
BF16 = jnp.bfloat16
VMEM_LIMIT = 12 << 20


def dot(a, b):
    return jnp.dot(a, b, preferred_element_type=F32)


def dot_nt(a, b):
    return lax.dot_general(a, b, (((1,), (1,)), ((), ())), preferred_element_type=F32)


def dot_tn(a, b):
    return lax.dot_general(a, b, (((0,), (0,)), ((), ())), preferred_element_type=F32)


def tiles_of(block):
    parts = [
        block[:, t * TILE : (t + 1) * TILE, :].reshape(PER, block.shape[2])
        for t in range(block.shape[1] // TILE)
    ]
    return jnp.concatenate(parts, axis=0)


def normalise(flat):
    mean = jnp.mean(flat, axis=-1, keepdims=True)
    centred = flat - mean
    inv_std = lax.rsqrt(jnp.mean(centred * centred, axis=-1, keepdims=True) + norm_epsilon)
    return centred * inv_std, inv_std


def pair_ones(width):
    row = lax.broadcasted_iota(jnp.int32, (2 * width, 2 * width), 0) // width
    col = lax.broadcasted_iota(jnp.int32, (2 * width, 2 * width), 1) // width
    return (row == col).astype(F32).astype(BF16)


def head_sums(x, ones):
    step = ones.shape[0]
    high = x.astype(BF16)
    low = (x - high.astype(F32)).astype(BF16)
    parts = [
        dot(high[:, p : p + step], ones) + dot(low[:, p : p + step], ones)
        for p in range(0, x.shape[1], step)
    ]
    return jnp.concatenate(parts, axis=1)


def head_normalise(raw, ones, width):
    squares = (raw * raw).astype(BF16)
    step = ones.shape[0]
    sums = [dot(squares[:, p : p + step], ones) for p in range(0, raw.shape[1], step)]
    factor = lax.rsqrt(jnp.concatenate(sums, axis=1) * (1.0 / width) + head_epsilon)
    return raw * factor, factor


def head_back(normal, factor, upstream, ones, width):
    inner = head_sums(upstream * normal, ones) * (1.0 / width)
    return factor * (upstream - normal * inner)


def split_heads(pair, width):
    lane = lax.broadcasted_iota(jnp.int32, (1, 2 * width), 1)
    first = (lane < width).astype(F32).astype(BF16)
    second = (lane >= width).astype(F32).astype(BF16)
    return jnp.concatenate([pair * first, pair * second], axis=0)


def join_heads(stacked, width):
    half = stacked.shape[0] // 2
    lane = lax.broadcasted_iota(jnp.int32, (1, 2 * width), 1)
    return jnp.where(lane < width, stacked[:half], stacked[half:])


def strip_tiles(strips, odd):
    tiles = []
    for n in range(3):
        tiles += strips[0] if n == 0 else [strips[n].at[0], strips[n].at[1]]
        for side in range(1, len(strips) // 3):
            tiles.append(strips[3 * side + n].at[odd if side == 1 else 1 - odd])
    return tiles


def own_parts(mine):
    own = 2 * PER
    packs = [mine.at[pl.ds(3 * own + t * BLK, BLK)] for t in range(2)]
    return [mine.at[pl.ds(n * own, own)] for n in range(3)] + [packs]


def pack_stats(stats, width):
    blank = jnp.zeros((8, width - 2 * PER), F32)
    return jnp.concatenate([stats[0:8], stats[8:16], blank], axis=1).astype(BF16)


def unpack_stats(tile):
    rows = tile[PER:BLK, 0 : 2 * PER].astype(F32)
    return jnp.concatenate([rows[:, 0:PER], rows[:, PER:]], axis=0)


def near_rows(groups, odd, n_tiles):
    lanes = n_tiles * PER
    group = (lax.broadcasted_iota(jnp.int32, (1, lanes), 1) // PER) % groups
    oddf = odd.astype(F32)
    left = jnp.where(group == 2, oddf, jnp.where(group == 3, 1.0 - oddf, 1.0))
    right = jnp.where(group == 2, 1.0 - oddf, jnp.where(group == 3, oddf, 1.0))
    return left, right


def prep_kernel(tissue, tokens, low_out):
    normed, _ = normalise(tiles_of(tokens[...].astype(F32)))
    low = normed.astype(BF16)
    width = low.shape[1]
    for t in range(2):
        low_out[t, 0:PER, :] = low[t * PER : (t + 1) * PER]
        low_out[t, PER:BLK, :] = jnp.full((BLK - PER, width), tissue[0, t].astype(F32)).astype(BF16)


def pile_kernel(*refs):
    *parts, out = refs
    for n, part in enumerate(parts):
        out[n] = part[0]


def assemble(index, spots, parts, out):
    z_count, per_block, _ = parts[0].shape
    for p, part in enumerate(parts):
        inner = jnp.bitwise_xor(index % (2 * spots), p)
        at = pl.multiple_of(inner * per_block, 16)
        for z in range(z_count):
            matrix = jnp.bitwise_xor(index // (2 * spots), z)
            out[matrix, pl.ds(at, per_block), :] = part[z]


def forward_kernel(groups, spots, *refs):
    scalars, tokens, teacher, *refs = refs
    n_strips = 3 * (groups - 1)
    n_parts = max(1, 2 * spots)
    parts, refs = refs[:n_parts], refs[n_parts:]
    (
        wq_out,
        wk_out,
        wv_out,
        x_out,
        k_out,
        v_out,
        mixed_out,
        gout_out,
        near_out,
        stats_out,
        mine_out,
        pack_out,
        w_scr,
        teacher_scr,
        sem,
    ) = refs[n_strips:]
    copy = pltpu.make_async_copy(teacher, teacher_scr, sem)
    copy.start()
    odd, index = scalars[0], scalars[3]
    own_strip, *others = refs[:n_strips]
    tiles = strip_tiles([[own_strip.at[0], own_strip.at[1]], *others], odd)
    model = tokens.shape[2]
    width = model // HEADS
    own = 2 * PER
    if spots > 0:
        assemble(index, spots, parts, w_scr)
    else:
        w_scr[...] = parts[0][...]
    for n, whole in enumerate((wq_out, wk_out, wv_out)):
        whole[...] = w_scr[n]
    n_tiles = 3 * groups
    flag_rows = []
    ones = pair_ones(width)
    for n, tile in enumerate(tiles):
        x_out[n * PER : (n + 1) * PER, :] = tile[0:PER, :]
        flag_rows.append(tile[PER:BLK, :].astype(F32)[0:1, 0:PER])
    x = x_out[...]
    k_normal, _ = head_normalise(dot(x, wk_out[...]), ones, width)
    keys = k_normal.astype(BF16)
    values = dot(x, wv_out[...]).astype(BF16)
    q_normal, _ = head_normalise(dot(x[0:own], wq_out[...]), ones, width)
    queries = q_normal.astype(BF16)
    k_out[...] = keys
    v_out[...] = values
    *own_outs, packs = own_parts(mine_out)
    for own_out, source in zip(own_outs, (x_out, k_out, v_out), strict=True):
        own_out[...] = source[0:own, :]

    flags = jnp.concatenate(flag_rows, axis=1)
    left, right = near_rows(groups, odd, n_tiles)
    near_out[...] = jnp.concatenate([flags * left, flags * right], axis=0)
    near = jnp.stack([flags * left, flags * right] * 2)
    own_mask = [flag_rows[t][0:1, 0:1] for t in range(2)]
    query_mask = jnp.concatenate(
        [jnp.broadcast_to(own_mask[t], (PER, 1)) for t in range(2)], axis=0
    )
    rest = 1.0 - jnp.concatenate([query_mask, query_mask], axis=0).reshape(4, PER, 1)
    scale = 1.0 / math.sqrt(width)
    mixed_parts, inverses = [], []
    for p in range(HEADS // 2):
        lanes = slice(2 * width * p, 2 * width * (p + 1))
        scores = dot_nt(split_heads(queries[:, lanes] * scale, width), keys[:, lanes])
        raised = jnp.exp(scores).reshape(4, PER, n_tiles * PER) * near
        total = jnp.sum(raised, axis=-1, keepdims=True) + rest
        inverse = (1.0 / total).astype(BF16).astype(F32)
        low = (raised * inverse).reshape(4 * PER, n_tiles * PER).astype(BF16)
        mixed_parts.append(join_heads(dot(low, values[:, lanes]), width))
        inverse = inverse.reshape(4 * PER, 1)
        inverses += [inverse[0:own], inverse[own:]]
    mixed = (jnp.concatenate(mixed_parts, axis=1) * query_mask).astype(BF16)
    mixed_out[...] = mixed
    w_o = w_scr[3]
    copy.wait()
    residual = tiles_of(tokens[...].astype(F32)) + dot(mixed, w_o)
    grad_out = query_mask * (residual - tiles_of(teacher_scr[...].astype(F32)))
    gout_out[...] = grad_out
    grad_mixed = dot_nt(grad_out.astype(BF16), w_o).astype(BF16)
    delta = head_sums(grad_mixed.astype(F32) * mixed.astype(F32), ones)
    lane = lax.broadcasted_iota(jnp.int32, (1, own), 1)
    table = jnp.zeros((own, own), F32)
    for h in range(HEADS):
        table = jnp.where(lane == h, inverses[h], table)
        table = jnp.where(lane == HEADS + h, delta[:, h * width : h * width + 1], table)
    table = jnp.where(lane == 2 * HEADS, query_mask, table)
    stats_out[...] = table
    stats = table.T[0:16, :]
    for t in range(2):
        here = slice(t * PER, (t + 1) * PER)
        pack_out[t, 0:PER, :] = grad_mixed[here]
        pack_out[t, PER:BLK, :] = pack_stats(stats[:, here], model)
        packs[t][...] = pack_out[t]


def store_terms(fast, odd, grads, outs):
    if not fast:
        for m, grad in enumerate(grads):
            outs[0][m] = grad
        return
    keep, send = outs
    rows = keep.shape[2]
    for m, grad in enumerate(grads):
        for b in range(keep.shape[1]):
            even_part = grad[2 * b * rows : (2 * b + 1) * rows]
            odd_part = grad[(2 * b + 1) * rows : (2 * b + 2) * rows]
            is_odd = odd == 1
            keep[m, b] = jnp.where(is_odd, odd_part, even_part).astype(BF16)
            send[m, b] = jnp.where(is_odd, even_part, odd_part).astype(BF16)


def halo_query_kernel(wq, x, wk, *refs):
    q_out, kn_out, kf_out, *sums = refs[-4:] if len(refs) > 3 else refs
    model = x.shape[1]
    width = model // HEADS
    ones = pair_ones(width)
    q_normal, _ = head_normalise(dot(x[...], wq[...]), ones, width)
    q_out[...] = q_normal.astype(BF16)
    kn_out[...], kf_out[...] = head_normalise(dot(x[0 : 2 * PER, :], wk[...]), ones, width)
    for sums_out in sums:
        sums_out[...] = (refs[0][...].astype(F32) + refs[1][...].astype(F32)).astype(BF16)


def query_kernel(fast, scalars, wq, k, v, mixed, gout, near_in, stats_in, mine, *outs):
    core = scalars[2]
    model = wq.shape[0]
    width = model // HEADS
    n_tiles = near_in.shape[1] // PER
    ones = pair_ones(width)
    x_own, _, _, packs = own_parts(mine)
    q_normal, q_factor = head_normalise(dot(x_own[...], wq[...]), ones, width)
    queries = q_normal.astype(BF16)
    near = jnp.stack([near_in[0:1], near_in[1:2]] * 2)
    stats = stats_in[...].astype(BF16).astype(F32)
    gq_out, *outs = outs
    grad_mixed = jnp.concatenate([pack[0:PER, :] for pack in packs], axis=0)
    scale = 1.0 / math.sqrt(width)
    parts = []
    for p in range(HEADS // 2):
        lanes = slice(2 * width * p, 2 * width * (p + 1))
        keys, values = k[:, lanes], v[:, lanes]
        scores = dot_nt(split_heads(queries[:, lanes] * scale, width), keys)
        inverse = jnp.concatenate([stats[:, 2 * p : 2 * p + 1], stats[:, 2 * p + 1 : 2 * p + 2]], axis=0)
        at = HEADS + 2 * p
        delta = jnp.concatenate([stats[:, at : at + 1], stats[:, at + 1 : at + 2]], axis=0)
        full = jnp.exp(scores).reshape(4, PER, n_tiles * PER) * near
        full = full.reshape(4 * PER, n_tiles * PER) * inverse
        grad_attn = dot_nt(split_heads(grad_mixed[:, lanes], width), values)
        grad_scores = (full * (grad_attn - delta)).astype(BF16)
        parts.append(join_heads(dot(grad_scores, keys), width) * scale)
    grad_qn = jnp.concatenate(parts, axis=1)
    grad_query = head_back(q_normal, q_factor, grad_qn, ones, width).astype(BF16)
    gq_out[...] = grad_query
    grad_wq = dot_tn(x_own[...], grad_query)
    grad_wo = dot_tn(mixed[...], gout[...].astype(BF16))
    store_terms(fast, core, [grad_wq, grad_wo], outs)


def key_kernel(groups, fast, scalars, mine, q, kn, kf, *refs):
    n_strips = 3 * (groups - 1)
    sources, refs = refs[: n_strips - 1], refs[n_strips - 1 :]
    *refs, g_scr = refs
    gk_out, gv_out, *outs = refs
    odd, core = scalars[0], scalars[2]
    model = q.shape[1]
    width = model // HEADS
    n_tiles = 3 * groups
    ones = pair_ones(width)
    x, k, v, packs = own_parts(mine)
    tiles = strip_tiles([packs, *sources], odd)
    x_own = x[...]
    stat_parts = []
    for n, tile in enumerate(tiles):
        g_scr[n * PER : (n + 1) * PER, :] = tile[0:PER, :]
        stat_parts.append(unpack_stats(tile))
    stats = jnp.concatenate(stat_parts, axis=1)
    left, right = near_rows(groups, odd, n_tiles)
    flag = stats[2 * HEADS : 2 * HEADS + 1]
    near = [left * flag[:, 0:1], right * flag[:, PER : PER + 1]]
    scale = 1.0 / math.sqrt(width)
    key_parts, value_parts = [], []
    for p in range(HEADS // 2):
        lanes = slice(2 * width * p, 2 * width * (p + 1))
        queries, grads = q[:, lanes], g_scr[:, lanes]
        scores = dot_nt(split_heads(k[:, lanes] * scale, width), queries)
        inv = [stats[2 * p + j : 2 * p + j + 1] for j in range(2)]
        rows = jnp.stack([inv[j] * near[t] for j in range(2) for t in range(2)])
        at = HEADS + 2 * p
        delta = jnp.stack([stats[at + j : at + j + 1] for j in range(2) for _ in range(2)])
        full = jnp.exp(scores).reshape(4, PER, n_tiles * PER) * rows
        grad_attn = dot_nt(split_heads(v[:, lanes], width), grads)
        grad_attn = grad_attn.reshape(4, PER, n_tiles * PER) - delta
        grad_scores = (full * grad_attn).reshape(4 * PER, n_tiles * PER).astype(BF16)
        low = full.reshape(4 * PER, n_tiles * PER).astype(BF16)
        key_parts.append(join_heads(dot(grad_scores, queries), width) * scale)
        value_parts.append(join_heads(dot(low, grads), width))
    grad_kn = jnp.concatenate(key_parts, axis=1)
    grad_key = head_back(kn[...], kf[...], grad_kn, ones, width).astype(BF16)
    grad_value = jnp.concatenate(value_parts, axis=1).astype(BF16)
    gk_out[...] = grad_key
    gv_out[...] = grad_value
    store_terms(fast, core, [dot_tn(x_own, grad_key), dot_tn(x_own, grad_value)], outs)


def final_kernel(tokens, wq, wk, wv, gq, gk, gv, gout, out):
    model = gk.shape[1]
    grad_lowered = (
        dot_nt(gq[...], wq[...]) + dot_nt(gk[...], wk[...]) + dot_nt(gv[...], wv[...])
    )
    normed, inv_std = normalise(tiles_of(tokens[...].astype(F32)))
    grads = gout[...] + inv_std * (
        grad_lowered
        - jnp.mean(grad_lowered, axis=-1, keepdims=True)
        - normed * jnp.mean(grad_lowered * normed, axis=-1, keepdims=True)
    )
    pieces = [grads[t * PER : (t + 1) * PER].reshape(TILE, TILE, model) for t in range(2)]
    out[...] = jnp.concatenate(pieces, axis=1).astype(BF16)


ANY = pl.BlockSpec(memory_space=pl.ANY)
SMEM = pl.BlockSpec(memory_space=pltpu.SMEM)
VMEM = pl.BlockSpec(memory_space=pltpu.VMEM)


def in_hbm(value):
    return pltpu.with_memory_space_constraint(value, pltpu.HBM)


def in_vmem(value):
    return pltpu.with_memory_space_constraint(value, pltpu.VMEM)


def call(kernel, in_specs, shapes, args, scratch=(), kept=0, held=()):
    args = [
        pltpu.with_memory_space_constraint(a, pltpu.VMEM) if n in held else a
        for n, a in enumerate(args)
    ]
    return pl.pallas_call(
        kernel,
        out_shape=[
            pltpu.VMEM(s, t) if n < kept else jax.ShapeDtypeStruct(s, t)
            for n, (s, t) in enumerate(shapes)
        ],
        in_specs=in_specs,
        out_specs=[VMEM] * len(shapes),
        scratch_shapes=list(scratch),
        compiler_params=pltpu.CompilerParams(vmem_limit_bytes=VMEM_LIMIT),
    )(*args)


def swap(value, count, mask):
    return lax.ppermute(value, AXES, [(i, i ^ mask) for i in range(count)])


def side_pairs(length, side):
    pairs = []
    for i in range(side, length - 1, 2):
        pairs += [(i, i + 1), (i + 1, i)]
    return pairs


def beside(strip):
    rows = lax.axis_size("rows")
    near = lax.ppermute(strip, "rows", side_pairs(rows, 0))
    return [strip, near, lax.ppermute(strip, "rows", side_pairs(rows, 1))]


def across(strips):
    cols = lax.axis_size("cols")
    sides = []
    for n in range(1 if cols == 2 else 2):
        for strip in strips:
            sides.append(lax.ppermute(strip, "cols", side_pairs(cols, n)))
    return sides


def layer(tokens, teacher, tissue, weights):
    model = tokens.shape[2]
    rows, cols = lax.axis_size("rows"), lax.axis_size("cols")
    count = rows * cols
    groups = 3 if cols == 2 else 4
    per_block = 4 * model // count
    fast = count & (count - 1) == 0 and count >= 16 and per_block % 16 == 0
    per_matrix = count // 4
    spots = per_matrix // 2
    index = lax.axis_index("rows") * cols + lax.axis_index("cols")
    odd = lax.axis_index("cols") % 2
    own = 2 * PER
    n_keys = 3 * groups * PER
    n_strips = 3 * (groups - 1)

    scalars = jnp.stack([odd, index % 2, index % 2, index]).astype(jnp.int32)

    (low,) = call(
        prep_kernel,
        [SMEM, VMEM],
        [((2, BLK, model), BF16)],
        (
            in_hbm(tissue),
            in_hbm(tokens),
        ),
    )
    if fast:
        block = weights.reshape(1, per_block, model)
        parts = [block] + [swap(block, count, per_matrix * step) for step in range(1, 4)]
        (pile,) = call(
            pile_kernel,
            [VMEM] * 4,
            [((4, per_block, model), BF16)],
            parts,
            kept=1,
            held=range(1, 4),
        )
        piles = [pile] + [swap(pile, count, 2 * step) for step in range(1, spots)]
        strips = beside(low)
        wide = []
        for pile in piles:
            wide.append(swap(pile, count, 1))
        parts = [in_vmem(part) for pair in zip(piles, wide, strict=True) for part in pair]
        strips = strips + across(strips)
    else:
        strips = beside(low)
        strips = strips + across(strips)
        whole = lax.all_gather(weights, AXES, axis=0, tiled=True)
        parts = [whole.reshape(4, model, model)]

    wq, wk, wv, x, k, v, mixed, gout, near, stats, mine, pack = call(
        functools.partial(forward_kernel, groups, spots if fast else 0),
        [SMEM, VMEM, ANY] + [VMEM] * (len(parts) + n_strips),
        [((model, model), BF16)] * 3
        + [((n_keys, model), BF16)] * 3
        + [
            ((own, model), BF16),
            ((own, model), F32),
            ((2, n_keys), F32),
            ((own, own), F32),
            ((3 * own + 2 * BLK, model), BF16),
            ((2, BLK, model), BF16),
        ],
        (scalars, tokens, in_hbm(teacher), *parts, *map(in_vmem, strips)),
        scratch=[
            pltpu.VMEM((4, model, model), BF16),
            pltpu.VMEM(teacher.shape, BF16),
            pltpu.SemaphoreType.DMA,
        ],
        kept=11,
    )
    packs = beside(pack)
    packs = packs + across(packs)

    if fast:
        term_shapes = [((2, spots, per_block, model), BF16)] * 2
    else:
        term_shapes = [((2, model, model), F32)]
    gq, *terms_qo = call(
        functools.partial(query_kernel, fast),
        [SMEM] + [VMEM] * 8,
        [((own, model), BF16)] + term_shapes,
        (scalars, wq, k, v, mixed, gout, near, stats, mine),
        kept=2,
        held=range(1, 9),
    )
    more = []
    if fast:
        more = [terms_qo[0], swap(terms_qo[1], count, 1)]
    q, kn, kf, *sums_qo = call(
        halo_query_kernel,
        [VMEM] * (3 + len(more)),
        [((n_keys, model), BF16)] + [((own, model), F32)] * 2 + term_shapes[: len(more) // 2],
        (wq, x, wk, *more),
        kept=4 if fast else 3,
        held=range(4 if fast else 3),
    )
    gk, gv, *terms_kv = call(
        functools.partial(key_kernel, groups, fast),
        [SMEM] + [VMEM] * (3 + n_strips),
        [((own, model), BF16)] * 2 + term_shapes,
        (scalars, mine, q, kn, kf, *map(in_vmem, packs[1:])),
        scratch=[pltpu.VMEM((n_keys, model), BF16)],
        kept=4 if fast else 2,
        held=range(1, 5),
    )
    (grads,) = call(
        final_kernel,
        [VMEM] * 8,
        [(tokens.shape, BF16)],
        (tokens, wq, wk, wv, gq, gk, gv, gout),
        held=range(1, 8),
    )

    n_tokens = tokens.shape[0] * rows * tokens.shape[1] * cols
    norm = math.sqrt(n_tokens)
    if not fast:
        whole = jnp.stack([terms_qo[0][0], terms_kv[0][0], terms_kv[0][1], terms_qo[0][1]])
        sums = lax.psum_scatter(whole.reshape(-1), AXES, scatter_dimension=0, tiled=True)
        return grads, sums / norm

    here, mine = index // 2 % spots, index // per_matrix

    def pick(values, at, axis):
        return lax.dynamic_index_in_dim(values, at, axis, keepdims=False)

    arrived = swap(terms_kv[1], count, 1).astype(F32)
    sums_kv = (terms_kv[0].astype(F32) + arrived).astype(BF16)

    def within_matrix(sums):
        arrived = [swap(pick(sums, here ^ step, 1), count, 2 * step) for step in range(1, spots)]
        total = pick(sums, here, 1).astype(F32)
        for part in arrived:
            total = total + part.astype(F32)
        return total

    total_qo = within_matrix(sums_qo[0])
    total_kv = within_matrix(sums_kv)
    pieces = jnp.concatenate([total_qo[0:1], total_kv, total_qo[1:2]], axis=0)
    arrived = [
        swap(pick(pieces, mine ^ step, 0).astype(BF16), count, per_matrix * step)
        for step in range(1, 4)
    ]
    result = pick(pieces, mine, 0)
    for part in arrived:
        result = result + part.astype(F32)
    return grads, (result / norm).reshape(-1)


def solution(mesh):
    return jax.shard_map(
        layer,
        mesh=mesh,
        in_specs=(
            P("rows", "cols", None),
            P("rows", "cols", None),
            P("rows", "cols"),
            P(("rows", "cols")),
        ),
        out_specs=(P("rows", "cols", None), P(("rows", "cols"))),
        check_vma=False,
    )
```

```python
import functools
import math

import jax
import jax.numpy as jnp
from jax import lax
from jax.experimental import pallas as pl
from jax.experimental.pallas import tpu as pltpu
from jax.sharding import PartitionSpec as P


HEADS = 6
TILE = 8
PER = TILE * TILE
BLK = PER + 8
AXES = ("rows", "cols")

norm_epsilon = 1e-05
head_epsilon = 1e-06

F32 = jnp.float32
BF16 = jnp.bfloat16
VMEM_LIMIT = 12 << 20


def dot(a, b):
    return jnp.dot(a, b, preferred_element_type=F32)


def dot_nt(a, b):
    return lax.dot_general(a, b, (((1,), (1,)), ((), ())), preferred_element_type=F32)


def dot_tn(a, b):
    return lax.dot_general(a, b, (((0,), (0,)), ((), ())), preferred_element_type=F32)


def tiles_of(block):
    parts = [
        block[:, t * TILE : (t + 1) * TILE, :].reshape(PER, block.shape[2])
        for t in range(block.shape[1] // TILE)
    ]
    return jnp.concatenate(parts, axis=0)


def normalise(flat):
    mean = jnp.mean(flat, axis=-1, keepdims=True)
    centred = flat - mean
    inv_std = lax.rsqrt(jnp.mean(centred * centred, axis=-1, keepdims=True) + norm_epsilon)
    return centred * inv_std, inv_std


def pair_ones(width):
    row = lax.broadcasted_iota(jnp.int32, (2 * width, 2 * width), 0) // width
    col = lax.broadcasted_iota(jnp.int32, (2 * width, 2 * width), 1) // width
    return (row == col).astype(F32).astype(BF16)


def head_sums(x, ones):
    step = ones.shape[0]
    high = x.astype(BF16)
    low = (x - high.astype(F32)).astype(BF16)
    parts = [
        dot(high[:, p : p + step], ones) + dot(low[:, p : p + step], ones)
        for p in range(0, x.shape[1], step)
    ]
    return jnp.concatenate(parts, axis=1)


def head_normalise(raw, ones, width):
    squares = (raw * raw).astype(BF16)
    step = ones.shape[0]
    sums = [dot(squares[:, p : p + step], ones) for p in range(0, raw.shape[1], step)]
    factor = lax.rsqrt(jnp.concatenate(sums, axis=1) * (1.0 / width) + head_epsilon)
    return raw * factor, factor


def head_back(normal, factor, upstream, ones, width):
    inner = head_sums(upstream * normal, ones) * (1.0 / width)
    return factor * (upstream - normal * inner)


def split_heads(pair, width):
    lane = lax.broadcasted_iota(jnp.int32, (1, 2 * width), 1)
    first = (lane < width).astype(F32).astype(BF16)
    second = (lane >= width).astype(F32).astype(BF16)
    return jnp.concatenate([pair * first, pair * second], axis=0)


def join_heads(stacked, width):
    half = stacked.shape[0] // 2
    lane = lax.broadcasted_iota(jnp.int32, (1, 2 * width), 1)
    return jnp.where(lane < width, stacked[:half], stacked[half:])


def strip_tiles(strips, odd):
    tiles = []
    for n in range(3):
        tiles += strips[0] if n == 0 else [strips[n].at[0], strips[n].at[1]]
        for side in range(1, len(strips) // 3):
            tiles.append(strips[3 * side + n].at[odd if side == 1 else 1 - odd])
    return tiles


def own_parts(mine):
    own = 2 * PER
    packs = [mine.at[pl.ds(3 * own + t * BLK, BLK)] for t in range(2)]
    return [mine.at[pl.ds(n * own, own)] for n in range(3)] + [packs]


def pack_stats(stats, width):
    blank = jnp.zeros((8, width - 2 * PER), F32)
    return jnp.concatenate([stats[0:8], stats[8:16], blank], axis=1).astype(BF16)


def unpack_stats(tile):
    rows = tile[PER:BLK, 0 : 2 * PER].astype(F32)
    return jnp.concatenate([rows[:, 0:PER], rows[:, PER:]], axis=0)


def near_rows(groups, odd, n_tiles):
    lanes = n_tiles * PER
    group = (lax.broadcasted_iota(jnp.int32, (1, lanes), 1) // PER) % groups
    oddf = odd.astype(F32)
    left = jnp.where(group == 2, oddf, jnp.where(group == 3, 1.0 - oddf, 1.0))
    right = jnp.where(group == 2, 1.0 - oddf, jnp.where(group == 3, oddf, 1.0))
    return left, right


def prep_kernel(tissue, tokens, low_out):
    normed, _ = normalise(tiles_of(tokens[...].astype(F32)))
    low = normed.astype(BF16)
    width = low.shape[1]
    for t in range(2):
        low_out[t, 0:PER, :] = low[t * PER : (t + 1) * PER]
        low_out[t, PER:BLK, :] = jnp.full((BLK - PER, width), tissue[0, t].astype(F32)).astype(BF16)


def pile_kernel(*refs):
    *parts, out = refs
    for n, part in enumerate(parts):
        out[n] = part[0]


def assemble(index, spots, parts, out):
    z_count, per_block, _ = parts[0].shape
    for p, part in enumerate(parts):
        inner = jnp.bitwise_xor(index % (2 * spots), p)
        at = pl.multiple_of(inner * per_block, 16)
        for z in range(z_count):
            matrix = jnp.bitwise_xor(index // (2 * spots), z)
            out[matrix, pl.ds(at, per_block), :] = part[z]


def forward_kernel(groups, spots, *refs):
    scalars, tokens, teacher, *refs = refs
    n_strips = 3 * (groups - 1)
    n_parts = max(1, 2 * spots)
    parts, refs = refs[:n_parts], refs[n_parts:]
    (
        wq_out,
        wk_out,
        wv_out,
        x_out,
        k_out,
        v_out,
        mixed_out,
        gout_out,
        near_out,
        stats_out,
        mine_out,
        pack_out,
        w_scr,
        teacher_scr,
        sem,
    ) = refs[n_strips:]
    copy = pltpu.make_async_copy(teacher, teacher_scr, sem)
    copy.start()
    odd, index = scalars[0], scalars[3]
    own_strip, *others = refs[:n_strips]
    tiles = strip_tiles([[own_strip.at[0], own_strip.at[1]], *others], odd)
    model = tokens.shape[2]
    width = model // HEADS
    own = 2 * PER
    if spots > 0:
        assemble(index, spots, parts, w_scr)
    else:
        w_scr[...] = parts[0][...]
    for n, whole in enumerate((wq_out, wk_out, wv_out)):
        whole[...] = w_scr[n]
    n_tiles = 3 * groups
    flag_rows = []
    ones = pair_ones(width)
    for n, tile in enumerate(tiles):
        x_out[n * PER : (n + 1) * PER, :] = tile[0:PER, :]
        flag_rows.append(tile[PER:BLK, :].astype(F32)[0:1, 0:PER])
    x = x_out[...]
    k_normal, _ = head_normalise(dot(x, wk_out[...]), ones, width)
    keys = k_normal.astype(BF16)
    values = dot(x, wv_out[...]).astype(BF16)
    q_normal, _ = head_normalise(dot(x[0:own], wq_out[...]), ones, width)
    queries = q_normal.astype(BF16)
    k_out[...] = keys
    v_out[...] = values
    *own_outs, packs = own_parts(mine_out)
    for own_out, source in zip(own_outs, (x_out, k_out, v_out), strict=True):
        own_out[...] = source[0:own, :]

    flags = jnp.concatenate(flag_rows, axis=1)
    left, right = near_rows(groups, odd, n_tiles)
    near_out[...] = jnp.concatenate([flags * left, flags * right], axis=0)
    near = jnp.stack([flags * left, flags * right] * 2)
    own_mask = [flag_rows[t][0:1, 0:1] for t in range(2)]
    query_mask = jnp.concatenate(
        [jnp.broadcast_to(own_mask[t], (PER, 1)) for t in range(2)], axis=0
    )
    rest = 1.0 - jnp.concatenate([query_mask, query_mask], axis=0).reshape(4, PER, 1)
    scale = 1.0 / math.sqrt(width)
    mixed_parts, inverses = [], []
    for p in range(HEADS // 2):
        lanes = slice(2 * width * p, 2 * width * (p + 1))
        scores = dot_nt(split_heads(queries[:, lanes] * scale, width), keys[:, lanes])
        raised = jnp.exp(scores).reshape(4, PER, n_tiles * PER) * near
        total = jnp.sum(raised, axis=-1, keepdims=True) + rest
        inverse = (1.0 / total).astype(BF16).astype(F32)
        low = raised.reshape(4 * PER, n_tiles * PER).astype(BF16)
        inverse = inverse.reshape(4 * PER, 1)
        mixed_parts.append(join_heads(dot(low, values[:, lanes]) * inverse, width))
        inverses += [inverse[0:own], inverse[own:]]
    mixed = (jnp.concatenate(mixed_parts, axis=1) * query_mask).astype(BF16)
    mixed_out[...] = mixed
    w_o = w_scr[3]
    copy.wait()
    residual = tiles_of(tokens[...].astype(F32)) + dot(mixed, w_o)
    grad_out = query_mask * (residual - tiles_of(teacher_scr[...].astype(F32)))
    gout_out[...] = grad_out
    grad_mixed = dot_nt(grad_out.astype(BF16), w_o).astype(BF16)
    delta = head_sums(grad_mixed.astype(F32) * mixed.astype(F32), ones)
    lane = lax.broadcasted_iota(jnp.int32, (1, own), 1)
    table = jnp.zeros((own, own), F32)
    for h in range(HEADS):
        table = jnp.where(lane == h, inverses[h], table)
        table = jnp.where(lane == HEADS + h, delta[:, h * width : h * width + 1], table)
    table = jnp.where(lane == 2 * HEADS, query_mask, table)
    stats_out[...] = table
    stats = table.T[0:16, :]
    for t in range(2):
        here = slice(t * PER, (t + 1) * PER)
        pack_out[t, 0:PER, :] = grad_mixed[here]
        pack_out[t, PER:BLK, :] = pack_stats(stats[:, here], model)
        packs[t][...] = pack_out[t]


def store_terms(fast, odd, grads, outs):
    if not fast:
        for m, grad in enumerate(grads):
            outs[0][m] = grad
        return
    keep, send = outs
    rows = keep.shape[2]
    for m, grad in enumerate(grads):
        for b in range(keep.shape[1]):
            even_part = grad[2 * b * rows : (2 * b + 1) * rows]
            odd_part = grad[(2 * b + 1) * rows : (2 * b + 2) * rows]
            is_odd = odd == 1
            keep[m, b] = jnp.where(is_odd, odd_part, even_part).astype(BF16)
            send[m, b] = jnp.where(is_odd, even_part, odd_part).astype(BF16)


def halo_query_kernel(wq, x, wk, *refs):
    q_out, kn_out, kf_out, *sums = refs[-4:] if len(refs) > 3 else refs
    model = x.shape[1]
    width = model // HEADS
    ones = pair_ones(width)
    q_normal, _ = head_normalise(dot(x[...], wq[...]), ones, width)
    q_out[...] = q_normal.astype(BF16)
    kn_out[...], kf_out[...] = head_normalise(dot(x[0 : 2 * PER, :], wk[...]), ones, width)
    for sums_out in sums:
        sums_out[...] = (refs[0][...].astype(F32) + refs[1][...].astype(F32)).astype(BF16)


def query_kernel(fast, scalars, wq, k, v, mixed, gout, near_in, stats_in, mine, *outs):
    core = scalars[2]
    model = wq.shape[0]
    width = model // HEADS
    n_tiles = near_in.shape[1] // PER
    ones = pair_ones(width)
    x_own, _, _, packs = own_parts(mine)
    q_normal, q_factor = head_normalise(dot(x_own[...], wq[...]), ones, width)
    queries = q_normal.astype(BF16)
    near = jnp.stack([near_in[0:1], near_in[1:2]] * 2)
    stats = stats_in[...].astype(BF16).astype(F32)
    gq_out, *outs = outs
    grad_mixed = jnp.concatenate([pack[0:PER, :] for pack in packs], axis=0)
    scale = 1.0 / math.sqrt(width)
    parts = []
    for p in range(HEADS // 2):
        lanes = slice(2 * width * p, 2 * width * (p + 1))
        keys, values = k[:, lanes], v[:, lanes]
        scores = dot_nt(split_heads(queries[:, lanes] * scale, width), keys)
        inverse = jnp.concatenate([stats[:, 2 * p : 2 * p + 1], stats[:, 2 * p + 1 : 2 * p + 2]], axis=0)
        at = HEADS + 2 * p
        delta = jnp.concatenate([stats[:, at : at + 1], stats[:, at + 1 : at + 2]], axis=0)
        full = jnp.exp(scores).reshape(4, PER, n_tiles * PER) * near
        full = full.reshape(4 * PER, n_tiles * PER)
        grad_attn = dot_nt(split_heads(grad_mixed[:, lanes], width), values)
        grad_scores = (full * (grad_attn - delta)).astype(BF16)
        parts.append(join_heads(dot(grad_scores, keys) * (inverse * scale), width))
    grad_qn = jnp.concatenate(parts, axis=1)
    grad_query = head_back(q_normal, q_factor, grad_qn, ones, width).astype(BF16)
    gq_out[...] = grad_query
    grad_wq = dot_tn(x_own[...], grad_query)
    grad_wo = dot_tn(mixed[...], gout[...].astype(BF16))
    store_terms(fast, core, [grad_wq, grad_wo], outs)


def key_kernel(groups, fast, scalars, mine, q, kn, kf, *refs):
    n_strips = 3 * (groups - 1)
    sources, refs = refs[: n_strips - 1], refs[n_strips - 1 :]
    *refs, g_scr = refs
    gk_out, gv_out, *outs = refs
    odd, core = scalars[0], scalars[2]
    model = q.shape[1]
    width = model // HEADS
    n_tiles = 3 * groups
    ones = pair_ones(width)
    x, k, v, packs = own_parts(mine)
    tiles = strip_tiles([packs, *sources], odd)
    x_own = x[...]
    stat_parts = []
    for n, tile in enumerate(tiles):
        g_scr[n * PER : (n + 1) * PER, :] = tile[0:PER, :]
        stat_parts.append(unpack_stats(tile))
    stats = jnp.concatenate(stat_parts, axis=1)
    left, right = near_rows(groups, odd, n_tiles)
    flag = stats[2 * HEADS : 2 * HEADS + 1]
    near = [left * flag[:, 0:1], right * flag[:, PER : PER + 1]]
    scale = 1.0 / math.sqrt(width)
    key_parts, value_parts = [], []
    for p in range(HEADS // 2):
        lanes = slice(2 * width * p, 2 * width * (p + 1))
        queries, grads = q[:, lanes], g_scr[:, lanes]
        scores = dot_nt(split_heads(k[:, lanes] * scale, width), queries)
        inv = [stats[2 * p + j : 2 * p + j + 1] for j in range(2)]
        rows = jnp.stack([inv[j] * near[t] for j in range(2) for t in range(2)])
        at = HEADS + 2 * p
        delta = jnp.stack([stats[at + j : at + j + 1] for j in range(2) for _ in range(2)])
        full = jnp.exp(scores).reshape(4, PER, n_tiles * PER) * rows
        grad_attn = dot_nt(split_heads(v[:, lanes], width), grads)
        grad_attn = grad_attn.reshape(4, PER, n_tiles * PER) - delta
        grad_scores = (full * grad_attn).reshape(4 * PER, n_tiles * PER).astype(BF16)
        low = full.reshape(4 * PER, n_tiles * PER).astype(BF16)
        key_parts.append(join_heads(dot(grad_scores, queries), width) * scale)
        value_parts.append(join_heads(dot(low, grads), width))
    grad_kn = jnp.concatenate(key_parts, axis=1)
    grad_key = head_back(kn[...], kf[...], grad_kn, ones, width).astype(BF16)
    grad_value = jnp.concatenate(value_parts, axis=1).astype(BF16)
    gk_out[...] = grad_key
    gv_out[...] = grad_value
    store_terms(fast, core, [dot_tn(x_own, grad_key), dot_tn(x_own, grad_value)], outs)


def final_kernel(tokens, wq, wk, wv, gq, gk, gv, gout, out):
    model = gk.shape[1]
    grad_lowered = (
        dot_nt(gq[...], wq[...]) + dot_nt(gk[...], wk[...]) + dot_nt(gv[...], wv[...])
    )
    normed, inv_std = normalise(tiles_of(tokens[...].astype(F32)))
    grads = gout[...] + inv_std * (
        grad_lowered
        - jnp.mean(grad_lowered, axis=-1, keepdims=True)
        - normed * jnp.mean(grad_lowered * normed, axis=-1, keepdims=True)
    )
    pieces = [grads[t * PER : (t + 1) * PER].reshape(TILE, TILE, model) for t in range(2)]
    out[...] = jnp.concatenate(pieces, axis=1).astype(BF16)


ANY = pl.BlockSpec(memory_space=pl.ANY)
SMEM = pl.BlockSpec(memory_space=pltpu.SMEM)
VMEM = pl.BlockSpec(memory_space=pltpu.VMEM)


def in_hbm(value):
    return pltpu.with_memory_space_constraint(value, pltpu.HBM)


def in_vmem(value):
    return pltpu.with_memory_space_constraint(value, pltpu.VMEM)


def call(kernel, in_specs, shapes, args, scratch=(), kept=0, held=()):
    args = [
        pltpu.with_memory_space_constraint(a, pltpu.VMEM) if n in held else a
        for n, a in enumerate(args)
    ]
    return pl.pallas_call(
        kernel,
        out_shape=[
            pltpu.VMEM(s, t) if n < kept else jax.ShapeDtypeStruct(s, t)
            for n, (s, t) in enumerate(shapes)
        ],
        in_specs=in_specs,
        out_specs=[VMEM] * len(shapes),
        scratch_shapes=list(scratch),
        compiler_params=pltpu.CompilerParams(vmem_limit_bytes=VMEM_LIMIT),
    )(*args)


def swap(value, count, mask):
    return lax.ppermute(value, AXES, [(i, i ^ mask) for i in range(count)])


def side_pairs(length, side):
    pairs = []
    for i in range(side, length - 1, 2):
        pairs += [(i, i + 1), (i + 1, i)]
    return pairs


def beside(strip):
    rows = lax.axis_size("rows")
    near = lax.ppermute(strip, "rows", side_pairs(rows, 0))
    return [strip, near, lax.ppermute(strip, "rows", side_pairs(rows, 1))]


def across(strips):
    cols = lax.axis_size("cols")
    sides = []
    for n in range(1 if cols == 2 else 2):
        for strip in strips:
            sides.append(lax.ppermute(strip, "cols", side_pairs(cols, n)))
    return sides


def layer(tokens, teacher, tissue, weights):
    model = tokens.shape[2]
    rows, cols = lax.axis_size("rows"), lax.axis_size("cols")
    count = rows * cols
    groups = 3 if cols == 2 else 4
    per_block = 4 * model // count
    fast = count & (count - 1) == 0 and count >= 16 and per_block % 16 == 0
    per_matrix = count // 4
    spots = per_matrix // 2
    index = lax.axis_index("rows") * cols + lax.axis_index("cols")
    odd = lax.axis_index("cols") % 2
    own = 2 * PER
    n_keys = 3 * groups * PER
    n_strips = 3 * (groups - 1)

    scalars = jnp.stack([odd, index % 2, index % 2, index]).astype(jnp.int32)

    (low,) = call(
        prep_kernel,
        [SMEM, VMEM],
        [((2, BLK, model), BF16)],
        (
            in_hbm(tissue),
            in_hbm(tokens),
        ),
    )
    if fast:
        block = weights.reshape(1, per_block, model)
        parts = [block] + [swap(block, count, per_matrix * step) for step in range(1, 4)]
        (pile,) = call(
            pile_kernel,
            [VMEM] * 4,
            [((4, per_block, model), BF16)],
            parts,
            kept=1,
            held=range(1, 4),
        )
        piles = [pile] + [swap(pile, count, 2 * step) for step in range(1, spots)]
        strips = beside(low)
        wide = []
        for pile in piles:
            wide.append(swap(pile, count, 1))
        parts = [in_vmem(part) for pair in zip(piles, wide, strict=True) for part in pair]
        strips = strips + across(strips)
    else:
        strips = beside(low)
        strips = strips + across(strips)
        whole = lax.all_gather(weights, AXES, axis=0, tiled=True)
        parts = [whole.reshape(4, model, model)]

    wq, wk, wv, x, k, v, mixed, gout, near, stats, mine, pack = call(
        functools.partial(forward_kernel, groups, spots if fast else 0),
        [SMEM, VMEM, ANY] + [VMEM] * (len(parts) + n_strips),
        [((model, model), BF16)] * 3
        + [((n_keys, model), BF16)] * 3
        + [
            ((own, model), BF16),
            ((own, model), F32),
            ((2, n_keys), F32),
            ((own, own), F32),
            ((3 * own + 2 * BLK, model), BF16),
            ((2, BLK, model), BF16),
        ],
        (scalars, tokens, in_hbm(teacher), *parts, *map(in_vmem, strips)),
        scratch=[
            pltpu.VMEM((4, model, model), BF16),
            pltpu.VMEM(teacher.shape, BF16),
            pltpu.SemaphoreType.DMA,
        ],
        kept=11,
    )
    packs = beside(pack)
    packs = packs + across(packs)

    if fast:
        term_shapes = [((2, spots, per_block, model), BF16)] * 2
    else:
        term_shapes = [((2, model, model), F32)]
    gq, *terms_qo = call(
        functools.partial(query_kernel, fast),
        [SMEM] + [VMEM] * 8,
        [((own, model), BF16)] + term_shapes,
        (scalars, wq, k, v, mixed, gout, near, stats, mine),
        kept=2,
        held=range(1, 9),
    )
    more = []
    if fast:
        more = [terms_qo[0], swap(terms_qo[1], count, 1)]
    q, kn, kf, *sums_qo = call(
        halo_query_kernel,
        [VMEM] * (3 + len(more)),
        [((n_keys, model), BF16)] + [((own, model), F32)] * 2 + term_shapes[: len(more) // 2],
        (wq, x, wk, *more),
        kept=4 if fast else 3,
        held=range(4 if fast else 3),
    )
    gk, gv, *terms_kv = call(
        functools.partial(key_kernel, groups, fast),
        [SMEM] + [VMEM] * (3 + n_strips),
        [((own, model), BF16)] * 2 + term_shapes,
        (scalars, mine, q, kn, kf, *map(in_vmem, packs[1:])),
        scratch=[pltpu.VMEM((n_keys, model), BF16)],
        kept=4 if fast else 2,
        held=range(1, 5),
    )
    (grads,) = call(
        final_kernel,
        [VMEM] * 8,
        [(tokens.shape, BF16)],
        (tokens, wq, wk, wv, gq, gk, gv, gout),
        held=range(1, 8),
    )

    n_tokens = tokens.shape[0] * rows * tokens.shape[1] * cols
    norm = math.sqrt(n_tokens)
    if not fast:
        whole = jnp.stack([terms_qo[0][0], terms_kv[0][0], terms_kv[0][1], terms_qo[0][1]])
        sums = lax.psum_scatter(whole.reshape(-1), AXES, scatter_dimension=0, tiled=True)
        return grads, sums / norm

    here, mine = index // 2 % spots, index // per_matrix

    def pick(values, at, axis):
        return lax.dynamic_index_in_dim(values, at, axis, keepdims=False)

    arrived = swap(terms_kv[1], count, 1).astype(F32)
    sums_kv = (terms_kv[0].astype(F32) + arrived).astype(BF16)

    def within_matrix(sums):
        arrived = [swap(pick(sums, here ^ step, 1), count, 2 * step) for step in range(1, spots)]
        total = pick(sums, here, 1).astype(F32)
        for part in arrived:
            total = total + part.astype(F32)
        return total

    total_qo = within_matrix(sums_qo[0])
    total_kv = within_matrix(sums_kv)
    pieces = jnp.concatenate([total_qo[0:1], total_kv, total_qo[1:2]], axis=0)
    arrived = [
        swap(pick(pieces, mine ^ step, 0).astype(BF16), count, per_matrix * step)
        for step in range(1, 4)
    ]
    result = pick(pieces, mine, 0)
    for part in arrived:
        result = result + part.astype(F32)
    return grads, (result / norm).reshape(-1)


def solution(mesh):
    return jax.shard_map(
        layer,
        mesh=mesh,
        in_specs=(
            P("rows", "cols", None),
            P("rows", "cols", None),
            P("rows", "cols"),
            P(("rows", "cols")),
        ),
        out_specs=(P("rows", "cols", None), P(("rows", "cols"))),
        check_vma=False,
    )
```

```python
import functools
import math

import jax
import jax.numpy as jnp
from jax import lax
from jax.experimental import pallas as pl
from jax.experimental.pallas import tpu as pltpu
from jax.sharding import PartitionSpec as P


HEADS = 6
TILE = 8
PER = TILE * TILE
BLK = PER + 8
AXES = ("rows", "cols")

norm_epsilon = 1e-05
head_epsilon = 1e-06

F32 = jnp.float32
BF16 = jnp.bfloat16
VMEM_LIMIT = 12 << 20


def dot(a, b):
    return jnp.dot(a, b, preferred_element_type=F32)


def dot_nt(a, b):
    return lax.dot_general(a, b, (((1,), (1,)), ((), ())), preferred_element_type=F32)


def dot_tn(a, b):
    return lax.dot_general(a, b, (((0,), (0,)), ((), ())), preferred_element_type=F32)


def tiles_of(block):
    parts = [
        block[:, t * TILE : (t + 1) * TILE, :].reshape(PER, block.shape[2])
        for t in range(block.shape[1] // TILE)
    ]
    return jnp.concatenate(parts, axis=0)


def normalise(flat):
    mean = jnp.mean(flat, axis=-1, keepdims=True)
    centred = flat - mean
    inv_std = lax.rsqrt(jnp.mean(centred * centred, axis=-1, keepdims=True) + norm_epsilon)
    return centred * inv_std, inv_std


def pair_ones(width):
    row = lax.broadcasted_iota(jnp.int32, (2 * width, 2 * width), 0) // width
    col = lax.broadcasted_iota(jnp.int32, (2 * width, 2 * width), 1) // width
    return (row == col).astype(F32).astype(BF16)


def head_sums(x, ones):
    step = ones.shape[0]
    high = x.astype(BF16)
    low = (x - high.astype(F32)).astype(BF16)
    parts = [
        dot(high[:, p : p + step], ones) + dot(low[:, p : p + step], ones)
        for p in range(0, x.shape[1], step)
    ]
    return jnp.concatenate(parts, axis=1)


def head_normalise(raw, ones, width):
    squares = (raw * raw).astype(BF16)
    step = ones.shape[0]
    sums = [dot(squares[:, p : p + step], ones) for p in range(0, raw.shape[1], step)]
    factor = lax.rsqrt(jnp.concatenate(sums, axis=1) * (1.0 / width) + head_epsilon)
    return raw * factor, factor


def head_back(normal, factor, upstream, ones, width):
    inner = head_sums(upstream * normal, ones) * (1.0 / width)
    return factor * (upstream - normal * inner)


def split_heads(pair, width):
    lane = lax.broadcasted_iota(jnp.int32, (1, 2 * width), 1)
    first = (lane < width).astype(F32).astype(BF16)
    second = (lane >= width).astype(F32).astype(BF16)
    return jnp.concatenate([pair * first, pair * second], axis=0)


def join_heads(stacked, width):
    half = stacked.shape[0] // 2
    lane = lax.broadcasted_iota(jnp.int32, (1, 2 * width), 1)
    return jnp.where(lane < width, stacked[:half], stacked[half:])


def strip_tiles(strips, odd):
    tiles = []
    for n in range(3):
        tiles += strips[0] if n == 0 else [strips[n].at[0], strips[n].at[1]]
        for side in range(1, len(strips) // 3):
            tiles.append(strips[3 * side + n].at[odd if side == 1 else 1 - odd])
    return tiles


def own_parts(mine):
    own = 2 * PER
    packs = [mine.at[pl.ds(3 * own + t * BLK, BLK)] for t in range(2)]
    return [mine.at[pl.ds(n * own, own)] for n in range(3)] + [packs]


def pack_stats(stats, width):
    blank = jnp.zeros((8, width - 2 * PER), F32)
    return jnp.concatenate([stats[0:8], stats[8:16], blank], axis=1).astype(BF16)


def unpack_stats(tile):
    rows = tile[PER:BLK, 0 : 2 * PER].astype(F32)
    return jnp.concatenate([rows[:, 0:PER], rows[:, PER:]], axis=0)


def near_rows(groups, odd, n_tiles):
    lanes = n_tiles * PER
    group = (lax.broadcasted_iota(jnp.int32, (1, lanes), 1) // PER) % groups
    oddf = odd.astype(F32)
    left = jnp.where(group == 2, oddf, jnp.where(group == 3, 1.0 - oddf, 1.0))
    right = jnp.where(group == 2, 1.0 - oddf, jnp.where(group == 3, oddf, 1.0))
    return left, right


def prep_kernel(tissue, tokens, low_out):
    normed, _ = normalise(tiles_of(tokens[...].astype(F32)))
    low = normed.astype(BF16)
    width = low.shape[1]
    for t in range(2):
        low_out[t, 0:PER, :] = low[t * PER : (t + 1) * PER]
        low_out[t, PER:BLK, :] = jnp.full((BLK - PER, width), tissue[0, t].astype(F32)).astype(BF16)


def pile_kernel(*refs):
    *parts, out = refs
    for n, part in enumerate(parts):
        out[n] = part[0]


def assemble(index, spots, parts, out):
    z_count, per_block, _ = parts[0].shape
    for p, part in enumerate(parts):
        inner = jnp.bitwise_xor(index % (2 * spots), p)
        at = pl.multiple_of(inner * per_block, 16)
        for z in range(z_count):
            matrix = jnp.bitwise_xor(index // (2 * spots), z)
            out[matrix, pl.ds(at, per_block), :] = part[z]


def forward_kernel(groups, spots, *refs):
    scalars, tokens, teacher, *refs = refs
    n_strips = 3 * (groups - 1)
    n_parts = max(1, 2 * spots)
    parts, refs = refs[:n_parts], refs[n_parts:]
    (
        wq_out,
        wk_out,
        wv_out,
        x_out,
        k_out,
        v_out,
        mixed_out,
        gout_out,
        near_out,
        stats_out,
        mine_out,
        pack_out,
        w_scr,
        teacher_scr,
        sem,
    ) = refs[n_strips:]
    copy = pltpu.make_async_copy(teacher, teacher_scr, sem)
    copy.start()
    odd, index = scalars[0], scalars[3]
    own_strip, *others = refs[:n_strips]
    tiles = strip_tiles([[own_strip.at[0], own_strip.at[1]], *others], odd)
    model = tokens.shape[2]
    width = model // HEADS
    own = 2 * PER
    if spots > 0:
        assemble(index, spots, parts, w_scr)
    else:
        w_scr[...] = parts[0][...]
    for n, whole in enumerate((wq_out, wk_out, wv_out)):
        whole[...] = w_scr[n]
    n_tiles = 3 * groups
    flag_rows = []
    ones = pair_ones(width)
    for n, tile in enumerate(tiles):
        x_out[n * PER : (n + 1) * PER, :] = tile[0:PER, :]
        flag_rows.append(tile[PER:BLK, :].astype(F32)[0:1, 0:PER])
    x = x_out[...]
    k_normal, _ = head_normalise(dot(x, w_scr[1]), ones, width)
    keys = k_normal.astype(BF16)
    values = dot(x, w_scr[2]).astype(BF16)
    q_normal, _ = head_normalise(dot(x[0:own], w_scr[0]), ones, width)
    queries = q_normal.astype(BF16)
    k_out[...] = keys
    v_out[...] = values
    *own_outs, packs = own_parts(mine_out)
    for own_out, source in zip(own_outs, (x_out, k_out, v_out), strict=True):
        own_out[...] = source[0:own, :]

    flags = jnp.concatenate(flag_rows, axis=1)
    left, right = near_rows(groups, odd, n_tiles)
    near_out[...] = jnp.concatenate([flags * left, flags * right], axis=0)
    near = jnp.stack([flags * left, flags * right] * 2)
    own_mask = [flag_rows[t][0:1, 0:1] for t in range(2)]
    query_mask = jnp.concatenate(
        [jnp.broadcast_to(own_mask[t], (PER, 1)) for t in range(2)], axis=0
    )
    rest = 1.0 - jnp.concatenate([query_mask, query_mask], axis=0).reshape(4, PER, 1)
    scale = 1.0 / math.sqrt(width)
    mixed_parts, inverses = [], []
    for p in range(HEADS // 2):
        lanes = slice(2 * width * p, 2 * width * (p + 1))
        scores = dot_nt(split_heads(queries[:, lanes] * scale, width), keys[:, lanes])
        raised = jnp.exp(scores).reshape(4, PER, n_tiles * PER) * near
        total = jnp.sum(raised, axis=-1, keepdims=True) + rest
        inverse = (1.0 / total).astype(BF16).astype(F32)
        low = raised.reshape(4 * PER, n_tiles * PER).astype(BF16)
        inverse = inverse.reshape(4 * PER, 1)
        mixed_parts.append(join_heads(dot(low, values[:, lanes]) * inverse, width))
        inverses += [inverse[0:own], inverse[own:]]
    mixed = (jnp.concatenate(mixed_parts, axis=1) * query_mask).astype(BF16)
    mixed_out[...] = mixed
    w_o = w_scr[3]
    copy.wait()
    residual = tiles_of(tokens[...].astype(F32)) + dot(mixed, w_o)
    grad_out = query_mask * (residual - tiles_of(teacher_scr[...].astype(F32)))
    gout_out[...] = grad_out
    grad_mixed = dot_nt(grad_out.astype(BF16), w_o).astype(BF16)
    delta = head_sums(grad_mixed.astype(F32) * mixed.astype(F32), ones)
    lane = lax.broadcasted_iota(jnp.int32, (1, own), 1)
    table = jnp.zeros((own, own), F32)
    for h in range(HEADS):
        table = jnp.where(lane == h, inverses[h], table)
        table = jnp.where(lane == HEADS + h, delta[:, h * width : h * width + 1], table)
    table = jnp.where(lane == 2 * HEADS, query_mask, table)
    stats_out[...] = table
    stats = table.T[0:16, :]
    for t in range(2):
        here = slice(t * PER, (t + 1) * PER)
        pack_out[t, 0:PER, :] = grad_mixed[here]
        pack_out[t, PER:BLK, :] = pack_stats(stats[:, here], model)
        packs[t][...] = pack_out[t]


def store_terms(fast, odd, grads, outs):
    if not fast:
        for m, grad in enumerate(grads):
            outs[0][m] = grad
        return
    keep, send = outs
    rows = keep.shape[2]
    for m, grad in enumerate(grads):
        for b in range(keep.shape[1]):
            even_part = grad[2 * b * rows : (2 * b + 1) * rows]
            odd_part = grad[(2 * b + 1) * rows : (2 * b + 2) * rows]
            is_odd = odd == 1
            keep[m, b] = jnp.where(is_odd, odd_part, even_part).astype(BF16)
            send[m, b] = jnp.where(is_odd, even_part, odd_part).astype(BF16)


def halo_query_kernel(wq, x, wk, *refs):
    q_out, kn_out, kf_out, *sums = refs[-4:] if len(refs) > 3 else refs
    model = x.shape[1]
    width = model // HEADS
    ones = pair_ones(width)
    q_normal, _ = head_normalise(dot(x[...], wq[...]), ones, width)
    q_out[...] = q_normal.astype(BF16)
    kn_out[...], kf_out[...] = head_normalise(dot(x[0 : 2 * PER, :], wk[...]), ones, width)
    for sums_out in sums:
        sums_out[...] = (refs[0][...].astype(F32) + refs[1][...].astype(F32)).astype(BF16)


def query_kernel(fast, scalars, wq, k, v, mixed, gout, near_in, stats_in, mine, *outs):
    core = scalars[2]
    model = wq.shape[0]
    width = model // HEADS
    n_tiles = near_in.shape[1] // PER
    ones = pair_ones(width)
    x_own, _, _, packs = own_parts(mine)
    q_normal, q_factor = head_normalise(dot(x_own[...], wq[...]), ones, width)
    queries = q_normal.astype(BF16)
    near = jnp.stack([near_in[0:1], near_in[1:2]] * 2)
    stats = stats_in[...].astype(BF16).astype(F32)
    gq_out, *outs = outs
    grad_mixed = jnp.concatenate([pack[0:PER, :] for pack in packs], axis=0)
    scale = 1.0 / math.sqrt(width)
    parts = []
    for p in range(HEADS // 2):
        lanes = slice(2 * width * p, 2 * width * (p + 1))
        keys, values = k[:, lanes], v[:, lanes]
        scores = dot_nt(split_heads(queries[:, lanes] * scale, width), keys)
        inverse = jnp.concatenate([stats[:, 2 * p : 2 * p + 1], stats[:, 2 * p + 1 : 2 * p + 2]], axis=0)
        at = HEADS + 2 * p
        delta = jnp.concatenate([stats[:, at : at + 1], stats[:, at + 1 : at + 2]], axis=0)
        full = jnp.exp(scores).reshape(4, PER, n_tiles * PER) * near
        full = full.reshape(4 * PER, n_tiles * PER)
        grad_attn = dot_nt(split_heads(grad_mixed[:, lanes], width), values)
        grad_scores = (full * (grad_attn - delta)).astype(BF16)
        parts.append(join_heads(dot(grad_scores, keys) * (inverse * scale), width))
    grad_qn = jnp.concatenate(parts, axis=1)
    grad_query = head_back(q_normal, q_factor, grad_qn, ones, width).astype(BF16)
    gq_out[...] = grad_query
    grad_wq = dot_tn(x_own[...], grad_query)
    grad_wo = dot_tn(mixed[...], gout[...].astype(BF16))
    store_terms(fast, core, [grad_wq, grad_wo], outs)


def key_kernel(groups, fast, scalars, mine, q, kn, kf, *refs):
    n_strips = 3 * (groups - 1)
    sources, refs = refs[: n_strips - 1], refs[n_strips - 1 :]
    *refs, g_scr = refs
    gk_out, gv_out, *outs = refs
    odd, core = scalars[0], scalars[2]
    model = q.shape[1]
    width = model // HEADS
    n_tiles = 3 * groups
    ones = pair_ones(width)
    x, k, v, packs = own_parts(mine)
    tiles = strip_tiles([packs, *sources], odd)
    x_own = x[...]
    stat_parts = []
    for n, tile in enumerate(tiles):
        g_scr[n * PER : (n + 1) * PER, :] = tile[0:PER, :]
        stat_parts.append(unpack_stats(tile))
    stats = jnp.concatenate(stat_parts, axis=1)
    left, right = near_rows(groups, odd, n_tiles)
    flag = stats[2 * HEADS : 2 * HEADS + 1]
    near = [left * flag[:, 0:1], right * flag[:, PER : PER + 1]]
    scale = 1.0 / math.sqrt(width)
    key_parts, value_parts = [], []
    for p in range(HEADS // 2):
        lanes = slice(2 * width * p, 2 * width * (p + 1))
        queries, grads = q[:, lanes], g_scr[:, lanes]
        scores = dot_nt(split_heads(k[:, lanes] * scale, width), queries)
        inv = [stats[2 * p + j : 2 * p + j + 1] for j in range(2)]
        rows = jnp.stack([inv[j] * near[t] for j in range(2) for t in range(2)])
        at = HEADS + 2 * p
        delta = jnp.stack([stats[at + j : at + j + 1] for j in range(2) for _ in range(2)])
        full = jnp.exp(scores).reshape(4, PER, n_tiles * PER) * rows
        grad_attn = dot_nt(split_heads(v[:, lanes], width), grads)
        grad_attn = grad_attn.reshape(4, PER, n_tiles * PER) - delta
        grad_scores = (full * grad_attn).reshape(4 * PER, n_tiles * PER).astype(BF16)
        low = full.reshape(4 * PER, n_tiles * PER).astype(BF16)
        key_parts.append(join_heads(dot(grad_scores, queries), width) * scale)
        value_parts.append(join_heads(dot(low, grads), width))
    grad_kn = jnp.concatenate(key_parts, axis=1)
    grad_key = head_back(kn[...], kf[...], grad_kn, ones, width).astype(BF16)
    grad_value = jnp.concatenate(value_parts, axis=1).astype(BF16)
    gk_out[...] = grad_key
    gv_out[...] = grad_value
    store_terms(fast, core, [dot_tn(x_own, grad_key), dot_tn(x_own, grad_value)], outs)


def final_kernel(tokens, wq, wk, wv, gq, gk, gv, gout, out):
    model = gk.shape[1]
    grad_lowered = (
        dot_nt(gq[...], wq[...]) + dot_nt(gk[...], wk[...]) + dot_nt(gv[...], wv[...])
    )
    normed, inv_std = normalise(tiles_of(tokens[...].astype(F32)))
    grads = gout[...] + inv_std * (
        grad_lowered
        - jnp.mean(grad_lowered, axis=-1, keepdims=True)
        - normed * jnp.mean(grad_lowered * normed, axis=-1, keepdims=True)
    )
    pieces = [grads[t * PER : (t + 1) * PER].reshape(TILE, TILE, model) for t in range(2)]
    out[...] = jnp.concatenate(pieces, axis=1).astype(BF16)


ANY = pl.BlockSpec(memory_space=pl.ANY)
SMEM = pl.BlockSpec(memory_space=pltpu.SMEM)
VMEM = pl.BlockSpec(memory_space=pltpu.VMEM)


def in_hbm(value):
    return pltpu.with_memory_space_constraint(value, pltpu.HBM)


def in_vmem(value):
    return pltpu.with_memory_space_constraint(value, pltpu.VMEM)


def call(kernel, in_specs, shapes, args, scratch=(), kept=0, held=()):
    args = [
        pltpu.with_memory_space_constraint(a, pltpu.VMEM) if n in held else a
        for n, a in enumerate(args)
    ]
    return pl.pallas_call(
        kernel,
        out_shape=[
            pltpu.VMEM(s, t) if n < kept else jax.ShapeDtypeStruct(s, t)
            for n, (s, t) in enumerate(shapes)
        ],
        in_specs=in_specs,
        out_specs=[VMEM] * len(shapes),
        scratch_shapes=list(scratch),
        compiler_params=pltpu.CompilerParams(vmem_limit_bytes=VMEM_LIMIT),
    )(*args)


def swap(value, count, mask):
    return lax.ppermute(value, AXES, [(i, i ^ mask) for i in range(count)])


def side_pairs(length, side):
    pairs = []
    for i in range(side, length - 1, 2):
        pairs += [(i, i + 1), (i + 1, i)]
    return pairs


def beside(strip):
    rows = lax.axis_size("rows")
    near = lax.ppermute(strip, "rows", side_pairs(rows, 0))
    return [strip, near, lax.ppermute(strip, "rows", side_pairs(rows, 1))]


def across(strips):
    cols = lax.axis_size("cols")
    sides = []
    for n in range(1 if cols == 2 else 2):
        for strip in strips:
            sides.append(lax.ppermute(strip, "cols", side_pairs(cols, n)))
    return sides


def layer(tokens, teacher, tissue, weights):
    model = tokens.shape[2]
    rows, cols = lax.axis_size("rows"), lax.axis_size("cols")
    count = rows * cols
    groups = 3 if cols == 2 else 4
    per_block = 4 * model // count
    fast = count & (count - 1) == 0 and count >= 16 and per_block % 16 == 0
    per_matrix = count // 4
    spots = per_matrix // 2
    index = lax.axis_index("rows") * cols + lax.axis_index("cols")
    odd = lax.axis_index("cols") % 2
    own = 2 * PER
    n_keys = 3 * groups * PER
    n_strips = 3 * (groups - 1)

    scalars = jnp.stack([odd, index % 2, index % 2, index]).astype(jnp.int32)

    (low,) = call(
        prep_kernel,
        [SMEM, VMEM],
        [((2, BLK, model), BF16)],
        (
            in_hbm(tissue),
            in_hbm(tokens),
        ),
    )
    if fast:
        block = weights.reshape(1, per_block, model)
        parts = [block] + [swap(block, count, per_matrix * step) for step in range(1, 4)]
        (pile,) = call(
            pile_kernel,
            [VMEM] * 4,
            [((4, per_block, model), BF16)],
            parts,
            kept=1,
            held=range(1, 4),
        )
        piles = [pile] + [swap(pile, count, 2 * step) for step in range(1, spots)]
        strips = beside(low)
        wide = []
        for pile in piles:
            wide.append(swap(pile, count, 1))
        parts = [in_vmem(part) for pair in zip(piles, wide, strict=True) for part in pair]
        strips = strips + across(strips)
    else:
        strips = beside(low)
        strips = strips + across(strips)
        whole = lax.all_gather(weights, AXES, axis=0, tiled=True)
        parts = [whole.reshape(4, model, model)]

    wq, wk, wv, x, k, v, mixed, gout, near, stats, mine, pack = call(
        functools.partial(forward_kernel, groups, spots if fast else 0),
        [SMEM, VMEM, ANY] + [VMEM] * (len(parts) + n_strips),
        [((model, model), BF16)] * 3
        + [((n_keys, model), BF16)] * 3
        + [
            ((own, model), BF16),
            ((own, model), F32),
            ((2, n_keys), F32),
            ((own, own), F32),
            ((3 * own + 2 * BLK, model), BF16),
            ((2, BLK, model), BF16),
        ],
        (scalars, tokens, in_hbm(teacher), *parts, *map(in_vmem, strips)),
        scratch=[
            pltpu.VMEM((4, model, model), BF16),
            pltpu.VMEM(teacher.shape, BF16),
            pltpu.SemaphoreType.DMA,
        ],
        kept=11,
    )
    packs = beside(pack)
    packs = packs + across(packs)

    if fast:
        term_shapes = [((2, spots, per_block, model), BF16)] * 2
    else:
        term_shapes = [((2, model, model), F32)]
    gq, *terms_qo = call(
        functools.partial(query_kernel, fast),
        [SMEM] + [VMEM] * 8,
        [((own, model), BF16)] + term_shapes,
        (scalars, wq, k, v, mixed, gout, near, stats, mine),
        kept=2,
        held=range(1, 9),
    )
    more = []
    if fast:
        more = [terms_qo[0], swap(terms_qo[1], count, 1)]
    q, kn, kf, *sums_qo = call(
        halo_query_kernel,
        [VMEM] * (3 + len(more)),
        [((n_keys, model), BF16)] + [((own, model), F32)] * 2 + term_shapes[: len(more) // 2],
        (wq, x, wk, *more),
        kept=4 if fast else 3,
        held=range(4 if fast else 3),
    )
    gk, gv, *terms_kv = call(
        functools.partial(key_kernel, groups, fast),
        [SMEM] + [VMEM] * (3 + n_strips),
        [((own, model), BF16)] * 2 + term_shapes,
        (scalars, mine, q, kn, kf, *map(in_vmem, packs[1:])),
        scratch=[pltpu.VMEM((n_keys, model), BF16)],
        kept=4 if fast else 2,
        held=range(1, 5),
    )
    (grads,) = call(
        final_kernel,
        [VMEM] * 8,
        [(tokens.shape, BF16)],
        (tokens, wq, wk, wv, gq, gk, gv, gout),
        held=range(1, 8),
    )

    n_tokens = tokens.shape[0] * rows * tokens.shape[1] * cols
    norm = math.sqrt(n_tokens)
    if not fast:
        whole = jnp.stack([terms_qo[0][0], terms_kv[0][0], terms_kv[0][1], terms_qo[0][1]])
        sums = lax.psum_scatter(whole.reshape(-1), AXES, scatter_dimension=0, tiled=True)
        return grads, sums / norm

    here, mine = index // 2 % spots, index // per_matrix

    def pick(values, at, axis):
        return lax.dynamic_index_in_dim(values, at, axis, keepdims=False)

    arrived = swap(terms_kv[1], count, 1).astype(F32)
    sums_kv = (terms_kv[0].astype(F32) + arrived).astype(BF16)

    def within_matrix(sums):
        arrived = [swap(pick(sums, here ^ step, 1), count, 2 * step) for step in range(1, spots)]
        total = pick(sums, here, 1).astype(F32)
        for part in arrived:
            total = total + part.astype(F32)
        return total

    total_qo = within_matrix(sums_qo[0])
    total_kv = within_matrix(sums_kv)
    pieces = jnp.concatenate([total_qo[0:1], total_kv, total_qo[1:2]], axis=0)
    arrived = [
        swap(pick(pieces, mine ^ step, 0).astype(BF16), count, per_matrix * step)
        for step in range(1, 4)
    ]
    result = pick(pieces, mine, 0)
    for part in arrived:
        result = result + part.astype(F32)
    return grads, (result / norm).reshape(-1)


def solution(mesh):
    return jax.shard_map(
        layer,
        mesh=mesh,
        in_specs=(
            P("rows", "cols", None),
            P("rows", "cols", None),
            P("rows", "cols"),
            P(("rows", "cols")),
        ),
        out_specs=(P("rows", "cols", None), P(("rows", "cols"))),
        check_vma=False,
    )
```
